32 devices in a mesh: dp: 8 (over y, x, core), tensor: 4 (over z).
Axes of the slice: x: 2, y: 2, z: 4, core: 2. Of those that a mesh axis runs over, the one named last changes fastest.
Arguments:
- inputs: bfloat16 [16384, 1024], P(('dp', 'tensor')), may hold values from -6 to 6
- teacher: bfloat16 [16384, 1024], P(('dp', 'tensor')), may hold values from -6 to 6
- lengths: int32 [8], replicated, may hold values from 512 to 2048, as said below
- w_qkv: bfloat16 [1024, 3, 1024], P('dp', None, 'tensor'), may hold values from -0.1875 to 0.1875
- w_out_t: bfloat16 [1024, 1024], P('dp', 'tensor'), may hold values from -0.5 to 0.5
- w_gate_up: bfloat16 [1024, 2, 4096], P('dp', None, 'tensor'), may hold values from -0.1875 to 0.1875
- w_down_t: bfloat16 [1024, 4096], P('dp', 'tensor'), may hold values from -0.09375 to 0.09375
- gains: bfloat16 [1024, 2], P('dp'), may hold values from 0.25 to 1.75
Outputs:
- output: bfloat16 [16384, 1024], P(('dp', 'tensor'))
- grad_inputs: float32 [16384, 1024], P(('dp', 'tensor'))
- grad_qkv: float32 [1024, 3, 1024], P('dp', None, 'tensor')
- grad_out_t: float32 [1024, 1024], P('dp', 'tensor')
- grad_gate_up: float32 [1024, 2, 4096], P('dp', None, 'tensor')
- grad_down_t: float32 [1024, 4096], P('dp', 'tensor')
- grad_gains: float32 [1024, 2], P(('dp', 'tensor'))
The draws below stay inside these ranges and needn't reach their ends.
Inputs may be any that keep to these rules, and one draw needn't show every extreme that they name: `lengths`: the longest slot is full, with 2048 valid rows.
All inputs are finite; a program needn't handle non-finite values.
Results may differ from the reference program's by a relative error of at most 0.017.
Values may be sent and summed in bfloat16 or wider, within the bound.
No kernel may reach another device: no remote copies, remote signals or barrier semaphores. Data moves between devices by JAX's collectives and lax.ppermute only.
A program may use at most 192 MiB of HBM per device.

```python
import math
import jax
import jax.numpy as jnp
from jax import lax

D = 1024
HEADS = 16
HEAD = 64
FF = 4096
SLOT = 2048
SEQS = 8
TOKENS = 16384


def draw_lengths(key, part):
    first_key, second_key = jax.random.split(jax.random.fold_in(key, 11))
    values = jax.random.randint(first_key, (SEQS,), SLOT // 4, SLOT + 1, dtype=jnp.int32)
    chosen = jax.random.randint(second_key, (), 0, SEQS, dtype=jnp.int32)
    return jnp.where(jnp.arange(SEQS, dtype=jnp.int32) == chosen, SLOT, values).astype(jnp.int32)


def levels(own_key, extent, cuts, low, top_value):
    def one(position, parts):
        draws = jax.random.uniform(jax.random.fold_in(jax.random.fold_in(own_key, 6), position), (parts,), jnp.float32, low / len(cuts), top_value / len(cuts))
        return jnp.repeat(jnp.exp(draws), extent[position] // parts).reshape((-1,) + (1,) * (len(extent) - position - 1))

    loudness = one(*cuts[0])
    for cut in cuts[1:]:
        loudness = loudness * one(*cut)
    return loudness


def normal_values(own_key, extent, deviation, reach, cuts=(), kind=jnp.bfloat16):
    values = jax.random.normal(own_key, extent, jnp.float32) * deviation
    if len(cuts) > 0:
        values = levels(own_key, extent, cuts, -0.22, 0.18) * values
    return jnp.clip(values, min=-reach, max=reach).astype(kind)


def setup_inputs(seed: int = 0) -> dict:
    arg_keys = jax.random.split(jax.random.key(seed), 9)
    inputs = normal_values(arg_keys[0], (TOKENS, D), 1.0, 6.0, ((0, 32),))
    teacher = normal_values(arg_keys[1], (TOKENS, D), 1.0, 6.0, ((0, 32),))
    lengths = draw_lengths(jax.random.fold_in(arg_keys[8], 71), 0)
    w_qkv = normal_values(arg_keys[3], (D, 3, D), D ** -0.5, 0.1875, ((0, 8), (2, 4)))
    w_out_t = normal_values(arg_keys[4], (D, D), (D // 8) ** -0.5, 0.5, ((0, 8), (1, 4)))
    w_gate_up = normal_values(arg_keys[5], (D, 2, FF), D ** -0.5, 0.1875, ((0, 8), (2, 4)))
    w_down_t = normal_values(arg_keys[6], (D, FF), FF ** -0.5, 0.09375, ((0, 8), (1, 4)))
    gains = jnp.clip(1.0 + 0.15 * jax.random.normal(arg_keys[7], (D, 2), jnp.float32), 0.25, 1.75).astype(jnp.bfloat16)
    return {"inputs": inputs, "teacher": teacher, "lengths": lengths, "w_qkv": w_qkv, "w_out_t": w_out_t, "w_gate_up": w_gate_up, "w_down_t": w_down_t, "gains": gains}


@jax.custom_vjp
def low(v):
    return lax.optimization_barrier(v.astype(jnp.bfloat16)).astype(jnp.float32)

@jax.custom_vjp
def low_back(v):
    return v

def low_keep(v):
    return (low(v), None)

def low_pass(kept, grad):
    return (grad,)

def back_keep(v):
    return (v, None)

def back_low(kept, grad):
    return (low(grad),)
low.defvjp(low_keep, low_pass)
low_back.defvjp(back_keep, back_low)
highest = lax.Precision.HIGHEST

def norm_rows(values, gain):
    meansq = lax.optimization_barrier(jnp.mean(values * values, axis=-1, keepdims=True))
    return values * lax.rsqrt(meansq + 1e-05) * gain

def layer_slot(rows, length, w_qkv, w_out_t, w_gate_up, w_down_t, gains):
    normed_one = low(norm_rows(rows, gains[:, 0]))
    qkv = jnp.einsum('rd,dcf->rcf', normed_one, w_qkv, precision=highest)
    scale = 1.0 / math.sqrt(HEAD)
    queries = low(low_back(qkv[:, 0] * scale)).reshape(SLOT, HEADS, HEAD)
    keys_all = low(low_back(qkv[:, 1])).reshape(SLOT, HEADS, HEAD)
    values_all = low(low_back(qkv[:, 2])).reshape(SLOT, HEADS, HEAD)
    block = min(512, SLOT)
    key_pos = jnp.arange(SLOT, dtype=jnp.int32)

    def attend(start):
        query_block = lax.dynamic_slice_in_dim(queries, start, block, 0)
        scores = jnp.einsum('qhe,khe->hqk', query_block, keys_all, precision=highest)
        scores = low_back(scores)
        query_pos = start + jnp.arange(block, dtype=jnp.int32)
        allowed = (key_pos[None, :] <= query_pos[:, None]) & (key_pos[None, :] < length)
        scores = jnp.where(allowed[None], scores, -1e+30)
        weights = low(jax.nn.softmax(scores, axis=-1))
        return jnp.einsum('hqk,khe->qhe', weights, values_all, precision=highest)
    starts = (jnp.arange(SLOT // block) * block).astype(jnp.int32)
    mixed = lax.map(jax.checkpoint(attend), starts).reshape(SLOT, D)
    mixed = low(low_back(mixed))
    branch = low_back(jnp.einsum('rk,dk->rd', mixed, w_out_t, precision=highest))
    middle = rows + branch
    normed_two = low(norm_rows(middle, gains[:, 1]))
    gate_up = jnp.einsum('rd,dcf->rcf', normed_two, w_gate_up, precision=highest)
    gate = low_back(gate_up[:, 0])
    upper = low_back(gate_up[:, 1])
    hidden = low(jax.nn.silu(gate) * upper)
    feed = low_back(jnp.einsum('rf,df->rd', hidden, w_down_t, precision=highest))
    return middle + feed

def reference(inputs, teacher, lengths, w_qkv, w_out_t, w_gate_up, w_down_t, gains):
    rows_all = inputs.astype(jnp.float32).reshape(SEQS, SLOT, D)
    target_all = teacher.astype(jnp.float32).reshape(SEQS, SLOT, D)
    count = jnp.sum(lengths).astype(jnp.float32)
    positions = jnp.arange(SLOT, dtype=jnp.int32)

    def forward(rows_all, w_qkv, w_out_t, w_gate_up, w_down_t, gains):

        def one_slot(total, inputs_slot):
            rows, length, target = inputs_slot
            final = layer_slot(rows, length, w_qkv, w_out_t, w_gate_up, w_down_t, gains)
            valid = (positions < length)[:, None]
            differ = jnp.where(valid, final - target, 0.0)
            return (total + jnp.sum(differ * differ), final)
        total, finals = lax.scan(one_slot, jnp.zeros((), jnp.float32), (rows_all, lengths, target_all))
        return (total * (TOKENS / (2.0 * count)), finals)
    primals = (rows_all, w_qkv.astype(jnp.float32), w_out_t.astype(jnp.float32), w_gate_up.astype(jnp.float32), w_down_t.astype(jnp.float32), gains.astype(jnp.float32))
    loss, pullback, finals = jax.vjp(forward, *primals, has_aux=True)
    grads = pullback(jnp.ones((), jnp.float32))
    output = finals.reshape(TOKENS, D).astype(jnp.bfloat16)
    grad_inputs = grads[0].reshape(TOKENS, D)
    return (output, grad_inputs, grads[1], grads[2], grads[3], grads[4], grads[5])
```

```python
import math

import jax
import jax.numpy as jnp
from jax import lax
from jax.experimental import pallas as pl
from jax.experimental.pallas import tpu as pltpu
from jax.sharding import PartitionSpec as P

HEAD = 64


negative = -1e30


def norm_forward(values):
    inverse = lax.rsqrt(jnp.mean(values * values, axis=-1, keepdims=True) + 1e-05)
    return (values * inverse, inverse)


def norm_backward(grad_normed, scaled, inverse, gain):
    grad_scaled = grad_normed * gain
    grad_values = inverse * (
        grad_scaled - scaled * jnp.mean(grad_scaled * scaled, axis=-1, keepdims=True)
    )
    return (grad_values, jnp.sum(grad_normed * scaled, axis=0))


def key_limit(query_index):
    return query_index + 1


def score_block(query_block, keys_all, query_start, key_start, length):
    block = query_block.shape[0]
    key_block = lax.dynamic_slice_in_dim(keys_all, key_start, block, 0)
    scores = jnp.einsum("qhe,khe->hqk", query_block, key_block, preferred_element_type=jnp.float32)
    query_pos = query_start + jnp.arange(block, dtype=jnp.int32)
    key_pos = key_start + jnp.arange(block, dtype=jnp.int32)
    allowed = (key_pos[None, :] <= query_pos[:, None]) & (key_pos[None, :] < length)
    return jnp.where(allowed[None], scores, negative)


def attention_forward(queries, keys_all, values_all, length):
    slot, heads, head = queries.shape
    block = min(512, slot)
    block_count = slot // block

    def query_step(index, carry):
        mixed, maxima, totals = carry
        query_start = index * block
        query_block = lax.dynamic_slice_in_dim(queries, query_start, block, 0)
        upper = key_limit(index)

        def stats_step(inner, state):
            maximum, total = state
            scores = score_block(query_block, keys_all, query_start, inner * block, length)
            larger = jnp.maximum(maximum, jnp.max(scores, axis=-1))
            total = total * jnp.exp(maximum - larger) + jnp.sum(
                jnp.exp(scores - larger[..., None]), axis=-1
            )
            return (larger, total)

        start_state = (
            jnp.full((heads, block), negative, jnp.float32),
            jnp.zeros((heads, block), jnp.float32),
        )
        maximum, total = lax.fori_loop(0, upper, stats_step, start_state)

        def mix_step(inner, accum):
            key_start = inner * block
            scores = score_block(query_block, keys_all, query_start, key_start, length)
            weights = (jnp.exp(scores - maximum[..., None]) / total[..., None]).astype(jnp.bfloat16)
            value_block = lax.dynamic_slice_in_dim(values_all, key_start, block, 0)
            return accum + jnp.einsum(
                "hqk,khe->qhe", weights, value_block, preferred_element_type=jnp.float32
            )

        accum = lax.fori_loop(0, upper, mix_step, jnp.zeros((block, heads, head), jnp.float32))
        mixed = lax.dynamic_update_slice_in_dim(mixed, accum, query_start, 0)
        maxima = lax.dynamic_update_index_in_dim(maxima, maximum, index, 0)
        totals = lax.dynamic_update_index_in_dim(totals, total, index, 0)
        return (mixed, maxima, totals)

    start = (
        jnp.zeros((slot, heads, head), jnp.float32),
        jnp.zeros((block_count, heads, block), jnp.float32),
        jnp.zeros((block_count, heads, block), jnp.float32),
    )
    return lax.fori_loop(0, block_count, query_step, start)


def attention_backward(queries, keys_all, values_all, grad_mixed, maxima, totals, length):
    slot, heads, head = queries.shape
    block = min(512, slot)
    block_count = slot // block

    def query_step(index, carry):
        grad_queries, grad_keys, grad_values = carry
        query_start = index * block
        query_block = lax.dynamic_slice_in_dim(queries, query_start, block, 0)
        grad_block = lax.dynamic_slice_in_dim(grad_mixed, query_start, block, 0)
        maximum = lax.dynamic_index_in_dim(maxima, index, 0, keepdims=False)
        total = lax.dynamic_index_in_dim(totals, index, 0, keepdims=False)
        upper = key_limit(index)

        def probs_of(inner):
            key_start = inner * block
            scores = score_block(query_block, keys_all, query_start, key_start, length)
            probs = jnp.exp(scores - maximum[..., None]) / total[..., None]
            value_block = lax.dynamic_slice_in_dim(values_all, key_start, block, 0)
            grad_probs = jnp.einsum(
                "qhe,khe->hqk", grad_block, value_block, preferred_element_type=jnp.float32
            )
            return (probs, grad_probs, key_start)

        def delta_step(inner, delta):
            probs, grad_probs, key_start = probs_of(inner)
            return delta + jnp.sum(probs * grad_probs, axis=-1)

        delta = lax.fori_loop(0, upper, delta_step, jnp.zeros((heads, block), jnp.float32))

        def grad_step(inner, state):
            grad_query, grad_keys, grad_values = state
            probs, grad_probs, key_start = probs_of(inner)
            grad_scores = (probs * (grad_probs - delta[..., None])).astype(jnp.bfloat16)
            key_block = lax.dynamic_slice_in_dim(keys_all, key_start, block, 0)
            grad_query = grad_query + jnp.einsum(
                "hqk,khe->qhe", grad_scores, key_block, preferred_element_type=jnp.float32
            )
            key_part = jnp.einsum(
                "hqk,qhe->khe", grad_scores, query_block, preferred_element_type=jnp.float32
            )
            value_part = jnp.einsum(
                "hqk,qhe->khe",
                probs.astype(jnp.bfloat16),
                grad_block,
                preferred_element_type=jnp.float32,
            )
            old_keys = lax.dynamic_slice_in_dim(grad_keys, key_start, block, 0)
            old_values = lax.dynamic_slice_in_dim(grad_values, key_start, block, 0)
            grad_keys = lax.dynamic_update_slice_in_dim(
                grad_keys, old_keys + key_part, key_start, 0
            )
            grad_values = lax.dynamic_update_slice_in_dim(
                grad_values, old_values + value_part, key_start, 0
            )
            return (grad_query, grad_keys, grad_values)

        start_state = (jnp.zeros((block, heads, head), jnp.float32), grad_keys, grad_values)
        grad_query, grad_keys, grad_values = lax.fori_loop(0, upper, grad_step, start_state)
        grad_queries = lax.dynamic_update_slice_in_dim(grad_queries, grad_query, query_start, 0)
        return (grad_queries, grad_keys, grad_values)

    empty = jnp.zeros((slot, heads, head), jnp.float32)
    return lax.fori_loop(0, block_count, query_step, (empty, empty, empty))


def on_device(inputs, teacher, lengths, w_qkv, w_out_t, w_gate_up, w_down_t, gains):
    own_rows = inputs.shape[0]
    slot = own_rows * lax.axis_size("tensor")
    total_rows = slot * lax.axis_size("dp")
    local_width = w_qkv.shape[2]
    local_heads = local_width // HEAD
    scale = 1.0 / math.sqrt(HEAD)
    length = lax.dynamic_index_in_dim(lengths, lax.axis_index("dp"), 0, keepdims=False)
    count = jnp.sum(lengths).astype(jnp.float32)
    own_start = lax.axis_index("tensor") * own_rows
    row_pos = own_start + jnp.arange(own_rows, dtype=jnp.int32)
    valid = (row_pos < length)[:, None]
    qkv_all, out_all, gains_all = (
        lax.all_gather(w_qkv, "dp", axis=0, tiled=True),
        lax.all_gather(w_out_t, "dp", axis=0, tiled=True),
        lax.all_gather(gains, "dp", axis=0, tiled=True),
    )
    gate_up_all, down_all = (
        lax.all_gather(w_gate_up, "dp", axis=0, tiled=True),
        lax.all_gather(w_down_t, "dp", axis=0, tiled=True),
    )
    gain_one = gains_all[:, 0].astype(jnp.float32)
    gain_two = gains_all[:, 1].astype(jnp.float32)
    rows = inputs.astype(jnp.float32)
    scaled_one, inverse_one = norm_forward(rows)
    normed_one = (scaled_one * gain_one).astype(jnp.bfloat16)
    gathered_one = lax.all_gather(normed_one, "tensor", axis=0, tiled=True)
    qkv = jnp.einsum("rd,dcf->rcf", gathered_one, qkv_all, preferred_element_type=jnp.float32)
    queries = (qkv[:, 0] * scale).astype(jnp.bfloat16).reshape(slot, local_heads, HEAD)
    keys_all = qkv[:, 1].astype(jnp.bfloat16).reshape(slot, local_heads, HEAD)
    values_all = qkv[:, 2].astype(jnp.bfloat16).reshape(slot, local_heads, HEAD)
    mixed, maxima, totals = attention_forward(queries, keys_all, values_all, length)
    mixed = mixed.reshape(slot, local_width).astype(jnp.bfloat16)
    piece = mixed
    middle = rows + lax.psum_scatter(
        jnp.einsum("rk,dk->rd", piece, out_all, preferred_element_type=jnp.float32).astype(
            jnp.bfloat16
        ),
        "tensor",
        scatter_dimension=0,
        tiled=True,
    ).astype(jnp.float32)
    scaled_two, inverse_two = norm_forward(middle)
    normed_two = (scaled_two * gain_two).astype(jnp.bfloat16)
    gathered_two = lax.all_gather(normed_two, "tensor", axis=0, tiled=True)
    rows_two = None
    gate_up = jnp.einsum(
        "rd,dcf->rcf", gathered_two, gate_up_all, preferred_element_type=jnp.float32
    )
    gate = gate_up[:, 0]
    upper = gate_up[:, 1]
    sigmoid = jax.nn.sigmoid(gate)
    hidden = (gate * sigmoid * upper).astype(jnp.bfloat16)
    piece = hidden
    final = middle + lax.psum_scatter(
        jnp.einsum("rf,df->rd", piece, down_all, preferred_element_type=jnp.float32).astype(
            jnp.bfloat16
        ),
        "tensor",
        scatter_dimension=0,
        tiled=True,
    ).astype(jnp.float32)
    output = final.astype(jnp.bfloat16)
    grad_final = jnp.where(valid, final - teacher.astype(jnp.float32), 0.0) * (total_rows / count)
    grad_feed = lax.all_gather(grad_final.astype(jnp.bfloat16), "tensor", axis=0, tiled=True)
    grad_down = jnp.einsum("rd,rf->df", grad_feed, hidden, preferred_element_type=jnp.float32)
    grad_hidden = jnp.einsum("rd,df->rf", grad_feed, down_all, preferred_element_type=jnp.float32)
    grad_gate = grad_hidden * upper * (sigmoid * (1.0 + gate * (1.0 - sigmoid)))
    grad_upper = grad_hidden * (gate * sigmoid)
    grad_gu = jnp.stack([grad_gate, grad_upper], axis=1).astype(jnp.bfloat16)
    rows_two = lax.all_gather(normed_two, "tensor", axis=0, tiled=True)
    grad_gate_up = jnp.einsum("rd,rcf->dcf", rows_two, grad_gu, preferred_element_type=jnp.float32)
    piece = grad_gu
    grad_normed_two = lax.psum_scatter(
        jnp.einsum("rcf,dcf->rd", piece, gate_up_all, preferred_element_type=jnp.float32).astype(
            jnp.bfloat16
        ),
        "tensor",
        scatter_dimension=0,
        tiled=True,
    ).astype(jnp.float32)
    grad_norm_two, grad_gain_two = norm_backward(grad_normed_two, scaled_two, inverse_two, gain_two)
    grad_middle = grad_final + grad_norm_two
    grad_branch = lax.all_gather(grad_middle.astype(jnp.bfloat16), "tensor", axis=0, tiled=True)
    grad_out = jnp.einsum("rd,rk->dk", grad_branch, mixed, preferred_element_type=jnp.float32)
    grad_mixed = jnp.einsum("rd,dk->rk", grad_branch, out_all, preferred_element_type=jnp.float32)
    grad_mixed = grad_mixed.astype(jnp.bfloat16).reshape(slot, local_heads, HEAD)
    grad_queries, grad_keys, grad_values = attention_backward(
        queries, keys_all, values_all, grad_mixed, maxima, totals, length
    )
    grad_rows_qkv = jnp.stack(
        [
            grad_queries.reshape(slot, local_width).astype(jnp.bfloat16) * scale,
            grad_keys.reshape(slot, local_width).astype(jnp.bfloat16),
            grad_values.reshape(slot, local_width).astype(jnp.bfloat16),
        ],
        axis=1,
    )
    rows_one = lax.all_gather(normed_one, "tensor", axis=0, tiled=True)
    grad_qkv = jnp.einsum(
        "rd,rcf->dcf", rows_one, grad_rows_qkv, preferred_element_type=jnp.float32
    )
    piece = grad_rows_qkv
    grad_normed_one = lax.psum_scatter(
        jnp.einsum("rcf,dcf->rd", piece, qkv_all, preferred_element_type=jnp.float32).astype(
            jnp.bfloat16
        ),
        "tensor",
        scatter_dimension=0,
        tiled=True,
    ).astype(jnp.float32)
    grad_norm_one, grad_gain_one = norm_backward(grad_normed_one, scaled_one, inverse_one, gain_one)
    grad_inputs = grad_middle + grad_norm_one
    grad_qkv, grad_out, grad_gate_up, grad_down = (
        lax.psum_scatter(
            grad_qkv.astype(jnp.bfloat16), "dp", scatter_dimension=0, tiled=True
        ).astype(jnp.float32),
        lax.psum_scatter(
            grad_out.astype(jnp.bfloat16), "dp", scatter_dimension=0, tiled=True
        ).astype(jnp.float32),
        lax.psum_scatter(
            grad_gate_up.astype(jnp.bfloat16), "dp", scatter_dimension=0, tiled=True
        ).astype(jnp.float32),
        lax.psum_scatter(
            grad_down.astype(jnp.bfloat16), "dp", scatter_dimension=0, tiled=True
        ).astype(jnp.float32),
    )
    grad_gains = lax.psum_scatter(
        jnp.stack([grad_gain_one, grad_gain_two], axis=1),
        ("dp", "tensor"),
        scatter_dimension=0,
        tiled=True,
    )
    return (output, grad_inputs, grad_qkv, grad_out, grad_gate_up, grad_down, grad_gains)


BF = jnp.bfloat16
F32 = jnp.float32
AXES = ("dp", "tensor")


def shift(value, where):
    pairs = []
    for y in range(2):
        for x in range(2):
            for c in range(2):
                for z in range(4):
                    to = where(y, x, c, z)
                    if to is not None:
                        ty, tx, tc, tz = to
                        pairs.append((((y * 2 + x) * 2 + c) * 4 + z, ((ty * 2 + tx) * 2 + tc) * 4 + tz))
    return lax.ppermute(value, AXES, pairs)


def core_swap(value):
    return shift(value, lambda y, x, c, z: (y, x, 1 - c, z))


def x_swap(value):
    return shift(value, lambda y, x, c, z: (y, 1 - x, c, z))


def y_swap(value):
    return shift(value, lambda y, x, c, z: (1 - y, x, c, z))


def z_swap(value, bits):
    return shift(value, lambda y, x, c, z: (y, x, c, z ^ bits))


def home_of(y, x, c, z):
    if (c == 1 and z < 2) or (c == 0 and z >= 2):
        return (y, x, 1 - c, 3 - z)
    return (y, x, c, z)


def home_swap(value):
    return shift(value, home_of)


def partner_of_home(y, x, c, z):
    y, x, c, z = home_of(y, x, c, z)
    z ^= 1
    if c == 1 and z in (1, 2):
        return None
    return (y, x, c, z)


def head_masks(rows):
    lanes = lax.broadcasted_iota(jnp.int32, (rows, 2 * HEAD), 1)
    return (lanes < HEAD, lanes >= HEAD)


def dot_nt(a, b):
    return lax.dot_general(a, b, (((1,), (1,)), ((), ())), preferred_element_type=F32)


def dot_nn(a, b):
    return lax.dot_general(a, b, (((1,), (0,)), ((), ())), preferred_element_type=F32)


def dot_tn(a, b):
    return lax.dot_general(a, b, (((0,), (0,)), ((), ())), preferred_element_type=F32)


def attend_forward_kernel(sc_ref, q_ref, k_ref, v_ref, o_ref, lse_ref, m_ref, l_ref, acc_ref):
    chunk = q_ref.shape[0] // 2
    tile = chunk // 2
    role = sc_ref[0]
    masks = head_masks(tile)

    def update(state, head, row, key, width, count, diagonal):
        query = jnp.where(masks[head], q_ref[pl.ds(row, tile), :], 0)
        scores = dot_nt(query, k_ref[pl.ds(key, width), :])
        cols = lax.broadcasted_iota(jnp.int32, (tile, width), 1)
        allowed = cols < count
        if diagonal is not None:
            allowed = allowed & (cols <= lax.broadcasted_iota(jnp.int32, (tile, width), 0) + diagonal)
        scores = jnp.where(allowed, scores, negative)
        top = jnp.max(scores, axis=1, keepdims=True)
        if state is None:
            larger = top
        else:
            maximum, total, accum = state
            larger = jnp.maximum(maximum, top)
        weights = jnp.exp(scores - larger)
        part = jnp.sum(weights, axis=1, keepdims=True)
        mix = dot_nn(weights.astype(BF), v_ref[pl.ds(key, width), :])
        if state is None:
            return (larger, part, mix)
        decay = jnp.exp(maximum - larger)
        return (larger, total * decay + part, accum * decay + mix)

    for head in range(2):
        for high in range(2):
            for half in range(2):
                row = high * chunk + half * tile
                state = None
                if high:
                    state = update(state, head, row, 0, chunk, sc_ref[1], None)
                    state = update(state, head, row, 2 * chunk, chunk, sc_ref[3], None)
                own = high * chunk
                state = update(state, head, row, own, (half + 1) * tile, sc_ref[1 + high], half * tile)
                m_ref[head, pl.ds(row, tile), :] = state[0]
                l_ref[head, pl.ds(row, tile), :] = state[1]
                acc_ref[head, pl.ds(row, tile), :] = state[2]
        extra_row = (1 - role) * chunk
        extra_key = (3 - role) * chunk
        for half in range(2):
            row = pl.multiple_of(extra_row + half * tile, tile)
            key = pl.multiple_of(extra_key, tile)
            state = (m_ref[head, pl.ds(row, tile), :], l_ref[head, pl.ds(row, tile), :], acc_ref[head, pl.ds(row, tile), :])
            state = update(state, head, row, key, chunk, sc_ref[5], None)
            m_ref[head, pl.ds(row, tile), :] = state[0]
            l_ref[head, pl.ds(row, tile), :] = state[1]
            acc_ref[head, pl.ds(row, tile), :] = state[2]
    for part in range(4):
        rows = pl.ds(part * tile, tile)
        mixed = [acc_ref[h, rows, :] / l_ref[h, rows, :] for h in range(2)]
        o_ref[rows, :] = jnp.where(masks[0], mixed[0], mixed[1]).astype(BF)
        lse = [m_ref[h, rows, :] + jnp.log(l_ref[h, rows, :]) for h in range(2)]
        turned = jnp.transpose(jnp.where(masks[0], lse[0], lse[1]))
        lse_ref[0, 0:1, rows] = turned[0:1]
        lse_ref[0, 1:2, rows] = turned[HEAD : HEAD + 1]


def attend_forward(scalars, queries, keys_all, values_all):
    rows, width = queries.shape
    slot = keys_all.shape[0]
    pairs = width // (2 * HEAD)
    column = lambda i, sc: (0, i)
    return pl.pallas_call(
        attend_forward_kernel,
        out_shape=(
            jax.ShapeDtypeStruct((rows, width), BF),
            jax.ShapeDtypeStruct((pairs, 8, rows), F32),
        ),
        grid_spec=pltpu.PrefetchScalarGridSpec(
            num_scalar_prefetch=1,
            grid=(pairs,),
            in_specs=[
                pl.BlockSpec((rows, 2 * HEAD), column),
                pl.BlockSpec((slot, 2 * HEAD), column),
                pl.BlockSpec((slot, 2 * HEAD), column),
            ],
            out_specs=(
                pl.BlockSpec((rows, 2 * HEAD), column),
                pl.BlockSpec((1, 8, rows), lambda i, sc: (i, 0, 0)),
            ),
            scratch_shapes=[
                pltpu.VMEM((2, rows, 1), F32),
                pltpu.VMEM((2, rows, 1), F32),
                pltpu.VMEM((2, rows, 2 * HEAD), F32),
            ],
        ),
        compiler_params=pltpu.CompilerParams(vmem_limit_bytes=40 << 20),
        cost_estimate=pl.CostEstimate(
            flops=pairs * 2 * 5 * 4 * (rows // 2) ** 2 * HEAD * 2,
            bytes_accessed=2 * width * (2 * rows + 2 * slot),
            transcendentals=pairs * 2 * 5 * (rows // 2) ** 2,
        ),
    )(scalars, queries, keys_all, values_all)


def attend_backward_kernel(sc_ref, q_ref, k_ref, v_ref, o_ref, g_ref, lse_ref, dq_ref, dk_ref, dv_ref, dq_acc, dk_acc, dv_acc, delta_ref):
    chunk = q_ref.shape[0] // 2
    tile = chunk // 2
    role = sc_ref[0]
    dq_acc[...] = jnp.zeros_like(dq_acc)
    dk_acc[...] = jnp.zeros_like(dk_acc)
    dv_acc[...] = jnp.zeros_like(dv_acc)
    for part in range(4):
        rows = pl.ds(part * tile, tile)
        product = jnp.transpose(o_ref[rows, :].astype(F32) * g_ref[rows, :].astype(F32))
        delta_ref[0:1, rows] = jnp.sum(product[:HEAD], axis=0, keepdims=True)
        delta_ref[1:2, rows] = jnp.sum(product[HEAD:], axis=0, keepdims=True)

    def step(head, row, width, key, count, shift_rows):
        rows = pl.ds(row, width)
        keys = pl.ds(key, tile)
        query = jnp.where(head_masks(width)[head], q_ref[rows, :], 0)
        grad = jnp.where(head_masks(width)[head], g_ref[rows, :], 0)
        key_block = k_ref[keys, :]
        scores = dot_nt(key_block, query)
        index = lax.broadcasted_iota(jnp.int32, (tile, width), 0)
        allowed = index < count
        if shift_rows is not None:
            allowed = allowed & (index <= lax.broadcasted_iota(jnp.int32, (tile, width), 1) + shift_rows)
        probs = jnp.exp(jnp.where(allowed, scores, negative) - lse_ref[0, head : head + 1, rows])
        grad_probs = dot_nt(v_ref[keys, :], grad)
        grad_scores = (probs * (grad_probs - delta_ref[head : head + 1, rows])).astype(BF)
        dv_acc[keys, :] += dot_nn(probs.astype(BF), grad)
        dk_acc[keys, :] += dot_nn(grad_scores, query)
        key_masked = jnp.where(head_masks(tile)[head], key_block, 0)
        dq_acc[rows, :] += dot_tn(grad_scores, key_masked)

    for head in range(2):
        for half in range(2):
            low = half * tile
            for high in range(2):
                own = high * chunk
                count = sc_ref[1 + high] - low
                step(head, own + low, chunk - low, own + low, count, 0)
            step(head, chunk, chunk, low, sc_ref[1] - low, None)
            step(head, chunk, chunk, 2 * chunk + low, sc_ref[3] - low, None)
            extra_row = pl.multiple_of((1 - role) * chunk, chunk)
            extra_key = pl.multiple_of((3 - role) * chunk + low, tile)
            step(head, extra_row, chunk, extra_key, sc_ref[5] - low, None)
    dq_ref[...] = (dq_acc[...] * (1.0 / math.sqrt(HEAD))).astype(BF)
    dk_ref[...] = dk_acc[...].astype(BF)
    dv_ref[...] = dv_acc[...].astype(BF)


def attend_backward(scalars, queries, keys_all, values_all, mixed, grad_mixed, lse):
    rows, width = queries.shape
    slot = keys_all.shape[0]
    pairs = width // (2 * HEAD)
    column = lambda i, sc: (0, i)
    row_spec = pl.BlockSpec((rows, 2 * HEAD), column)
    slot_spec = pl.BlockSpec((slot, 2 * HEAD), column)
    return pl.pallas_call(
        attend_backward_kernel,
        out_shape=(
            jax.ShapeDtypeStruct((rows, width), BF),
            jax.ShapeDtypeStruct((slot, width), BF),
            jax.ShapeDtypeStruct((slot, width), BF),
        ),
        grid_spec=pltpu.PrefetchScalarGridSpec(
            num_scalar_prefetch=1,
            grid=(pairs,),
            in_specs=[row_spec, slot_spec, slot_spec, row_spec, row_spec, pl.BlockSpec((1, 8, rows), lambda i, sc: (i, 0, 0))],
            out_specs=(row_spec, slot_spec, slot_spec),
            scratch_shapes=[
                pltpu.VMEM((rows, 2 * HEAD), F32),
                pltpu.VMEM((slot, 2 * HEAD), F32),
                pltpu.VMEM((slot, 2 * HEAD), F32),
                pltpu.VMEM((8, rows), F32),
            ],
        ),
        compiler_params=pltpu.CompilerParams(vmem_limit_bytes=40 << 20),
        cost_estimate=pl.CostEstimate(
            flops=pairs * 2 * 5 * 10 * (rows // 2) ** 2 * HEAD * 2,
            bytes_accessed=2 * width * (4 * rows + 4 * slot),
            transcendentals=pairs * 2 * 5 * (rows // 2) ** 2,
        ),
    )(scalars, queries, keys_all, values_all, mixed, grad_mixed, lse)


def gather_pieces(piece):
    out = []
    for k in range(4):
        own = piece if k == 0 else z_swap(piece, k)
        x = x_swap(own)
        y = y_swap(own)
        diagonal = y_swap(x) if k % 2 == 0 else x_swap(y)
        out.append(jnp.concatenate([own, x, y, diagonal], axis=1))
    return out


def scatter_pieces(grads):
    total = None
    for k in range(4):
        own, x, y, diagonal = jnp.split(grads[k], 4, axis=1)
        if k % 2 == 0:
            x = (x.astype(F32) + y_swap(diagonal.astype(BF)).astype(F32)).astype(BF)
        else:
            y = (y.astype(F32) + x_swap(diagonal.astype(BF)).astype(F32)).astype(BF)
        part = own.astype(F32) + x_swap(x.astype(BF)).astype(F32) + y_swap(y.astype(BF)).astype(F32)
        total = part if k == 0 else total + z_swap(part.astype(BF), k).astype(F32)
    return total


def on_square(inputs, teacher, lengths, w_qkv, w_out_t, w_gate_up, w_down_t, gains):
    chunk, model = inputs.shape
    slot = chunk * 4
    total_rows = slot * 8
    dp = lax.axis_index("dp")
    z = lax.axis_index("tensor")
    core = dp % 2
    first = core == 0
    odd_x = (dp // 2) % 2 == 1
    odd_y = dp // 4 == 1
    inner = jnp.where((z == 1) | (z == 2), 1, 0)
    chunk_low, chunk_high = inner, 3 - inner
    length = lax.dynamic_index_in_dim(lengths, (dp // 2) * 2 + z // 2, 0, keepdims=False)
    count = jnp.sum(lengths).astype(F32)
    places = jnp.stack([chunk_low, chunk_high, 1 - chunk_low, 5 - chunk_high]) * chunk
    places = places.at[3].set((2 + inner) * chunk)
    counts = jnp.clip(length - places, 0, chunk)
    scalars = jnp.concatenate([jnp.stack([inner]), counts, jnp.stack([jnp.where(inner == 0, counts[3], counts[2])])]).astype(jnp.int32)

    def turn(value):
        a, b, c, d = jnp.split(value, 4, axis=-1)
        a, b, c, d = jnp.where(odd_x, b, a), jnp.where(odd_x, a, b), jnp.where(odd_x, d, c), jnp.where(odd_x, c, d)
        return jnp.concatenate([jnp.where(odd_y, c, a), jnp.where(odd_y, d, b), jnp.where(odd_y, a, c), jnp.where(odd_y, b, d)], axis=-1)

    def sort_cores(own, other, axis):
        return jnp.where(first, jnp.concatenate([own, other], axis=axis), jnp.concatenate([other, own], axis=axis))

    def pick(pair):
        return jnp.where(first, pair[0], pair[1]), jnp.where(first, pair[1], pair[0])

    def join_rows(partial):
        return partial[:chunk] + core_swap(partial[chunk:].astype(BF)).astype(F32)

    def core_piece(stacked):
        keep, give = pick(jnp.split(stacked, 2, axis=2))
        return sort_cores(keep, core_swap(give), 1)

    attention_piece = core_piece(jnp.concatenate([jnp.swapaxes(w_qkv, 0, 1), w_out_t[None]], axis=0))
    feed_piece = core_piece(jnp.concatenate([jnp.swapaxes(w_gate_up, 0, 1), w_down_t[None]], axis=0))
    gains_pair = sort_cores(gains, core_swap(gains), 0)
    gains_x = x_swap(gains_pair)
    gains_all = jnp.concatenate([gains_pair, gains_x, y_swap(gains_pair), y_swap(gains_x)], axis=0)
    gain_one = gains_all[:, 0].astype(F32)
    gain_two = gains_all[:, 1].astype(F32)

    inputs_rel = turn(inputs)
    own_rows = home_swap(inputs_rel)
    partner_rows = shift(inputs_rel, partner_of_home)
    other_rows = core_swap(own_rows)
    other_partner = core_swap(partner_rows)
    attention_w = jnp.concatenate(gather_pieces(attention_piece), axis=2)
    feed_w = jnp.concatenate(gather_pieces(feed_piece), axis=2)
    w_queries, w_keys, w_values, w_out = attention_w[0], attention_w[1], attention_w[2], attention_w[3]
    w_gate, w_up, w_down = feed_w[0], feed_w[1], feed_w[2]

    low, high = pick((own_rows, other_rows))
    low_partner, high_partner = pick((partner_rows, other_partner))
    rows_all = jnp.concatenate([low, high, low_partner, high_partner], axis=0).astype(F32)
    scaled_all, _ = norm_forward(rows_all)
    normed_all = (scaled_all * gain_one).astype(BF)
    normed_own = normed_all[: 2 * chunk]
    rows = own_rows.astype(F32)

    def matmul(a, b):
        return jnp.einsum("ab,bc->ac", a, b, preferred_element_type=F32)

    def matmul_nt(a, b):
        return jnp.einsum("ab,cb->ac", a, b, preferred_element_type=F32)

    def matmul_tn(a, b):
        return jnp.einsum("ba,bc->ac", a, b, preferred_element_type=F32)

    queries = (matmul(normed_own, w_queries) * (1.0 / math.sqrt(HEAD))).astype(BF)
    keys_all = matmul(normed_all, w_keys).astype(BF)
    values_all = matmul(normed_all, w_values).astype(BF)
    mixed, lse = attend_forward(scalars, queries, keys_all, values_all)
    branch = matmul_nt(mixed, w_out)
    keep, give = pick((branch[:chunk], branch[chunk:]))
    middle = rows + keep + core_swap(give.astype(BF)).astype(F32)

    scaled_two, inverse_two = norm_forward(middle)
    normed_two = (scaled_two * gain_two).astype(BF)
    normed_two_all = jnp.concatenate([normed_two, core_swap(normed_two)], axis=0)
    gate = matmul(normed_two_all, w_gate)
    upper = matmul(normed_two_all, w_up)
    sigmoid = jax.nn.sigmoid(gate)
    hidden = (gate * sigmoid * upper).astype(BF)
    final = middle + join_rows(matmul_nt(hidden, w_down))
    output = home_swap(turn(final.astype(BF)))

    teacher_rows = home_swap(turn(teacher)).astype(F32)
    own_place = jnp.where(first, chunk_low, chunk_high) * chunk
    valid = (own_place + jnp.arange(chunk, dtype=jnp.int32) < length)[:, None]
    grad_final = jnp.where(valid, final - teacher_rows, 0.0) * (total_rows / count)
    grad_feed = grad_final.astype(BF)
    grad_feed_all = jnp.concatenate([grad_feed, core_swap(grad_feed)], axis=0)
    grad_hidden = matmul(grad_feed_all, w_down)
    grad_gate = (grad_hidden * upper * (sigmoid * (1.0 + gate * (1.0 - sigmoid)))).astype(BF)
    grad_upper = (grad_hidden * (gate * sigmoid)).astype(BF)
    grad_normed_two = join_rows(matmul_nt(grad_gate, w_gate) + matmul_nt(grad_upper, w_up))
    grad_down = matmul_tn(grad_feed_all, hidden).astype(BF)
    grad_w_gate = matmul_tn(normed_two_all, grad_gate).astype(BF)
    grad_w_up = matmul_tn(normed_two_all, grad_upper).astype(BF)
    feed_grads = [
        jnp.stack([g[:, k * (g.shape[1] // 4) : (k + 1) * (g.shape[1] // 4)] for g in (grad_w_gate, grad_w_up, grad_down)])
        for k in range(4)
    ]
    feed_total = scatter_pieces(feed_grads)

    grad_norm_two, grad_gain_two = norm_backward(grad_normed_two, scaled_two, inverse_two, gain_two)
    grad_middle = grad_final + grad_norm_two
    grad_branch = grad_middle.astype(BF)
    grad_branch_both = sort_cores(grad_branch, core_swap(grad_branch), 0)
    grad_mixed = matmul(grad_branch_both, w_out).astype(BF)
    grad_out = matmul_tn(grad_branch_both, mixed).astype(BF)
    grad_queries, grad_keys, grad_values = attend_backward(scalars, queries, keys_all, values_all, mixed, grad_mixed, lse)

    part_all = matmul_nt(grad_keys, w_keys) + matmul_nt(grad_values, w_values)
    part_own = part_all[: 2 * chunk] + matmul_nt(grad_queries, w_queries)
    part_partner = part_all[2 * chunk :]
    keep_own, give_own = pick((part_own[:chunk], part_own[chunk:]))
    keep_partner, give_partner = pick((part_partner[:chunk], part_partner[chunk:]))
    for_partner = keep_partner + core_swap(give_partner.astype(BF)).astype(F32)
    grad_normed_one = (
        keep_own + core_swap(give_own.astype(BF)).astype(F32) + z_swap(for_partner.astype(BF), 1).astype(F32)
    )
    scaled_one, inverse_one = norm_forward(rows)
    grad_norm_one, grad_gain_one = norm_backward(grad_normed_one, scaled_one, inverse_one, gain_one)
    grad_inputs = home_swap(turn((grad_middle + grad_norm_one).astype(BF))).astype(F32)

    grad_w_queries = matmul_tn(normed_own, grad_queries).astype(BF)
    grad_w_keys = matmul_tn(normed_all, grad_keys).astype(BF)
    grad_w_values = matmul_tn(normed_all, grad_values).astype(BF)
    attention_grads = [
        jnp.stack([g[:, k * (g.shape[1] // 4) : (k + 1) * (g.shape[1] // 4)] for g in (grad_w_queries, grad_w_keys, grad_w_values, grad_out)])
        for k in range(4)
    ]
    attention_total = scatter_pieces(attention_grads)

    def to_home(total):
        keep, give = pick(jnp.split(total, 2, axis=1))
        return sort_cores(keep, core_swap(give.astype(BF)).astype(F32), 2)

    attention_out = to_home(attention_total)
    feed_out = to_home(feed_total)

    both = jnp.stack([grad_gain_one, grad_gain_two], axis=0)
    quarter = model // 4
    a, b, c, d = jnp.split(both, 4, axis=1)
    sent = x_swap(jnp.concatenate([b, d], axis=1))
    a, c = a + sent[:, :quarter], c + sent[:, quarter:]
    a = a + y_swap(c)
    keep, give = pick(jnp.split(a, 2, axis=1))
    a = keep + core_swap(give)
    size = a.shape[1] // 4
    total = lax.dynamic_slice_in_dim(a, z * size, size, 1)
    for k in range(1, 4):
        total = total + z_swap(lax.dynamic_slice_in_dim(a, (z ^ k) * size, size, 1), k)
    grad_gains = jnp.swapaxes(total, 0, 1)

    return (
        output,
        grad_inputs,
        jnp.swapaxes(attention_out[:3], 0, 1),
        attention_out[3],
        jnp.swapaxes(feed_out[:2], 0, 1),
        feed_out[2],
        grad_gains,
    )


def solution(mesh):
    square = dict(mesh.shape) == {"dp": 8, "tensor": 4}
    return jax.shard_map(
        on_square if square else on_device,
        mesh=mesh,
        in_specs=(
            P(("dp", "tensor"), None),
            P(("dp", "tensor"), None),
            P(),
            P("dp", None, "tensor"),
            P("dp", "tensor"),
            P("dp", None, "tensor"),
            P("dp", "tensor"),
            P("dp", None),
        ),
        out_specs=(
            P(("dp", "tensor"), None),
            P(("dp", "tensor"), None),
            P("dp", None, "tensor"),
            P("dp", "tensor"),
            P("dp", None, "tensor"),
            P("dp", "tensor"),
            P(("dp", "tensor"), None),
        ),
        check_vma=False,
    )
```

```python
import math

import jax
import jax.numpy as jnp
from jax import lax
from jax.experimental import pallas as pl
from jax.experimental.pallas import tpu as pltpu
from jax.sharding import PartitionSpec as P

HEAD = 64


negative = -1e30


def norm_forward(values):
    inverse = lax.rsqrt(jnp.mean(values * values, axis=-1, keepdims=True) + 1e-05)
    return (values * inverse, inverse)


def norm_backward(grad_normed, scaled, inverse, gain):
    grad_scaled = grad_normed * gain
    grad_values = inverse * (
        grad_scaled - scaled * jnp.mean(grad_scaled * scaled, axis=-1, keepdims=True)
    )
    return (grad_values, jnp.sum(grad_normed * scaled, axis=0))


def key_limit(query_index):
    return query_index + 1


def score_block(query_block, keys_all, query_start, key_start, length):
    block = query_block.shape[0]
    key_block = lax.dynamic_slice_in_dim(keys_all, key_start, block, 0)
    scores = jnp.einsum("qhe,khe->hqk", query_block, key_block, preferred_element_type=jnp.float32)
    query_pos = query_start + jnp.arange(block, dtype=jnp.int32)
    key_pos = key_start + jnp.arange(block, dtype=jnp.int32)
    allowed = (key_pos[None, :] <= query_pos[:, None]) & (key_pos[None, :] < length)
    return jnp.where(allowed[None], scores, negative)


def attention_forward(queries, keys_all, values_all, length):
    slot, heads, head = queries.shape
    block = min(512, slot)
    block_count = slot // block

    def query_step(index, carry):
        mixed, maxima, totals = carry
        query_start = index * block
        query_block = lax.dynamic_slice_in_dim(queries, query_start, block, 0)
        upper = key_limit(index)

        def stats_step(inner, state):
            maximum, total = state
            scores = score_block(query_block, keys_all, query_start, inner * block, length)
            larger = jnp.maximum(maximum, jnp.max(scores, axis=-1))
            total = total * jnp.exp(maximum - larger) + jnp.sum(
                jnp.exp(scores - larger[..., None]), axis=-1
            )
            return (larger, total)

        start_state = (
            jnp.full((heads, block), negative, jnp.float32),
            jnp.zeros((heads, block), jnp.float32),
        )
        maximum, total = lax.fori_loop(0, upper, stats_step, start_state)

        def mix_step(inner, accum):
            key_start = inner * block
            scores = score_block(query_block, keys_all, query_start, key_start, length)
            weights = (jnp.exp(scores - maximum[..., None]) / total[..., None]).astype(jnp.bfloat16)
            value_block = lax.dynamic_slice_in_dim(values_all, key_start, block, 0)
            return accum + jnp.einsum(
                "hqk,khe->qhe", weights, value_block, preferred_element_type=jnp.float32
            )

        accum = lax.fori_loop(0, upper, mix_step, jnp.zeros((block, heads, head), jnp.float32))
        mixed = lax.dynamic_update_slice_in_dim(mixed, accum, query_start, 0)
        maxima = lax.dynamic_update_index_in_dim(maxima, maximum, index, 0)
        totals = lax.dynamic_update_index_in_dim(totals, total, index, 0)
        return (mixed, maxima, totals)

    start = (
        jnp.zeros((slot, heads, head), jnp.float32),
        jnp.zeros((block_count, heads, block), jnp.float32),
        jnp.zeros((block_count, heads, block), jnp.float32),
    )
    return lax.fori_loop(0, block_count, query_step, start)


def attention_backward(queries, keys_all, values_all, grad_mixed, maxima, totals, length):
    slot, heads, head = queries.shape
    block = min(512, slot)
    block_count = slot // block

    def query_step(index, carry):
        grad_queries, grad_keys, grad_values = carry
        query_start = index * block
        query_block = lax.dynamic_slice_in_dim(queries, query_start, block, 0)
        grad_block = lax.dynamic_slice_in_dim(grad_mixed, query_start, block, 0)
        maximum = lax.dynamic_index_in_dim(maxima, index, 0, keepdims=False)
        total = lax.dynamic_index_in_dim(totals, index, 0, keepdims=False)
        upper = key_limit(index)

        def probs_of(inner):
            key_start = inner * block
            scores = score_block(query_block, keys_all, query_start, key_start, length)
            probs = jnp.exp(scores - maximum[..., None]) / total[..., None]
            value_block = lax.dynamic_slice_in_dim(values_all, key_start, block, 0)
            grad_probs = jnp.einsum(
                "qhe,khe->hqk", grad_block, value_block, preferred_element_type=jnp.float32
            )
            return (probs, grad_probs, key_start)

        def delta_step(inner, delta):
            probs, grad_probs, key_start = probs_of(inner)
            return delta + jnp.sum(probs * grad_probs, axis=-1)

        delta = lax.fori_loop(0, upper, delta_step, jnp.zeros((heads, block), jnp.float32))

        def grad_step(inner, state):
            grad_query, grad_keys, grad_values = state
            probs, grad_probs, key_start = probs_of(inner)
            grad_scores = (probs * (grad_probs - delta[..., None])).astype(jnp.bfloat16)
            key_block = lax.dynamic_slice_in_dim(keys_all, key_start, block, 0)
            grad_query = grad_query + jnp.einsum(
                "hqk,khe->qhe", grad_scores, key_block, preferred_element_type=jnp.float32
            )
            key_part = jnp.einsum(
                "hqk,qhe->khe", grad_scores, query_block, preferred_element_type=jnp.float32
            )
            value_part = jnp.einsum(
                "hqk,qhe->khe",
                probs.astype(jnp.bfloat16),
                grad_block,
                preferred_element_type=jnp.float32,
            )
            old_keys = lax.dynamic_slice_in_dim(grad_keys, key_start, block, 0)
            old_values = lax.dynamic_slice_in_dim(grad_values, key_start, block, 0)
            grad_keys = lax.dynamic_update_slice_in_dim(
                grad_keys, old_keys + key_part, key_start, 0
            )
            grad_values = lax.dynamic_update_slice_in_dim(
                grad_values, old_values + value_part, key_start, 0
            )
            return (grad_query, grad_keys, grad_values)

        start_state = (jnp.zeros((block, heads, head), jnp.float32), grad_keys, grad_values)
        grad_query, grad_keys, grad_values = lax.fori_loop(0, upper, grad_step, start_state)
        grad_queries = lax.dynamic_update_slice_in_dim(grad_queries, grad_query, query_start, 0)
        return (grad_queries, grad_keys, grad_values)

    empty = jnp.zeros((slot, heads, head), jnp.float32)
    return lax.fori_loop(0, block_count, query_step, (empty, empty, empty))


def on_device(inputs, teacher, lengths, w_qkv, w_out_t, w_gate_up, w_down_t, gains):
    own_rows = inputs.shape[0]
    slot = own_rows * lax.axis_size("tensor")
    total_rows = slot * lax.axis_size("dp")
    local_width = w_qkv.shape[2]
    local_heads = local_width // HEAD
    scale = 1.0 / math.sqrt(HEAD)
    length = lax.dynamic_index_in_dim(lengths, lax.axis_index("dp"), 0, keepdims=False)
    count = jnp.sum(lengths).astype(jnp.float32)
    own_start = lax.axis_index("tensor") * own_rows
    row_pos = own_start + jnp.arange(own_rows, dtype=jnp.int32)
    valid = (row_pos < length)[:, None]
    qkv_all, out_all, gains_all = (
        lax.all_gather(w_qkv, "dp", axis=0, tiled=True),
        lax.all_gather(w_out_t, "dp", axis=0, tiled=True),
        lax.all_gather(gains, "dp", axis=0, tiled=True),
    )
    gate_up_all, down_all = (
        lax.all_gather(w_gate_up, "dp", axis=0, tiled=True),
        lax.all_gather(w_down_t, "dp", axis=0, tiled=True),
    )
    gain_one = gains_all[:, 0].astype(jnp.float32)
    gain_two = gains_all[:, 1].astype(jnp.float32)
    rows = inputs.astype(jnp.float32)
    scaled_one, inverse_one = norm_forward(rows)
    normed_one = (scaled_one * gain_one).astype(jnp.bfloat16)
    gathered_one = lax.all_gather(normed_one, "tensor", axis=0, tiled=True)
    qkv = jnp.einsum("rd,dcf->rcf", gathered_one, qkv_all, preferred_element_type=jnp.float32)
    queries = (qkv[:, 0] * scale).astype(jnp.bfloat16).reshape(slot, local_heads, HEAD)
    keys_all = qkv[:, 1].astype(jnp.bfloat16).reshape(slot, local_heads, HEAD)
    values_all = qkv[:, 2].astype(jnp.bfloat16).reshape(slot, local_heads, HEAD)
    mixed, maxima, totals = attention_forward(queries, keys_all, values_all, length)
    mixed = mixed.reshape(slot, local_width).astype(jnp.bfloat16)
    piece = mixed
    middle = rows + lax.psum_scatter(
        jnp.einsum("rk,dk->rd", piece, out_all, preferred_element_type=jnp.float32).astype(
            jnp.bfloat16
        ),
        "tensor",
        scatter_dimension=0,
        tiled=True,
    ).astype(jnp.float32)
    scaled_two, inverse_two = norm_forward(middle)
    normed_two = (scaled_two * gain_two).astype(jnp.bfloat16)
    gathered_two = lax.all_gather(normed_two, "tensor", axis=0, tiled=True)
    rows_two = None
    gate_up = jnp.einsum(
        "rd,dcf->rcf", gathered_two, gate_up_all, preferred_element_type=jnp.float32
    )
    gate = gate_up[:, 0]
    upper = gate_up[:, 1]
    sigmoid = jax.nn.sigmoid(gate)
    hidden = (gate * sigmoid * upper).astype(jnp.bfloat16)
    piece = hidden
    final = middle + lax.psum_scatter(
        jnp.einsum("rf,df->rd", piece, down_all, preferred_element_type=jnp.float32).astype(
            jnp.bfloat16
        ),
        "tensor",
        scatter_dimension=0,
        tiled=True,
    ).astype(jnp.float32)
    output = final.astype(jnp.bfloat16)
    grad_final = jnp.where(valid, final - teacher.astype(jnp.float32), 0.0) * (total_rows / count)
    grad_feed = lax.all_gather(grad_final.astype(jnp.bfloat16), "tensor", axis=0, tiled=True)
    grad_down = jnp.einsum("rd,rf->df", grad_feed, hidden, preferred_element_type=jnp.float32)
    grad_hidden = jnp.einsum("rd,df->rf", grad_feed, down_all, preferred_element_type=jnp.float32)
    grad_gate = grad_hidden * upper * (sigmoid * (1.0 + gate * (1.0 - sigmoid)))
    grad_upper = grad_hidden * (gate * sigmoid)
    grad_gu = jnp.stack([grad_gate, grad_upper], axis=1).astype(jnp.bfloat16)
    rows_two = lax.all_gather(normed_two, "tensor", axis=0, tiled=True)
    grad_gate_up = jnp.einsum("rd,rcf->dcf", rows_two, grad_gu, preferred_element_type=jnp.float32)
    piece = grad_gu
    grad_normed_two = lax.psum_scatter(
        jnp.einsum("rcf,dcf->rd", piece, gate_up_all, preferred_element_type=jnp.float32).astype(
            jnp.bfloat16
        ),
        "tensor",
        scatter_dimension=0,
        tiled=True,
    ).astype(jnp.float32)
    grad_norm_two, grad_gain_two = norm_backward(grad_normed_two, scaled_two, inverse_two, gain_two)
    grad_middle = grad_final + grad_norm_two
    grad_branch = lax.all_gather(grad_middle.astype(jnp.bfloat16), "tensor", axis=0, tiled=True)
    grad_out = jnp.einsum("rd,rk->dk", grad_branch, mixed, preferred_element_type=jnp.float32)
    grad_mixed = jnp.einsum("rd,dk->rk", grad_branch, out_all, preferred_element_type=jnp.float32)
    grad_mixed = grad_mixed.astype(jnp.bfloat16).reshape(slot, local_heads, HEAD)
    grad_queries, grad_keys, grad_values = attention_backward(
        queries, keys_all, values_all, grad_mixed, maxima, totals, length
    )
    grad_rows_qkv = jnp.stack(
        [
            grad_queries.reshape(slot, local_width).astype(jnp.bfloat16) * scale,
            grad_keys.reshape(slot, local_width).astype(jnp.bfloat16),
            grad_values.reshape(slot, local_width).astype(jnp.bfloat16),
        ],
        axis=1,
    )
    rows_one = lax.all_gather(normed_one, "tensor", axis=0, tiled=True)
    grad_qkv = jnp.einsum(
        "rd,rcf->dcf", rows_one, grad_rows_qkv, preferred_element_type=jnp.float32
    )
    piece = grad_rows_qkv
    grad_normed_one = lax.psum_scatter(
        jnp.einsum("rcf,dcf->rd", piece, qkv_all, preferred_element_type=jnp.float32).astype(
            jnp.bfloat16
        ),
        "tensor",
        scatter_dimension=0,
        tiled=True,
    ).astype(jnp.float32)
    grad_norm_one, grad_gain_one = norm_backward(grad_normed_one, scaled_one, inverse_one, gain_one)
    grad_inputs = grad_middle + grad_norm_one
    grad_qkv, grad_out, grad_gate_up, grad_down = (
        lax.psum_scatter(
            grad_qkv.astype(jnp.bfloat16), "dp", scatter_dimension=0, tiled=True
        ).astype(jnp.float32),
        lax.psum_scatter(
            grad_out.astype(jnp.bfloat16), "dp", scatter_dimension=0, tiled=True
        ).astype(jnp.float32),
        lax.psum_scatter(
            grad_gate_up.astype(jnp.bfloat16), "dp", scatter_dimension=0, tiled=True
        ).astype(jnp.float32),
        lax.psum_scatter(
            grad_down.astype(jnp.bfloat16), "dp", scatter_dimension=0, tiled=True
        ).astype(jnp.float32),
    )
    grad_gains = lax.psum_scatter(
        jnp.stack([grad_gain_one, grad_gain_two], axis=1),
        ("dp", "tensor"),
        scatter_dimension=0,
        tiled=True,
    )
    return (output, grad_inputs, grad_qkv, grad_out, grad_gate_up, grad_down, grad_gains)


BF = jnp.bfloat16
F32 = jnp.float32
AXES = ("dp", "tensor")
LIGHT = pl.CostEstimate(flops=1000, bytes_accessed=1000, transcendentals=0)


def shift(value, where):
    pairs = []
    for y in range(2):
        for x in range(2):
            for c in range(2):
                for z in range(4):
                    to = where(y, x, c, z)
                    if to is not None:
                        ty, tx, tc, tz = to
                        pairs.append((((y * 2 + x) * 2 + c) * 4 + z, ((ty * 2 + tx) * 2 + tc) * 4 + tz))
    return lax.ppermute(value, AXES, pairs)


def core_swap(value):
    return shift(value, lambda y, x, c, z: (y, x, 1 - c, z))


def core_swap_halves(value):
    half = value.shape[0] // 2
    return jnp.concatenate([core_swap(value[:half]), core_swap(value[half:])], axis=0)


def x_swap(value):
    return shift(value, lambda y, x, c, z: (y, 1 - x, c, z))


def y_swap(value):
    return shift(value, lambda y, x, c, z: (1 - y, x, c, z))


def square_swap(value):
    return shift(value, lambda y, x, c, z: (1 - y, 1 - x, c, z))


def z_swap(value, bits):
    return shift(value, lambda y, x, c, z: (y, x, c, z ^ bits))


def home_of(y, x, c, z):
    if (c == 1 and z < 2) or (c == 0 and z >= 2):
        return (y, x, 1 - c, 3 - z)
    return (y, x, c, z)


def home_swap(value):
    return shift(value, home_of)


def partner_of_home(y, x, c, z):
    y, x, c, z = home_of(y, x, c, z)
    z ^= 1
    if c == 1 and z in (1, 2):
        return None
    return (y, x, c, z)


def head_masks(rows):
    lanes = lax.broadcasted_iota(jnp.int32, (rows, 2 * HEAD), 1)
    return (lanes < HEAD, lanes >= HEAD)


def dot_nt(a, b):
    return lax.dot_general(a, b, (((1,), (1,)), ((), ())), preferred_element_type=F32)


def dot_nn(a, b):
    return lax.dot_general(a, b, (((1,), (0,)), ((), ())), preferred_element_type=F32)


def dot_tn(a, b):
    return lax.dot_general(a, b, (((0,), (0,)), ((), ())), preferred_element_type=F32)


def attend_forward_kernel(outer_ref, sc_ref, q_ref, k_ref, v_ref, o_ref, lse_ref):
    chunk = q_ref.shape[0] // 2
    tile = chunk // 2
    lanes = 2 * HEAD
    head = pl.program_id(0) % 2
    low, high, low_partner, extra_row, extra_key = [pl.multiple_of(sc_ref[i], chunk) for i in range(5)]
    mine = lax.broadcasted_iota(jnp.int32, (tile, lanes), 1) // HEAD == head

    def fold(op, parts):
        parts = [p[:, i * lanes : (i + 1) * lanes] for p in parts for i in range(p.shape[1] // lanes)]
        while len(parts) > 1:
            parts = [op(parts[i], parts[i + 1]) if i + 1 < len(parts) else parts[i] for i in range(0, len(parts), 2)]
        return parts[0]

    def unit(row, own, own_count, half, others):
        rows = pl.ds(pl.multiple_of(row + half * tile, tile), tile)
        query = jnp.where(mine, q_ref[rows, :], 0)
        blocks = [(pl.ds(start, chunk), count, chunk, None) for start, count in others]
        blocks.append((pl.ds(own, (half + 1) * tile), own_count, (half + 1) * tile, half * tile))
        scores = []
        for keys, count, width, diagonal in blocks:
            s = dot_nt(query, k_ref[keys, :])
            s = s + jnp.where(lax.broadcasted_iota(jnp.int32, (1, width), 1) < count, 0.0, negative)
            if diagonal is not None:
                cols = lax.broadcasted_iota(jnp.int32, (tile, width), 1)
                s = jnp.where(cols <= lax.broadcasted_iota(jnp.int32, (tile, width), 0) + diagonal, s, negative)
            scores.append(s)
        top = jnp.max(fold(jnp.maximum, scores), axis=1, keepdims=True)
        weights = [jnp.exp(s - top) for s in scores]
        total = jnp.sum(fold(jnp.add, weights), axis=1, keepdims=True)
        mixed = None
        for w, (keys, _, _, _) in zip(weights, blocks):
            part = dot_nn(w.astype(BF), v_ref[keys, :])
            mixed = part if mixed is None else mixed + part
        return rows, mixed / total, top + jnp.log(total)

    def finish(units):
        for rows, mixed, lse in units:
            mixed = mixed.astype(BF)
            o_ref[rows, :] = jnp.where(mine, mixed, o_ref[rows, :])
            lse_ref[0, pl.ds(head, 1), rows] = jnp.transpose(jnp.broadcast_to(lse, (tile, lanes)))[0:1]

    near = [(low, sc_ref[5]), (low_partner, sc_ref[7])]
    extra = [(extra_key, sc_ref[8])]

    @pl.when(outer_ref[0] == 1)
    def _():
        for half in range(2):
            finish([unit(high, high, sc_ref[6], half, near + extra), unit(low, low, sc_ref[5], half, [])])

    @pl.when(outer_ref[0] == 0)
    def _():
        for half in range(2):
            finish([unit(high, high, sc_ref[6], half, near), unit(low, low, sc_ref[5], half, extra)])


def attend_forward(outer, scalars, queries, keys_all, values_all, start, pairs):
    rows = queries.shape[0]
    width = pairs * 2 * HEAD
    slot = keys_all.shape[0]
    own = lambda i, *_: (0, i // 2)
    column = lambda i, *_: (0, i // 2 + start)
    return pl.pallas_call(
        attend_forward_kernel,
        out_shape=(
            jax.ShapeDtypeStruct((rows, width), BF),
            jax.ShapeDtypeStruct((pairs, 8, rows), F32),
        ),
        grid_spec=pltpu.PrefetchScalarGridSpec(
            num_scalar_prefetch=2,
            grid=(2 * pairs,),
            in_specs=[
                pl.BlockSpec((rows, 2 * HEAD), column),
                pl.BlockSpec((slot, 2 * HEAD), column),
                pl.BlockSpec((slot, 2 * HEAD), column),
            ],
            out_specs=(
                pl.BlockSpec((rows, 2 * HEAD), own),
                pl.BlockSpec((1, 8, rows), lambda i, *_: (i // 2, 0, 0)),
            ),
        ),
        compiler_params=pltpu.CompilerParams(vmem_limit_bytes=24 << 20),
        cost_estimate=LIGHT,
        name="attend_forward",
    )(outer, scalars, queries, keys_all, values_all)


def attend_backward_kernel(sc_ref, q_ref, k_ref, v_ref, o_ref, g_ref, lse_ref, dq_ref, dk_ref, dv_ref, dq_acc, dk_acc, dv_acc, delta_ref):
    chunk = q_ref.shape[0] // 2
    tile = chunk // 2
    low, high_row, low_partner, extra_row, extra_key = [pl.multiple_of(sc_ref[i], chunk) for i in range(5)]
    dq_acc[...] = jnp.zeros_like(dq_acc)
    dk_acc[...] = jnp.zeros_like(dk_acc)
    dv_acc[...] = jnp.zeros_like(dv_acc)
    for part in range(4):
        rows = pl.ds(part * tile, tile)
        product = jnp.transpose(o_ref[rows, :].astype(F32) * g_ref[rows, :].astype(F32))
        delta_ref[0:1, rows] = jnp.sum(product[:HEAD], axis=0, keepdims=True)
        delta_ref[1:2, rows] = jnp.sum(product[HEAD:], axis=0, keepdims=True)

    def step(head, row, width, key, count, shift_rows):
        rows = pl.ds(row, width)
        keys = pl.ds(key, tile)
        query = jnp.where(head_masks(width)[head], q_ref[rows, :], 0)
        grad = jnp.where(head_masks(width)[head], g_ref[rows, :], 0)
        key_block = k_ref[keys, :]
        scores = dot_nt(key_block, query)
        index = lax.broadcasted_iota(jnp.int32, (tile, width), 0)
        allowed = index < count
        if shift_rows is not None:
            allowed = allowed & (index <= lax.broadcasted_iota(jnp.int32, (tile, width), 1) + shift_rows)
        probs = jnp.exp(jnp.where(allowed, scores, negative) - lse_ref[0, head : head + 1, rows])
        grad_probs = dot_nt(v_ref[keys, :], grad)
        grad_scores = (probs * (grad_probs - delta_ref[head : head + 1, rows])).astype(BF)
        dv_acc[keys, :] += dot_nn(probs.astype(BF), grad)
        dk_acc[keys, :] += dot_nn(grad_scores, query)
        key_masked = jnp.where(head_masks(tile)[head], key_block, 0)
        dq_acc[rows, :] += dot_tn(grad_scores, key_masked)

    for head in range(2):
        for half in range(2):
            down = half * tile
            add = lambda start: pl.multiple_of(start + down, tile)
            step(head, add(low), chunk - down, add(low), sc_ref[5] - down, 0)
            step(head, add(high_row), chunk - down, add(high_row), sc_ref[6] - down, 0)
            step(head, high_row, chunk, add(low), sc_ref[5] - down, None)
            step(head, high_row, chunk, add(low_partner), sc_ref[7] - down, None)
            step(head, extra_row, chunk, add(extra_key), sc_ref[8] - down, None)
    dq_ref[...] = (dq_acc[...] * (1.0 / math.sqrt(HEAD))).astype(BF)
    dk_ref[...] = dk_acc[...].astype(BF)
    dv_ref[...] = dv_acc[...].astype(BF)


def attend_backward(scalars, queries, keys_all, values_all, mixed, grad_mixed, lse, start):
    rows, width = mixed.shape
    pairs = width // (2 * HEAD)
    slot = keys_all.shape[0]
    own = lambda i, sc: (0, i)
    column = lambda i, sc: (0, i + start)
    own_spec = pl.BlockSpec((rows, 2 * HEAD), own)
    row_spec = pl.BlockSpec((rows, 2 * HEAD), column)
    slot_spec = pl.BlockSpec((slot, 2 * HEAD), column)
    return pl.pallas_call(
        attend_backward_kernel,
        out_shape=(
            jax.ShapeDtypeStruct((rows, width), BF),
            jax.ShapeDtypeStruct((slot, width), BF),
            jax.ShapeDtypeStruct((slot, width), BF),
        ),
        grid_spec=pltpu.PrefetchScalarGridSpec(
            num_scalar_prefetch=1,
            grid=(pairs,),
            in_specs=[row_spec, slot_spec, slot_spec, own_spec, row_spec, pl.BlockSpec((1, 8, rows), lambda i, sc: (i, 0, 0))],
            out_specs=(own_spec, pl.BlockSpec((slot, 2 * HEAD), own), pl.BlockSpec((slot, 2 * HEAD), own)),
            scratch_shapes=[
                pltpu.VMEM((rows, 2 * HEAD), F32),
                pltpu.VMEM((slot, 2 * HEAD), F32),
                pltpu.VMEM((slot, 2 * HEAD), F32),
                pltpu.VMEM((8, rows), F32),
            ],
        ),
        compiler_params=pltpu.CompilerParams(vmem_limit_bytes=32 << 20),
        cost_estimate=LIGHT,
    )(scalars, queries, keys_all, values_all, mixed, grad_mixed, lse)


def project_kernel(*refs):
    rows_refs, gain_ref, (low_ref, low_x_ref, low_yd_ref, high_ref, high_y_ref, high_xd_ref) = refs[:4], refs[4], refs[5:11]
    normed_ref, q_ref, k_ref, v_ref, wq_ref, wk_ref, wv_ref, wo_ref = refs[11:]
    step = pl.program_id(0)
    _, block, width = low_ref.shape
    part = width // 4
    tile = rows_refs[0].shape[0] // 2

    @pl.when(step == 0)
    def _():
        for k in range(4):
            if k < 2:
                blocks = (low_ref.at[k], low_x_ref.at[k], low_yd_ref.at[k], low_yd_ref.at[k + 2])
            else:
                blocks = (high_ref.at[k - 2], high_xd_ref.at[k - 2], high_y_ref.at[k - 2], high_xd_ref.at[k])
            for r in range(4):
                for n, out in enumerate((wq_ref, wk_ref, wv_ref, wo_ref)):
                    out[r * block : (r + 1) * block, k * part : (k + 1) * part] = blocks[r][:, n * part : (n + 1) * part]

    for n in range(4):

        @pl.when(step == n)
        def _():
            for half in range(2):
                rows = slice(half * tile, (half + 1) * tile)
                values = rows_refs[n][rows, :].astype(F32)
                inverse = lax.rsqrt(jnp.mean(values * values, axis=-1, keepdims=True) + 1e-05)
                normed = (values * inverse * gain_ref[...]).astype(BF)
                normed_ref[rows, :] = normed
                k_ref[rows, :] = dot_nn(normed, wk_ref[...]).astype(BF)
                v_ref[rows, :] = dot_nn(normed, wv_ref[...]).astype(BF)
                if n < 2:
                    q_ref[rows, :] = (dot_nn(normed, wq_ref[...]) * (1.0 / math.sqrt(HEAD))).astype(BF)


def project(rows_parts, gain, weights):
    chunk, model = rows_parts[0].shape
    _, block, width = weights[0].shape
    whole = lambda shape: pl.BlockSpec(shape, lambda i: (0,) * len(shape))
    tiles = lambda cols: pl.BlockSpec((chunk, cols), lambda i: (i, 0))
    shape = lambda r, c: jax.ShapeDtypeStruct((r, c), BF)
    return pl.pallas_call(
        project_kernel,
        out_shape=(
            shape(4 * chunk, model),
            shape(2 * chunk, width),
            shape(4 * chunk, width),
            shape(4 * chunk, width),
            shape(model, width),
            shape(model, width),
            shape(model, width),
            shape(model, width),
        ),
        grid=(4,),
        in_specs=[whole((chunk, model))] * 4 + [whole((1, model))] + [whole(w.shape) for w in weights],
        out_specs=(
            tiles(model),
            pl.BlockSpec((chunk, width), lambda i: (jnp.minimum(i, 1), 0)),
            tiles(width),
            tiles(width),
        )
        + tuple(whole((model, width)) for _ in range(4)),
        compiler_params=pltpu.CompilerParams(vmem_limit_bytes=60 << 20),
        cost_estimate=LIGHT,
        name="project",
    )(*rows_parts, gain, *weights)


def feed_forward_kernel(first_piece, *refs):
    x_ref, weight_refs = refs[0], refs[1:5]
    block = weight_refs[0].shape[1]
    if not first_piece:
        y_in_ref = refs[5]
    silu_ref, slope_ref, hidden_ref, y_ref = refs[-4:]
    x = x_ref[...]
    gate = upper = None
    for r in range(4):
        part = x[:, r * block : (r + 1) * block]
        g = dot_nn(part, weight_refs[r][0])
        u = dot_nn(part, weight_refs[r][1])
        gate = g if gate is None else gate + g
        upper = u if upper is None else upper + u
    sigmoid = jax.nn.sigmoid(gate)
    silu = gate * sigmoid
    hidden = (silu * upper).astype(BF)
    silu_ref[...] = silu.astype(BF)
    slope_ref[...] = (upper * (sigmoid * (1.0 + gate * (1.0 - sigmoid)))).astype(BF)
    hidden_ref[...] = hidden
    for r in range(4):
        cols = slice(r * block, (r + 1) * block)
        y = dot_nt(hidden, weight_refs[r][2])
        y_ref[:, cols] = y if first_piece else y + y_in_ref[:, cols]


def alone(piece):
    return (piece[None], 0)


def feed_forward(x, pieces, y):
    rows, model = x.shape
    _, _, block, width = pieces[0][0].shape
    tile = rows // 4
    tiles = lambda cols: pl.BlockSpec((tile, cols), lambda i: (i, 0))
    weight_specs = [pl.BlockSpec((None, 3, block, width), lambda i, n=n: (n, 0, 0, 0)) for _, n in pieces]
    extra = [] if y is None else [y]
    return pl.pallas_call(
        lambda *refs: feed_forward_kernel(y is None, *refs),
        out_shape=tuple(jax.ShapeDtypeStruct((rows, width), BF) for _ in range(3)) + (jax.ShapeDtypeStruct((rows, model), F32),),
        grid=(4,),
        in_specs=[tiles(model)] + weight_specs + [tiles(model) for _ in extra],
        out_specs=(tiles(width), tiles(width), tiles(width), tiles(model)),
        input_output_aliases={5: 3} if extra else {},
        compiler_params=pltpu.CompilerParams(vmem_limit_bytes=24 << 20),
        cost_estimate=LIGHT,
        name="feed_forward",
    )(x, *[w for w, _ in pieces], *extra)


def feed_backward_kernel(places, has_sum, last, *refs):
    count = len(places) // 4
    refs = list(refs)
    take = lambda n: [refs.pop(0) for _ in range(n)]
    x_ref, g_ref = take(2)
    silu_hbm, slope_hbm, hidden_hbm, weight_hbm = take(count), take(count), take(count), take(4 * count)
    sum_ref = take(1)[0] if has_sum else None
    dx_ref, dx_other_ref = take(2) if last else take(1) * 2
    out_hbm = take(4 * count)
    xt_ref, gt_ref, kept_ref, hidden_ref, gu_ref, down_ref, acc_ref, out_ref, act_sem, weight_sem, out_sem = refs
    _, _, block, width = weight_hbm[0].shape
    rows_all = x_ref.shape[0]
    half = rows_all // 2
    copies_of, late_copies = [], []
    for p in range(count):
        copies = []
        for n, source in enumerate((slope_hbm[p], silu_hbm[p])):
            copies.append(pltpu.make_async_copy(source, kept_ref.at[p, :, pl.ds(n * width, width)], act_sem.at[p, n]))
        for r in range(4):
            features = pl.ds(r * block, block)
            source = weight_hbm[p * 4 + r].at[places[p * 4 + r]]
            for n, target in enumerate((gu_ref.at[p, features, pl.ds(0, width)], gu_ref.at[p, features, pl.ds(width, width)], down_ref.at[p, features, :])):
                copies.append(pltpu.make_async_copy(source.at[n], target, weight_sem.at[p, r, n]))
        copies_of.append(copies)
        late_copies.append(pltpu.make_async_copy(hidden_hbm[p], hidden_ref.at[p], act_sem.at[p, 2]))
    for copy in copies_of[0]:
        copy.start()
    for t in range(4):
        rows = slice(t * rows_all // 4, (t + 1) * rows_all // 4)
        xt_ref[:, rows] = jnp.transpose(x_ref[rows, :])
        gt_ref[:, rows] = jnp.transpose(g_ref[rows, :])

    for p in range(count):
        for copy in copies_of[p]:
            copy.wait()
        for copy in copies_of[p + 1] if p < count - 1 else late_copies:
            copy.start()
        for t in range(2):
            rows = slice(t * half, (t + 1) * half)
            grad_hidden = dot_nn(g_ref[rows, :], down_ref[p])
            kept_ref[p, rows, :width] = (grad_hidden * kept_ref[p, rows, :width].astype(F32)).astype(BF)
            kept_ref[p, rows, width:] = (grad_hidden * kept_ref[p, rows, width:].astype(F32)).astype(BF)
            part = dot_nt(kept_ref[p, rows, :], gu_ref[p])
            if p > 0:
                part = acc_ref[rows, :] + part
            elif has_sum:
                part = sum_ref[rows, :] + part
            if p < count - 1:
                acc_ref[rows, :] = part
            elif not last:
                dx_ref[rows, :] = part
            elif t == 0:
                dx_ref[...] = part
            else:
                dx_other_ref[...] = part.astype(BF)

    slots = out_ref.shape[0]
    copies = []
    for p in range(count):
        late_copies[p].wait()
        for r in range(3, -1, -1):
            features = slice(r * block, (r + 1) * block)
            slot = len(copies) % slots
            if len(copies) >= slots:
                copies[len(copies) - slots].wait()
            gu = dot_nn(xt_ref[features, :], kept_ref[p]).astype(BF)
            out_ref[slot, 0] = gu[:, :width]
            out_ref[slot, 1] = gu[:, width:]
            out_ref[slot, 2] = dot_nn(gt_ref[features, :], hidden_ref[p]).astype(BF)
            copies.append(pltpu.make_async_copy(out_ref.at[slot], out_hbm[p * 4 + r], out_sem.at[slot]))
            copies[-1].start()
    for copy in copies[-slots:]:
        copy.wait()


def feed_backward(x, g, silus, slopes, hiddens, pieces, total, last):
    count = len(pieces)
    extra = [] if total is None else [total]
    rows, model = x.shape
    _, _, block, width = pieces[0][0][0].shape
    places = [n for piece in pieces for _, n in piece]
    vmem = pl.BlockSpec(memory_space=pltpu.VMEM)
    hbm = pl.BlockSpec(memory_space=pl.ANY)
    outs = pl.pallas_call(
        lambda *refs: feed_backward_kernel(places, total is not None, last, *refs),
        out_shape=(
            (jax.ShapeDtypeStruct((rows // 2, model), F32), jax.ShapeDtypeStruct((rows // 2, model), BF))
            if last
            else (jax.ShapeDtypeStruct((rows, model), F32),)
        )
        + tuple(jax.ShapeDtypeStruct((3, block, width), BF) for _ in range(4 * count)),
        in_specs=[vmem] * 2 + [hbm] * (7 * count) + [vmem] * len(extra),
        out_specs=((vmem, vmem) if last else (vmem,)) + (hbm,) * (4 * count),
        scratch_shapes=[
            pltpu.VMEM((model, rows), BF),
            pltpu.VMEM((model, rows), BF),
            pltpu.VMEM((count, rows, 2 * width), BF),
            pltpu.VMEM((count, rows, width), BF),
            pltpu.VMEM((count, model, 2 * width), BF),
            pltpu.VMEM((count, model, width), BF),
            pltpu.VMEM((rows, model), F32),
            pltpu.VMEM((3, 3, block, width), BF),
            pltpu.SemaphoreType.DMA((count, 3)),
            pltpu.SemaphoreType.DMA((count, 4, 3)),
            pltpu.SemaphoreType.DMA((3,)),
        ],
        compiler_params=pltpu.CompilerParams(vmem_limit_bytes=60 << 20),
        cost_estimate=LIGHT,
        name="feed_backward",
    )(x, g, *silus, *slopes, *hiddens, *[w for piece in pieces for w, _ in piece], *extra)
    first = 2 if last else 1
    return outs[:first], [outs[first + 4 * p : first + 4 + 4 * p] for p in range(count)]


class Order:
    def __init__(self):
        self.last = ()

    def event(self, *values):
        out = lax.optimization_barrier((*values, *self.last))[: len(values)]
        self.last = out
        return out


def on_square(inputs, teacher, lengths, w_qkv, w_out_t, w_gate_up, w_down_t, gains):
    chunk, model = inputs.shape
    slot = chunk * 4
    total_rows = slot * 8
    dp = lax.axis_index("dp")
    z = lax.axis_index("tensor")
    core = dp % 2
    first = core == 0
    odd_x = (dp // 2) % 2 == 1
    odd_y = dp // 4 == 1
    inner = jnp.where((z == 1) | (z == 2), 1, 0)
    chunk_low, chunk_high = inner, 3 - inner
    length = lax.dynamic_index_in_dim(lengths, (dp // 2) * 2 + z // 2, 0, keepdims=False)
    count = jnp.sum(lengths).astype(F32)
    places = jnp.stack([chunk_low, chunk_high, 1 - chunk_low, 2 + inner]) * chunk
    counts = jnp.clip(length - places, 0, chunk)
    outer = 1 - inner
    low_row, high_row = core * chunk, (1 - core) * chunk
    low_partner, high_partner = low_row + 2 * chunk, high_row + 2 * chunk
    scalars = jnp.stack(
        [
            low_row,
            high_row,
            low_partner,
            jnp.where(outer == 1, high_row, low_row),
            jnp.where(outer == 1, high_partner, low_partner),
            counts[0],
            counts[1],
            counts[2],
            jnp.where(outer == 1, counts[3], counts[2]),
        ]
    ).astype(jnp.int32)

    def turn(value):
        a, b, c, d = jnp.split(value, 4, axis=-1)
        a, b, c, d = jnp.where(odd_x, b, a), jnp.where(odd_x, a, b), jnp.where(odd_x, d, c), jnp.where(odd_x, c, d)
        return jnp.concatenate([jnp.where(odd_y, c, a), jnp.where(odd_y, d, b), jnp.where(odd_y, a, c), jnp.where(odd_y, b, d)], axis=-1)

    def sort_cores(own, other, axis):
        return jnp.where(first, jnp.concatenate([own, other], axis=axis), jnp.concatenate([other, own], axis=axis))

    def pick(pair):
        return jnp.where(first, pair[0], pair[1]), jnp.where(first, pair[1], pair[0])

    def join_rows(partial):
        return partial[:chunk] + core_swap(partial[chunk:].astype(BF)).astype(F32)

    def core_piece(stacked):
        keep, give = pick(jnp.split(stacked, 2, axis=2))
        return sort_cores(keep, core_swap(give), 1)

    def matmul(a, b):
        return jnp.einsum("ab,bc->ac", a, b, preferred_element_type=F32)

    def matmul_nt(a, b):
        return jnp.einsum("ab,cb->ac", a, b, preferred_element_type=F32)

    def matmul_tn(a, b):
        return jnp.einsum("ba,bc->ac", a, b, preferred_element_type=F32)

    order = Order()
    event = order.event

    attention_piece = core_piece(jnp.concatenate([jnp.swapaxes(w_qkv, 0, 1), w_out_t[None]], axis=0))
    attention_piece = jnp.concatenate([attention_piece[n] for n in range(4)], axis=1)
    feed_piece = core_piece(jnp.concatenate([jnp.swapaxes(w_gate_up, 0, 1), w_down_t[None]], axis=0))
    feed_p, feed_x, feed_y, feed_d = [None] * 4, [None] * 4, [None] * 4, [None] * 4
    (gains_pair,) = event(sort_cores(gains, core_swap(gains), 0))
    gains_x, gains_y, gains_d = x_swap(gains_pair), y_swap(gains_pair), square_swap(gains_pair)
    inputs_rel = turn(inputs)
    gains_x, gains_y, gains_d, attention_piece, feed_p[0] = event(gains_x, gains_y, gains_d, attention_piece, feed_piece)
    gains_all = jnp.concatenate([gains_pair, gains_x, gains_y, gains_d], axis=0)

    att_1, att_2, att_3 = z_swap(attention_piece, 1), z_swap(attention_piece, 2), z_swap(attention_piece, 3)
    feed_x[0], feed_y[0] = x_swap(feed_p[0]), y_swap(feed_p[0])
    att_1, att_2, att_3, inputs_rel = event(att_1, att_2, att_3, inputs_rel)
    att_low, att_high = jnp.stack([attention_piece, att_1]), jnp.stack([att_2, att_3])
    own_rows, partner_rows = home_swap(inputs_rel), shift(inputs_rel, partner_of_home)
    att_low_x, att_high_y = x_swap(att_low), y_swap(att_high)
    feed_x[0], feed_y[0] = event(feed_x[0], feed_y[0])
    att_low_x, att_high_y, feed_piece = event(att_low_x, att_high_y, feed_p[0])
    att_low_yd = y_swap(jnp.concatenate([att_low, att_low_x], axis=0))
    att_high_xd = x_swap(jnp.concatenate([att_high, att_high_y], axis=0))
    own_rows, feed_piece = event(own_rows, feed_piece)
    partner_rows, feed_piece, feed_x[0] = event(partner_rows, feed_piece, feed_x[0])
    other_rows, other_partner = core_swap(own_rows), core_swap(partner_rows)
    feed_p[1] = z_swap(feed_piece, 1)
    feed_d[0] = y_swap(feed_x[0])
    att_low_yd, att_high_xd = event(att_low_yd, att_high_xd)
    other_rows, other_partner, feed_piece = event(other_rows, other_partner, feed_piece)
    feed_p[2] = z_swap(feed_piece, 2)
    rows = own_rows.astype(F32)
    gain_one = gains_all[:, 0].astype(F32)
    gain_two = gains_all[:, 1].astype(F32)

    normed_all, queries, keys_all, values_all, w_queries, w_keys, w_values, w_out = project(
        (own_rows, other_rows, partner_rows, other_partner), gain_one[None], [att_low, att_low_x, att_low_yd, att_high, att_high_y, att_high_xd]
    )
    normed_own = normed_all[: 2 * chunk]
    outer_only = (1 - inner)[None].astype(jnp.int32)
    parts = [None] * 4

    def attend(n):
        return attend_forward(outer_only, scalars, queries, keys_all, values_all, n, 1)

    queries, feed_d[0], feed_p[1] = event(queries, feed_d[0], feed_p[1])
    feed_x[1], feed_y[1] = x_swap(feed_p[1]), y_swap(feed_p[1])
    parts[0] = attend(0)
    parts[1] = attend(1)
    queries, feed_x[1], feed_y[1], feed_p[2], _, _ = event(queries, feed_x[1], feed_y[1], feed_p[2], parts[0][0], parts[1][0])
    feed_p[3] = z_swap(feed_p[2], 1)
    batch_x = x_swap(jnp.stack([feed_y[1], feed_p[2]]))
    feed_y[2] = y_swap(feed_p[2])
    parts[2] = attend(2)
    parts[3] = attend(3)
    mixed = jnp.concatenate([p[0] for p in parts], axis=1)
    branch = matmul_nt(mixed, w_out)
    branch_own, branch_other, feed_p[3], feed_y[2], batch_x, teacher = event(
        branch[:chunk], branch[chunk:].astype(BF), feed_p[3], feed_y[2], batch_x, teacher
    )
    batch_y = y_swap(jnp.stack([feed_p[3], batch_x[1]]))
    feed_x[3] = x_swap(feed_p[3])
    teacher_rel = turn(teacher)
    middle = rows + branch_own + core_swap_halves(branch_other).astype(F32)

    scaled_two, inverse_two = norm_forward(middle)
    normed_two = (scaled_two * gain_two).astype(BF)
    normed_two_all = jnp.concatenate([normed_two, core_swap_halves(normed_two)], axis=0)
    silus, slopes, hiddens, feed = [None] * 4, [None] * 4, [None] * 4, None
    pieces = [
        [alone(feed_p[0]), alone(feed_x[0]), alone(feed_y[0]), alone(feed_d[0])],
        [alone(feed_p[1]), alone(feed_x[1]), alone(feed_y[1]), (batch_x, 0)],
    ]
    for k in range(4):
        if k == 2:
            feed, batch_y, feed_x[3], teacher_rel = event(feed, batch_y, feed_x[3], teacher_rel)
            feed_d[3] = x_swap(batch_y[0])
            teacher_rows = home_swap(teacher_rel)
            pieces.append([alone(feed_p[2]), (batch_x, 1), alone(feed_y[2]), (batch_y, 1)])
        if k == 3:
            feed, feed_d[3] = event(feed, feed_d[3])
            pieces.append([alone(feed_p[3]), alone(feed_x[3]), (batch_y, 0), alone(feed_d[3])])
        silus[k], slopes[k], hiddens[k], feed = feed_forward(normed_two_all, pieces[k], feed)
    feed_own, feed_other, teacher_rows = event(feed[:chunk], feed[chunk:].astype(BF), teacher_rows)
    final = middle + feed_own + core_swap(feed_other).astype(F32)

    own_place = jnp.where(first, chunk_low, chunk_high) * chunk
    valid = (own_place + jnp.arange(chunk, dtype=jnp.int32) < length)[:, None]
    grad_final = jnp.where(valid, final - teacher_rows.astype(F32), 0.0) * (total_rows / count)
    grad_feed = grad_final.astype(BF)
    grad_feed_all, output = event(jnp.concatenate([grad_feed, core_swap(grad_feed)], axis=0), turn(final.astype(BF)))
    output = home_swap(output)

    def add(a, b):
        return (a.astype(F32) + b.astype(F32)).astype(BF)

    def total_of(own, x, y):
        return own.astype(F32) + x.astype(F32) + y.astype(F32)

    def feed_back(k, total):
        pair = slice(k, k + 2)
        return feed_backward(normed_two_all, grad_feed_all, silus[pair], slopes[pair], hiddens[pair], pieces[pair], total, k == 0)

    (grad_x,), ((own_2, x_2, y_2, d_2), (own_3, x_3, y_3, d_3)) = feed_back(2, None)
    grad_x, d_2, d_3 = event(grad_x, d_2, d_3)
    d_2, d_3 = y_swap(d_2), x_swap(d_3)
    (grad_x, grad_x_other), ((own_0, x_0, y_0, d_0), (own_1, x_1, y_1, d_1)) = feed_back(0, grad_x)
    grad_x, grad_x_other, output, d_2, d_3, d_0, d_1, y_2, x_3 = event(grad_x, grad_x_other, output, d_2, d_3, d_0, d_1, y_2, x_3)
    batch_x, batch_y = x_swap(jnp.stack([add(x_2, d_2), x_3])), y_swap(jnp.stack([y_2, add(y_3, d_3)]))
    grad_normed_two = grad_x + core_swap_halves(grad_x_other).astype(F32)

    grad_norm_two, grad_gain_two = norm_backward(grad_normed_two, scaled_two, inverse_two, gain_two)
    grad_middle = grad_final + grad_norm_two
    grad_branch = grad_middle.astype(BF)
    grad_branch_both = jnp.concatenate([grad_branch, core_swap_halves(grad_branch)], axis=0)
    grad_mixed = matmul(grad_branch_both, w_out).astype(BF)
    half_width = mixed.shape[1] // 2

    def attend_back(n):
        lse = jnp.concatenate([parts[2 * n][1], parts[2 * n + 1][1]], axis=0)
        return attend_backward(scalars, queries, keys_all, values_all, mixed[:, n * half_width : (n + 1) * half_width], grad_mixed, lse, 2 * n)

    gq_a, gk_a, gv_a = attend_back(0)
    gq_a, grad_mixed, d_0, d_1 = event(gq_a, grad_mixed, d_0, d_1)
    d_0, d_1 = y_swap(d_0), x_swap(d_1)
    gq_b, gk_b, gv_b = attend_back(1)

    gq_b, batch_x, batch_y = event(gq_b, batch_x, batch_y)
    part_3 = z_swap(total_of(own_3, batch_x[1], batch_y[1]).astype(BF), 1)
    part_2 = total_of(own_2, batch_x[0], batch_y[0]).astype(BF)

    grad_queries = jnp.concatenate([gq_a, gq_b], axis=1)
    grad_keys = jnp.concatenate([gk_a, gk_b], axis=1)
    grad_values = jnp.concatenate([gv_a, gv_b], axis=1)
    part_all = (matmul_nt(grad_keys, w_keys) + matmul_nt(grad_values, w_values))
    part_own = part_all[: 2 * chunk] + matmul_nt(grad_queries, w_queries)
    part_own, part_other = part_own[:chunk], part_own[chunk:].astype(BF)
    part_own, part_other, part_all, grad_queries, grad_keys, grad_values = event(
        part_own, part_other, part_all[2 * chunk :], grad_queries, grad_keys, grad_values
    )
    part_other, other_partner_part = core_swap(part_other), core_swap(part_all[chunk:].astype(BF))

    grad_out = matmul_tn(grad_branch_both, mixed).astype(BF)
    grad_w_queries = matmul_tn(normed_own, grad_queries).astype(BF)
    grad_w_keys = matmul_tn(normed_all, grad_keys).astype(BF)
    grad_w_values = matmul_tn(normed_all, grad_values).astype(BF)
    quarter_cols = grad_w_queries.shape[1] // 4

    def attention_group(pieces):
        cols = [g[:, k * quarter_cols : (k + 1) * quarter_cols] for k in pieces for g in (grad_w_queries, grad_w_keys, grad_w_values, grad_out)]
        return jnp.split(jnp.concatenate(cols, axis=1), 4, axis=0)

    half_cols = 4 * quarter_cols
    own_e, x_e, y_e, d_e = attention_group((0, 1))
    own_o, x_o, y_o, d_o = attention_group((2, 3))
    own_e, own_o, x_e, y_e, d_e, x_o, y_o, d_o, d_0, d_1, x_1, y_0, part_other, other_partner_part = event(
        own_e, own_o, x_e, y_e, d_e, x_o, y_o, d_o, d_0, d_1, x_1, y_0, part_other, other_partner_part
    )
    batch_x, batch_y = x_swap(jnp.stack([add(x_0, d_0), x_1])), y_swap(jnp.stack([y_0, add(y_1, d_1)]))
    from_partner = z_swap((part_all[:chunk] + other_partner_part.astype(F32)).astype(BF), 1)
    part_3, part_2 = event(part_3, part_2)
    part_2 = z_swap(add(part_2, part_3), 2)
    (from_partner,) = event(from_partner)
    grad_normed_one = part_own + part_other.astype(F32) + from_partner.astype(F32)
    scaled_one, inverse_one = norm_forward(rows)
    grad_norm_one, grad_gain_one = norm_backward(grad_normed_one, scaled_one, inverse_one, gain_one)
    grad_rows, gain_a, gain_b, batch_x, batch_y = event(
        turn((grad_middle + grad_norm_one).astype(BF)), grad_gain_one, grad_gain_two, batch_x, batch_y
    )
    grad_inputs = home_swap(grad_rows)
    part_0 = total_of(own_0, batch_x[0], batch_y[0])
    part_1 = z_swap(total_of(own_1, batch_x[1], batch_y[1]).astype(BF), 1)
    d_e, d_o = y_swap(d_e), x_swap(d_o)
    d_e, d_o, y_e, x_o = event(d_e, d_o, y_e, x_o)
    batch_x, batch_y = x_swap(jnp.stack([add(x_e, d_e), x_o])), y_swap(jnp.stack([y_e, add(y_o, d_o)]))
    (grad_inputs,) = event(grad_inputs)
    part_1, part_2, part_0 = event(part_1, part_2, part_0)
    feed_total = part_0 + part_1.astype(F32) + part_2.astype(F32)
    feed_keep, feed_give = pick(jnp.split(feed_total, 2, axis=1))
    feed_give = core_swap(feed_give.astype(BF))

    quarter = model // 4
    a, b, c, d = jnp.split(jnp.stack([gain_a, gain_b], axis=0), 4, axis=1)
    sent = x_swap(jnp.concatenate([b, d], axis=1))

    batch_x, batch_y, sent = event(batch_x, batch_y, sent)
    even, odd = total_of(own_e, batch_x[0], batch_y[0]), total_of(own_o, batch_x[1], batch_y[1])
    att_3, att_1, att_2 = odd[:, half_cols:].astype(BF), even[:, half_cols:].astype(BF), odd[:, :half_cols].astype(BF)
    att_3, att_1, a, c, sent = event(att_3, att_1, a, c, sent)
    att_3, att_1 = z_swap(att_3, 1), z_swap(att_1, 1)
    a, c = a + sent[:, :quarter], c + sent[:, quarter:]
    sent = y_swap(c)
    att_3, att_2, sent = event(att_3, att_2, sent)
    att_2 = z_swap(add(att_2, att_3), 2)
    a = a + sent
    keep, give = pick(jnp.split(a, 2, axis=1))
    sent = core_swap(give)
    feed_give, sent = event(feed_give, sent)
    a = keep + sent
    size = a.shape[1] // 4
    total = lax.dynamic_slice_in_dim(a, z * size, size, 1)
    for k in range(1, 4):
        total = total + z_swap(lax.dynamic_slice_in_dim(a, (z ^ k) * size, size, 1), k)
    grad_gains = jnp.swapaxes(total, 0, 1)
    grad_inputs = grad_inputs.astype(F32)
    feed_out = sort_cores(feed_keep, feed_give.astype(F32), 2)
    attention_total = even[:, :half_cols] + att_1.astype(F32) + att_2.astype(F32)
    attention_total = jnp.stack([attention_total[:, n * quarter_cols : (n + 1) * quarter_cols] for n in range(4)])

    def to_home(total):
        keep, give = pick(jnp.split(total, 2, axis=1))
        return sort_cores(keep, core_swap(give.astype(BF)).astype(F32), 2)

    attention_out = to_home(attention_total)

    return (
        output,
        grad_inputs,
        jnp.swapaxes(attention_out[:3], 0, 1),
        attention_out[3],
        jnp.swapaxes(feed_out[:2], 0, 1),
        feed_out[2],
        grad_gains,
    )


def solution(mesh):
    square = dict(mesh.shape) == {"dp": 8, "tensor": 4}
    return jax.shard_map(
        on_square if square else on_device,
        mesh=mesh,
        in_specs=(
            P(("dp", "tensor"), None),
            P(("dp", "tensor"), None),
            P(),
            P("dp", None, "tensor"),
            P("dp", "tensor"),
            P("dp", None, "tensor"),
            P("dp", "tensor"),
            P("dp", None),
        ),
        out_specs=(
            P(("dp", "tensor"), None),
            P(("dp", "tensor"), None),
            P("dp", None, "tensor"),
            P("dp", "tensor"),
            P("dp", None, "tensor"),
            P("dp", "tensor"),
            P(("dp", "tensor"), None),
        ),
        check_vma=False,
    )
```

```python
import math

import jax
import jax.numpy as jnp
from jax import lax
from jax.experimental import pallas as pl
from jax.experimental.pallas import tpu as pltpu
from jax.sharding import PartitionSpec as P

HEAD = 64


negative = -1e30


def norm_forward(values):
    inverse = lax.rsqrt(jnp.mean(values * values, axis=-1, keepdims=True) + 1e-05)
    return (values * inverse, inverse)


def norm_backward(grad_normed, scaled, inverse, gain):
    grad_scaled = grad_normed * gain
    grad_values = inverse * (
        grad_scaled - scaled * jnp.mean(grad_scaled * scaled, axis=-1, keepdims=True)
    )
    return (grad_values, jnp.sum(grad_normed * scaled, axis=0))


def key_limit(query_index):
    return query_index + 1


def score_block(query_block, keys_all, query_start, key_start, length):
    block = query_block.shape[0]
    key_block = lax.dynamic_slice_in_dim(keys_all, key_start, block, 0)
    scores = jnp.einsum("qhe,khe->hqk", query_block, key_block, preferred_element_type=jnp.float32)
    query_pos = query_start + jnp.arange(block, dtype=jnp.int32)
    key_pos = key_start + jnp.arange(block, dtype=jnp.int32)
    allowed = (key_pos[None, :] <= query_pos[:, None]) & (key_pos[None, :] < length)
    return jnp.where(allowed[None], scores, negative)


def attention_forward(queries, keys_all, values_all, length):
    slot, heads, head = queries.shape
    block = min(512, slot)
    block_count = slot // block

    def query_step(index, carry):
        mixed, maxima, totals = carry
        query_start = index * block
        query_block = lax.dynamic_slice_in_dim(queries, query_start, block, 0)
        upper = key_limit(index)

        def stats_step(inner, state):
            maximum, total = state
            scores = score_block(query_block, keys_all, query_start, inner * block, length)
            larger = jnp.maximum(maximum, jnp.max(scores, axis=-1))
            total = total * jnp.exp(maximum - larger) + jnp.sum(
                jnp.exp(scores - larger[..., None]), axis=-1
            )
            return (larger, total)

        start_state = (
            jnp.full((heads, block), negative, jnp.float32),
            jnp.zeros((heads, block), jnp.float32),
        )
        maximum, total = lax.fori_loop(0, upper, stats_step, start_state)

        def mix_step(inner, accum):
            key_start = inner * block
            scores = score_block(query_block, keys_all, query_start, key_start, length)
            weights = (jnp.exp(scores - maximum[..., None]) / total[..., None]).astype(jnp.bfloat16)
            value_block = lax.dynamic_slice_in_dim(values_all, key_start, block, 0)
            return accum + jnp.einsum(
                "hqk,khe->qhe", weights, value_block, preferred_element_type=jnp.float32
            )

        accum = lax.fori_loop(0, upper, mix_step, jnp.zeros((block, heads, head), jnp.float32))
        mixed = lax.dynamic_update_slice_in_dim(mixed, accum, query_start, 0)
        maxima = lax.dynamic_update_index_in_dim(maxima, maximum, index, 0)
        totals = lax.dynamic_update_index_in_dim(totals, total, index, 0)
        return (mixed, maxima, totals)

    start = (
        jnp.zeros((slot, heads, head), jnp.float32),
        jnp.zeros((block_count, heads, block), jnp.float32),
        jnp.zeros((block_count, heads, block), jnp.float32),
    )
    return lax.fori_loop(0, block_count, query_step, start)


def attention_backward(queries, keys_all, values_all, grad_mixed, maxima, totals, length):
    slot, heads, head = queries.shape
    block = min(512, slot)
    block_count = slot // block

    def query_step(index, carry):
        grad_queries, grad_keys, grad_values = carry
        query_start = index * block
        query_block = lax.dynamic_slice_in_dim(queries, query_start, block, 0)
        grad_block = lax.dynamic_slice_in_dim(grad_mixed, query_start, block, 0)
        maximum = lax.dynamic_index_in_dim(maxima, index, 0, keepdims=False)
        total = lax.dynamic_index_in_dim(totals, index, 0, keepdims=False)
        upper = key_limit(index)

        def probs_of(inner):
            key_start = inner * block
            scores = score_block(query_block, keys_all, query_start, key_start, length)
            probs = jnp.exp(scores - maximum[..., None]) / total[..., None]
            value_block = lax.dynamic_slice_in_dim(values_all, key_start, block, 0)
            grad_probs = jnp.einsum(
                "qhe,khe->hqk", grad_block, value_block, preferred_element_type=jnp.float32
            )
            return (probs, grad_probs, key_start)

        def delta_step(inner, delta):
            probs, grad_probs, key_start = probs_of(inner)
            return delta + jnp.sum(probs * grad_probs, axis=-1)

        delta = lax.fori_loop(0, upper, delta_step, jnp.zeros((heads, block), jnp.float32))

        def grad_step(inner, state):
            grad_query, grad_keys, grad_values = state
            probs, grad_probs, key_start = probs_of(inner)
            grad_scores = (probs * (grad_probs - delta[..., None])).astype(jnp.bfloat16)
            key_block = lax.dynamic_slice_in_dim(keys_all, key_start, block, 0)
            grad_query = grad_query + jnp.einsum(
                "hqk,khe->qhe", grad_scores, key_block, preferred_element_type=jnp.float32
            )
            key_part = jnp.einsum(
                "hqk,qhe->khe", grad_scores, query_block, preferred_element_type=jnp.float32
            )
            value_part = jnp.einsum(
                "hqk,qhe->khe",
                probs.astype(jnp.bfloat16),
                grad_block,
                preferred_element_type=jnp.float32,
            )
            old_keys = lax.dynamic_slice_in_dim(grad_keys, key_start, block, 0)
            old_values = lax.dynamic_slice_in_dim(grad_values, key_start, block, 0)
            grad_keys = lax.dynamic_update_slice_in_dim(
                grad_keys, old_keys + key_part, key_start, 0
            )
            grad_values = lax.dynamic_update_slice_in_dim(
                grad_values, old_values + value_part, key_start, 0
            )
            return (grad_query, grad_keys, grad_values)

        start_state = (jnp.zeros((block, heads, head), jnp.float32), grad_keys, grad_values)
        grad_query, grad_keys, grad_values = lax.fori_loop(0, upper, grad_step, start_state)
        grad_queries = lax.dynamic_update_slice_in_dim(grad_queries, grad_query, query_start, 0)
        return (grad_queries, grad_keys, grad_values)

    empty = jnp.zeros((slot, heads, head), jnp.float32)
    return lax.fori_loop(0, block_count, query_step, (empty, empty, empty))


def on_device(inputs, teacher, lengths, w_qkv, w_out_t, w_gate_up, w_down_t, gains):
    own_rows = inputs.shape[0]
    slot = own_rows * lax.axis_size("tensor")
    total_rows = slot * lax.axis_size("dp")
    local_width = w_qkv.shape[2]
    local_heads = local_width // HEAD
    scale = 1.0 / math.sqrt(HEAD)
    length = lax.dynamic_index_in_dim(lengths, lax.axis_index("dp"), 0, keepdims=False)
    count = jnp.sum(lengths).astype(jnp.float32)
    own_start = lax.axis_index("tensor") * own_rows
    row_pos = own_start + jnp.arange(own_rows, dtype=jnp.int32)
    valid = (row_pos < length)[:, None]
    qkv_all, out_all, gains_all = (
        lax.all_gather(w_qkv, "dp", axis=0, tiled=True),
        lax.all_gather(w_out_t, "dp", axis=0, tiled=True),
        lax.all_gather(gains, "dp", axis=0, tiled=True),
    )
    gate_up_all, down_all = (
        lax.all_gather(w_gate_up, "dp", axis=0, tiled=True),
        lax.all_gather(w_down_t, "dp", axis=0, tiled=True),
    )
    gain_one = gains_all[:, 0].astype(jnp.float32)
    gain_two = gains_all[:, 1].astype(jnp.float32)
    rows = inputs.astype(jnp.float32)
    scaled_one, inverse_one = norm_forward(rows)
    normed_one = (scaled_one * gain_one).astype(jnp.bfloat16)
    gathered_one = lax.all_gather(normed_one, "tensor", axis=0, tiled=True)
    qkv = jnp.einsum("rd,dcf->rcf", gathered_one, qkv_all, preferred_element_type=jnp.float32)
    queries = (qkv[:, 0] * scale).astype(jnp.bfloat16).reshape(slot, local_heads, HEAD)
    keys_all = qkv[:, 1].astype(jnp.bfloat16).reshape(slot, local_heads, HEAD)
    values_all = qkv[:, 2].astype(jnp.bfloat16).reshape(slot, local_heads, HEAD)
    mixed, maxima, totals = attention_forward(queries, keys_all, values_all, length)
    mixed = mixed.reshape(slot, local_width).astype(jnp.bfloat16)
    piece = mixed
    middle = rows + lax.psum_scatter(
        jnp.einsum("rk,dk->rd", piece, out_all, preferred_element_type=jnp.float32).astype(
            jnp.bfloat16
        ),
        "tensor",
        scatter_dimension=0,
        tiled=True,
    ).astype(jnp.float32)
    scaled_two, inverse_two = norm_forward(middle)
    normed_two = (scaled_two * gain_two).astype(jnp.bfloat16)
    gathered_two = lax.all_gather(normed_two, "tensor", axis=0, tiled=True)
    rows_two = None
    gate_up = jnp.einsum(
        "rd,dcf->rcf", gathered_two, gate_up_all, preferred_element_type=jnp.float32
    )
    gate = gate_up[:, 0]
    upper = gate_up[:, 1]
    sigmoid = jax.nn.sigmoid(gate)
    hidden = (gate * sigmoid * upper).astype(jnp.bfloat16)
    piece = hidden
    final = middle + lax.psum_scatter(
        jnp.einsum("rf,df->rd", piece, down_all, preferred_element_type=jnp.float32).astype(
            jnp.bfloat16
        ),
        "tensor",
        scatter_dimension=0,
        tiled=True,
    ).astype(jnp.float32)
    output = final.astype(jnp.bfloat16)
    grad_final = jnp.where(valid, final - teacher.astype(jnp.float32), 0.0) * (total_rows / count)
    grad_feed = lax.all_gather(grad_final.astype(jnp.bfloat16), "tensor", axis=0, tiled=True)
    grad_down = jnp.einsum("rd,rf->df", grad_feed, hidden, preferred_element_type=jnp.float32)
    grad_hidden = jnp.einsum("rd,df->rf", grad_feed, down_all, preferred_element_type=jnp.float32)
    grad_gate = grad_hidden * upper * (sigmoid * (1.0 + gate * (1.0 - sigmoid)))
    grad_upper = grad_hidden * (gate * sigmoid)
    grad_gu = jnp.stack([grad_gate, grad_upper], axis=1).astype(jnp.bfloat16)
    rows_two = lax.all_gather(normed_two, "tensor", axis=0, tiled=True)
    grad_gate_up = jnp.einsum("rd,rcf->dcf", rows_two, grad_gu, preferred_element_type=jnp.float32)
    piece = grad_gu
    grad_normed_two = lax.psum_scatter(
        jnp.einsum("rcf,dcf->rd", piece, gate_up_all, preferred_element_type=jnp.float32).astype(
            jnp.bfloat16
        ),
        "tensor",
        scatter_dimension=0,
        tiled=True,
    ).astype(jnp.float32)
    grad_norm_two, grad_gain_two = norm_backward(grad_normed_two, scaled_two, inverse_two, gain_two)
    grad_middle = grad_final + grad_norm_two
    grad_branch = lax.all_gather(grad_middle.astype(jnp.bfloat16), "tensor", axis=0, tiled=True)
    grad_out = jnp.einsum("rd,rk->dk", grad_branch, mixed, preferred_element_type=jnp.float32)
    grad_mixed = jnp.einsum("rd,dk->rk", grad_branch, out_all, preferred_element_type=jnp.float32)
    grad_mixed = grad_mixed.astype(jnp.bfloat16).reshape(slot, local_heads, HEAD)
    grad_queries, grad_keys, grad_values = attention_backward(
        queries, keys_all, values_all, grad_mixed, maxima, totals, length
    )
    grad_rows_qkv = jnp.stack(
        [
            grad_queries.reshape(slot, local_width).astype(jnp.bfloat16) * scale,
            grad_keys.reshape(slot, local_width).astype(jnp.bfloat16),
            grad_values.reshape(slot, local_width).astype(jnp.bfloat16),
        ],
        axis=1,
    )
    rows_one = lax.all_gather(normed_one, "tensor", axis=0, tiled=True)
    grad_qkv = jnp.einsum(
        "rd,rcf->dcf", rows_one, grad_rows_qkv, preferred_element_type=jnp.float32
    )
    piece = grad_rows_qkv
    grad_normed_one = lax.psum_scatter(
        jnp.einsum("rcf,dcf->rd", piece, qkv_all, preferred_element_type=jnp.float32).astype(
            jnp.bfloat16
        ),
        "tensor",
        scatter_dimension=0,
        tiled=True,
    ).astype(jnp.float32)
    grad_norm_one, grad_gain_one = norm_backward(grad_normed_one, scaled_one, inverse_one, gain_one)
    grad_inputs = grad_middle + grad_norm_one
    grad_qkv, grad_out, grad_gate_up, grad_down = (
        lax.psum_scatter(
            grad_qkv.astype(jnp.bfloat16), "dp", scatter_dimension=0, tiled=True
        ).astype(jnp.float32),
        lax.psum_scatter(
            grad_out.astype(jnp.bfloat16), "dp", scatter_dimension=0, tiled=True
        ).astype(jnp.float32),
        lax.psum_scatter(
            grad_gate_up.astype(jnp.bfloat16), "dp", scatter_dimension=0, tiled=True
        ).astype(jnp.float32),
        lax.psum_scatter(
            grad_down.astype(jnp.bfloat16), "dp", scatter_dimension=0, tiled=True
        ).astype(jnp.float32),
    )
    grad_gains = lax.psum_scatter(
        jnp.stack([grad_gain_one, grad_gain_two], axis=1),
        ("dp", "tensor"),
        scatter_dimension=0,
        tiled=True,
    )
    return (output, grad_inputs, grad_qkv, grad_out, grad_gate_up, grad_down, grad_gains)


BF = jnp.bfloat16
F32 = jnp.float32
AXES = ("dp", "tensor")
LIGHT = pl.CostEstimate(flops=1000, bytes_accessed=1000, transcendentals=0)


def shift(value, where):
    pairs = []
    for y in range(2):
        for x in range(2):
            for c in range(2):
                for z in range(4):
                    to = where(y, x, c, z)
                    if to is not None:
                        ty, tx, tc, tz = to
                        pairs.append((((y * 2 + x) * 2 + c) * 4 + z, ((ty * 2 + tx) * 2 + tc) * 4 + tz))
    return lax.ppermute(value, AXES, pairs)


def core_swap(value):
    return shift(value, lambda y, x, c, z: (y, x, 1 - c, z))


def core_swap_halves(value):
    half = value.shape[0] // 2
    return jnp.concatenate([core_swap(value[:half]), core_swap(value[half:])], axis=0)


def x_swap(value):
    return shift(value, lambda y, x, c, z: (y, 1 - x, c, z))


def y_swap(value):
    return shift(value, lambda y, x, c, z: (1 - y, x, c, z))


def square_swap(value):
    return shift(value, lambda y, x, c, z: (1 - y, 1 - x, c, z))


def z_swap(value, bits):
    return shift(value, lambda y, x, c, z: (y, x, c, z ^ bits))


def home_of(y, x, c, z):
    if (c == 1 and z < 2) or (c == 0 and z >= 2):
        return (y, x, 1 - c, 3 - z)
    return (y, x, c, z)


def home_swap(value):
    return shift(value, home_of)


def moved_home(value):
    return shift(value, lambda *place: None if home_of(*place) == place else home_of(*place))


def partner_of_home(y, x, c, z):
    y, x, c, z = home_of(y, x, c, z)
    z ^= 1
    if c == 1 and z in (1, 2):
        return None
    return (y, x, c, z)


def head_masks(rows):
    lanes = lax.broadcasted_iota(jnp.int32, (rows, 2 * HEAD), 1)
    return (lanes < HEAD, lanes >= HEAD)


def dot_nt(a, b):
    return lax.dot_general(a, b, (((1,), (1,)), ((), ())), preferred_element_type=F32)


def dot_nn(a, b):
    return lax.dot_general(a, b, (((1,), (0,)), ((), ())), preferred_element_type=F32)


def dot_tn(a, b):
    return lax.dot_general(a, b, (((0,), (0,)), ((), ())), preferred_element_type=F32)


def attend_forward_kernel(outer_ref, sc_ref, q_ref, k_ref, v_ref, o_ref, lse_ref):
    chunk = q_ref.shape[0] // 2
    tile = chunk // 2
    lanes = 2 * HEAD
    head = pl.program_id(0) % 2
    low, high, low_partner, extra_row, extra_key = [pl.multiple_of(sc_ref[i], chunk) for i in range(5)]
    mine = lax.broadcasted_iota(jnp.int32, (tile, lanes), 1) // HEAD == head

    def fold(op, parts):
        parts = [p[:, i * lanes : (i + 1) * lanes] for p in parts for i in range(p.shape[1] // lanes)]
        while len(parts) > 1:
            parts = [op(parts[i], parts[i + 1]) if i + 1 < len(parts) else parts[i] for i in range(0, len(parts), 2)]
        return parts[0]

    def unit(row, own, own_count, half, others):
        rows = pl.ds(pl.multiple_of(row + half * tile, tile), tile)
        query = jnp.where(mine, q_ref[rows, :], 0)
        blocks = [(pl.ds(start, chunk), count, chunk, None) for start, count in others]
        blocks.append((pl.ds(own, (half + 1) * tile), own_count, (half + 1) * tile, half * tile))
        scores = []
        for keys, count, width, diagonal in blocks:
            s = dot_nt(query, k_ref[keys, :])
            s = s + jnp.where(lax.broadcasted_iota(jnp.int32, (1, width), 1) < count, 0.0, negative)
            if diagonal is not None:
                cols = lax.broadcasted_iota(jnp.int32, (tile, width), 1)
                s = jnp.where(cols <= lax.broadcasted_iota(jnp.int32, (tile, width), 0) + diagonal, s, negative)
            scores.append(s)
        top = jnp.max(fold(jnp.maximum, scores), axis=1, keepdims=True)
        weights = [jnp.exp(s - top) for s in scores]
        total = jnp.sum(fold(jnp.add, weights), axis=1, keepdims=True)
        mixed = None
        for w, (keys, _, _, _) in zip(weights, blocks):
            part = dot_nn(w.astype(BF), v_ref[keys, :])
            mixed = part if mixed is None else mixed + part
        return rows, mixed / total, top + jnp.log(total)

    def finish(units):
        for rows, mixed, lse in units:
            mixed = mixed.astype(BF)
            o_ref[rows, :] = jnp.where(mine, mixed, o_ref[rows, :])
            lse_ref[0, pl.ds(head, 1), rows] = jnp.transpose(jnp.broadcast_to(lse, (tile, lanes)))[0:1]

    near = [(low, sc_ref[5]), (low_partner, sc_ref[7])]
    extra = [(extra_key, sc_ref[8])]

    @pl.when(outer_ref[0] == 1)
    def _():
        for half in range(2):
            finish([unit(high, high, sc_ref[6], half, near + extra), unit(low, low, sc_ref[5], half, [])])

    @pl.when(outer_ref[0] == 0)
    def _():
        for half in range(2):
            finish([unit(high, high, sc_ref[6], half, near), unit(low, low, sc_ref[5], half, extra)])


def attend_forward(outer, scalars, queries, keys_all, values_all, start, pairs):
    rows = queries.shape[0]
    width = pairs * 2 * HEAD
    slot = keys_all.shape[0]
    own = lambda i, *_: (0, i // 2)
    column = lambda i, *_: (0, i // 2 + start)
    return pl.pallas_call(
        attend_forward_kernel,
        out_shape=(
            jax.ShapeDtypeStruct((rows, width), BF),
            jax.ShapeDtypeStruct((pairs, 8, rows), F32),
        ),
        grid_spec=pltpu.PrefetchScalarGridSpec(
            num_scalar_prefetch=2,
            grid=(2 * pairs,),
            in_specs=[
                pl.BlockSpec((rows, 2 * HEAD), column),
                pl.BlockSpec((slot, 2 * HEAD), column),
                pl.BlockSpec((slot, 2 * HEAD), column),
            ],
            out_specs=(
                pl.BlockSpec((rows, 2 * HEAD), own),
                pl.BlockSpec((1, 8, rows), lambda i, *_: (i // 2, 0, 0)),
            ),
        ),
        compiler_params=pltpu.CompilerParams(vmem_limit_bytes=24 << 20),
        cost_estimate=LIGHT,
        name="attend_forward",
    )(outer, scalars, queries, keys_all, values_all)


def attend_backward_kernel(sc_ref, q_ref, k_ref, v_ref, o_ref, g_ref, lse_ref, dq_ref, dk_ref, dv_ref, dq_acc, dk_acc, dv_acc, delta_ref):
    chunk = q_ref.shape[0] // 2
    tile = chunk // 2
    low, high_row, low_partner, extra_row, extra_key = [pl.multiple_of(sc_ref[i], chunk) for i in range(5)]
    dq_acc[...] = jnp.zeros_like(dq_acc)
    dk_acc[...] = jnp.zeros_like(dk_acc)
    dv_acc[...] = jnp.zeros_like(dv_acc)
    for part in range(4):
        rows = pl.ds(part * tile, tile)
        product = jnp.transpose(o_ref[rows, :].astype(F32) * g_ref[rows, :].astype(F32))
        delta_ref[0:1, rows] = jnp.sum(product[:HEAD], axis=0, keepdims=True)
        delta_ref[1:2, rows] = jnp.sum(product[HEAD:], axis=0, keepdims=True)

    def step(head, row, width, key, count, shift_rows):
        rows = pl.ds(row, width)
        keys = pl.ds(key, tile)
        query = jnp.where(head_masks(width)[head], q_ref[rows, :], 0)
        grad = jnp.where(head_masks(width)[head], g_ref[rows, :], 0)
        key_block = k_ref[keys, :]
        scores = dot_nt(key_block, query)
        index = lax.broadcasted_iota(jnp.int32, (tile, width), 0)
        allowed = index < count
        if shift_rows is not None:
            allowed = allowed & (index <= lax.broadcasted_iota(jnp.int32, (tile, width), 1) + shift_rows)
        probs = jnp.exp(jnp.where(allowed, scores, negative) - lse_ref[0, head : head + 1, rows])
        grad_probs = dot_nt(v_ref[keys, :], grad)
        grad_scores = (probs * (grad_probs - delta_ref[head : head + 1, rows])).astype(BF)
        dv_acc[keys, :] += dot_nn(probs.astype(BF), grad)
        dk_acc[keys, :] += dot_nn(grad_scores, query)
        key_masked = jnp.where(head_masks(tile)[head], key_block, 0)
        dq_acc[rows, :] += dot_tn(grad_scores, key_masked)

    for head in range(2):
        for half in range(2):
            down = half * tile
            add = lambda start: pl.multiple_of(start + down, tile)
            step(head, add(low), chunk - down, add(low), sc_ref[5] - down, 0)
            step(head, add(high_row), chunk - down, add(high_row), sc_ref[6] - down, 0)
            step(head, high_row, chunk, add(low), sc_ref[5] - down, None)
            step(head, high_row, chunk, add(low_partner), sc_ref[7] - down, None)
            step(head, extra_row, chunk, add(extra_key), sc_ref[8] - down, None)
    dq_ref[...] = (dq_acc[...] * (1.0 / math.sqrt(HEAD))).astype(BF)
    dk_ref[...] = dk_acc[...].astype(BF)
    dv_ref[...] = dv_acc[...].astype(BF)


def attend_backward(scalars, queries, keys_all, values_all, mixed, grad_mixed, lse, start):
    rows, width = mixed.shape
    pairs = width // (2 * HEAD)
    slot = keys_all.shape[0]
    own = lambda i, sc: (0, i)
    column = lambda i, sc: (0, i + start)
    own_spec = pl.BlockSpec((rows, 2 * HEAD), own)
    row_spec = pl.BlockSpec((rows, 2 * HEAD), column)
    slot_spec = pl.BlockSpec((slot, 2 * HEAD), column)
    return pl.pallas_call(
        attend_backward_kernel,
        out_shape=(
            jax.ShapeDtypeStruct((rows, width), BF),
            jax.ShapeDtypeStruct((slot, width), BF),
            jax.ShapeDtypeStruct((slot, width), BF),
        ),
        grid_spec=pltpu.PrefetchScalarGridSpec(
            num_scalar_prefetch=1,
            grid=(pairs,),
            in_specs=[row_spec, slot_spec, slot_spec, own_spec, row_spec, pl.BlockSpec((1, 8, rows), lambda i, sc: (i, 0, 0))],
            out_specs=(own_spec, pl.BlockSpec((slot, 2 * HEAD), own), pl.BlockSpec((slot, 2 * HEAD), own)),
            scratch_shapes=[
                pltpu.VMEM((rows, 2 * HEAD), F32),
                pltpu.VMEM((slot, 2 * HEAD), F32),
                pltpu.VMEM((slot, 2 * HEAD), F32),
                pltpu.VMEM((8, rows), F32),
            ],
        ),
        compiler_params=pltpu.CompilerParams(vmem_limit_bytes=32 << 20),
        cost_estimate=LIGHT,
    )(scalars, queries, keys_all, values_all, mixed, grad_mixed, lse)


def project_kernel(*refs):
    rows_refs, gain_ref, weight_refs = refs[:4], refs[4], (refs[5:9], refs[9:13])
    normed_ref, q_ref, k_ref, v_ref, wq_ref, wk_ref, wv_ref, wo_ref = refs[13:]
    step = pl.program_id(0)
    _, block, width = weight_refs[0][0].shape
    part = width // 4
    tile = rows_refs[0].shape[0] // 2

    @pl.when(step == 0)
    def _():
        for k in range(4):
            for r in range(4):
                source = weight_refs[k // 2][r].at[k % 2]
                for n, out in enumerate((wq_ref, wk_ref, wv_ref, wo_ref)):
                    out[r * block : (r + 1) * block, k * part : (k + 1) * part] = source[:, n * part : (n + 1) * part]

    for n in range(4):

        @pl.when(step == n)
        def _():
            for half in range(2):
                rows = slice(half * tile, (half + 1) * tile)
                values = rows_refs[n][rows, :].astype(F32)
                inverse = lax.rsqrt(jnp.mean(values * values, axis=-1, keepdims=True) + 1e-05)
                normed = (values * inverse * gain_ref[...]).astype(BF)
                normed_ref[rows, :] = normed
                k_ref[rows, :] = dot_nn(normed, wk_ref[...]).astype(BF)
                v_ref[rows, :] = dot_nn(normed, wv_ref[...]).astype(BF)
                if n < 2:
                    q_ref[rows, :] = (dot_nn(normed, wq_ref[...]) * (1.0 / math.sqrt(HEAD))).astype(BF)


def project(rows_parts, gain, weights):
    chunk, model = rows_parts[0].shape
    _, block, width = weights[0].shape
    whole = lambda shape: pl.BlockSpec(shape, lambda i: (0,) * len(shape))
    tiles = lambda cols: pl.BlockSpec((chunk, cols), lambda i: (i, 0))
    shape = lambda r, c: jax.ShapeDtypeStruct((r, c), BF)
    return pl.pallas_call(
        project_kernel,
        out_shape=(
            shape(4 * chunk, model),
            shape(2 * chunk, width),
            shape(4 * chunk, width),
            shape(4 * chunk, width),
            shape(model, width),
            shape(model, width),
            shape(model, width),
            shape(model, width),
        ),
        grid=(4,),
        in_specs=[whole((chunk, model))] * 4 + [whole((1, model))] + [whole(w.shape) for w in weights],
        out_specs=(
            tiles(model),
            pl.BlockSpec((chunk, width), lambda i: (jnp.minimum(i, 1), 0)),
            tiles(width),
            tiles(width),
        )
        + tuple(whole((model, width)) for _ in range(4)),
        compiler_params=pltpu.CompilerParams(vmem_limit_bytes=60 << 20),
        cost_estimate=LIGHT,
        name="project",
    )(*rows_parts, gain, *weights)


def rows_grads_kernel(dq_ref, dk_ref, dv_ref, wq_ref, wk_ref, wv_ref, own_ref, other_ref, partner_ref, partner_other_ref):
    step = pl.program_id(0)
    part = dot_nt(dk_ref[...], wk_ref[...]) + dot_nt(dv_ref[...], wv_ref[...])

    @pl.when(step == 0)
    def _():
        own_ref[...] = part + dot_nt(dq_ref[...], wq_ref[...])

    @pl.when(step == 1)
    def _():
        other_ref[...] = (part + dot_nt(dq_ref[...], wq_ref[...])).astype(BF)

    @pl.when(step == 2)
    def _():
        partner_ref[...] = part

    @pl.when(step == 3)
    def _():
        partner_other_ref[...] = part.astype(BF)


def rows_grads(dq, dk, dv, wq, wk, wv):
    slot, width = dk.shape
    model = wq.shape[0]
    chunk = slot // 4
    whole = pl.BlockSpec((model, width), lambda i: (0, 0))
    tiles = pl.BlockSpec((chunk, width), lambda i: (i, 0))
    out = pl.BlockSpec((chunk, model), lambda i: (0, 0))
    shape = lambda t: jax.ShapeDtypeStruct((chunk, model), t)
    return pl.pallas_call(
        rows_grads_kernel,
        out_shape=(shape(F32), shape(BF), shape(F32), shape(BF)),
        grid=(4,),
        in_specs=[pl.BlockSpec((chunk, width), lambda i: (jnp.minimum(i, 1), 0)), tiles, tiles, whole, whole, whole],
        out_specs=(out,) * 4,
        compiler_params=pltpu.CompilerParams(vmem_limit_bytes=40 << 20),
        cost_estimate=LIGHT,
        name="rows_grads",
    )(dq, dk, dv, wq, wk, wv)


def attention_grads_kernel(x_ref, g_ref, dq_ref, dk_ref, dv_ref, mixed_ref, *out_refs):
    rows = g_ref.shape[0]
    x_turned = jnp.transpose(x_ref[...])
    g_turned = jnp.transpose(g_ref[...])
    grads = (
        dot_nn(x_turned[:, :rows], dq_ref[...]),
        dot_nn(x_turned, dk_ref[...]),
        dot_nn(x_turned, dv_ref[...]),
        dot_nn(g_turned, mixed_ref[...]),
    )
    part = dq_ref.shape[1] // 4
    for r in range(4):

        @pl.when(pl.program_id(0) == r)
        def _():
            for k in range(4):
                for n in range(4):
                    start = (k % 2 * 4 + n) * part
                    out_refs[k // 2 * 4 + r][:, start : start + part] = grads[n][:, k * part : (k + 1) * part].astype(BF)


def attention_grads(x, g, dq, dk, dv, mixed):
    rows, model = g.shape
    slot, width = dk.shape
    block = model // 4
    whole = lambda a: pl.BlockSpec(a.shape, lambda i: (0, 0))
    out = pl.pallas_call(
        attention_grads_kernel,
        out_shape=(jax.ShapeDtypeStruct((block, 2 * width), BF),) * 8,
        grid=(4,),
        in_specs=[
            pl.BlockSpec((slot, block), lambda i: (0, i)),
            pl.BlockSpec((rows, block), lambda i: (0, i)),
            whole(dq),
            whole(dk),
            whole(dv),
            whole(mixed),
        ],
        out_specs=(pl.BlockSpec((block, 2 * width), lambda i: (0, 0)),) * 8,
        compiler_params=pltpu.CompilerParams(vmem_limit_bytes=40 << 20),
        cost_estimate=LIGHT,
        name="attention_grads",
    )(x, g, dq, dk, dv, mixed)
    return out[:4], out[4:]


def norm_grads_kernel(part_ref, first_ref, second_ref, values_ref, grad_ref, gain_ref, out_ref, low_ref, gain_grad_ref):
    step = pl.program_id(0)
    values = values_ref[...]
    inverse = lax.rsqrt(jnp.mean(values * values, axis=-1, keepdims=True) + 1e-05)
    scaled = values * inverse

    @pl.when(step == 0)
    def _():
        gain_grad_ref[...] = jnp.zeros_like(gain_grad_ref)

    received = jnp.where(step < 2, first_ref[...].astype(F32), second_ref[...].astype(F32))
    grad_normed = part_ref[...] + received
    grad_scaled = grad_normed * gain_ref[...]
    grad = grad_ref[...] + inverse * (grad_scaled - scaled * jnp.mean(grad_scaled * scaled, axis=-1, keepdims=True))
    out_ref[...] = grad
    low_ref[...] = grad.astype(BF)
    gain_grad_ref[...] += jnp.sum(grad_normed * scaled, axis=0, keepdims=True)


def norm_grads(part, first, second, values, grad, gain):
    rows, model = part.shape
    tile = rows // 4
    tiles = pl.BlockSpec((tile, model), lambda i: (i, 0))
    row = pl.BlockSpec((1, model), lambda i: (0, 0))
    return pl.pallas_call(
        norm_grads_kernel,
        out_shape=(
            jax.ShapeDtypeStruct((rows, model), F32),
            jax.ShapeDtypeStruct((rows, model), BF),
            jax.ShapeDtypeStruct((1, model), F32),
        ),
        grid=(4,),
        in_specs=[
            tiles,
            pl.BlockSpec((tile, model), lambda i: (jnp.minimum(i, 1), 0)),
            pl.BlockSpec((tile, model), lambda i: (jnp.maximum(i - 2, 0), 0)),
            tiles,
            tiles,
            row,
        ],
        out_specs=(tiles, tiles, row),
        compiler_params=pltpu.CompilerParams(vmem_limit_bytes=24 << 20),
        cost_estimate=LIGHT,
        name="norm_grads",
    )(part, first, second, values, grad, gain[None])


def feed_forward_kernel(first_piece, *refs):
    x_ref, weight_refs = refs[0], refs[1:5]
    block = weight_refs[0].shape[1]
    if not first_piece:
        y_in_ref = refs[5]
    silu_ref, slope_ref, hidden_ref, y_ref = refs[-4:]
    x = x_ref[...]
    gate = upper = None
    for r in range(4):
        part = x[:, r * block : (r + 1) * block]
        g = dot_nn(part, weight_refs[r][0])
        u = dot_nn(part, weight_refs[r][1])
        gate = g if gate is None else gate + g
        upper = u if upper is None else upper + u
    sigmoid = jax.nn.sigmoid(gate)
    silu = gate * sigmoid
    hidden = (silu * upper).astype(BF)
    silu_ref[...] = silu.astype(BF)
    slope_ref[...] = (upper * (sigmoid * (1.0 + gate * (1.0 - sigmoid)))).astype(BF)
    hidden_ref[...] = hidden
    for r in range(4):
        cols = slice(r * block, (r + 1) * block)
        y = dot_nt(hidden, weight_refs[r][2])
        y_ref[:, cols] = y if first_piece else y + y_in_ref[:, cols]


def alone(piece):
    return (piece[None], 0)


def feed_forward(x, pieces, y):
    rows, model = x.shape
    _, _, block, width = pieces[0][0].shape
    tile = rows // 4
    tiles = lambda cols: pl.BlockSpec((tile, cols), lambda i: (i, 0))
    weight_specs = [pl.BlockSpec((None, 3, block, width), lambda i, n=n: (n, 0, 0, 0)) for _, n in pieces]
    extra = [] if y is None else [y]
    return pl.pallas_call(
        lambda *refs: feed_forward_kernel(y is None, *refs),
        out_shape=tuple(jax.ShapeDtypeStruct((rows, width), BF) for _ in range(3)) + (jax.ShapeDtypeStruct((rows, model), F32),),
        grid=(4,),
        in_specs=[tiles(model)] + weight_specs + [tiles(model) for _ in extra],
        out_specs=(tiles(width), tiles(width), tiles(width), tiles(model)),
        input_output_aliases={5: 3} if extra else {},
        compiler_params=pltpu.CompilerParams(vmem_limit_bytes=24 << 20),
        cost_estimate=LIGHT,
        name="feed_forward",
    )(x, *[w for w, _ in pieces], *extra)


def feed_backward_kernel(places, has_sum, last, *refs):
    count = len(places) // 4
    refs = list(refs)
    take = lambda n: [refs.pop(0) for _ in range(n)]
    x_ref, g_ref = take(2)
    silu_hbm, slope_hbm, hidden_hbm, weight_hbm = take(count), take(count), take(count), take(4 * count)
    sum_ref = take(1)[0] if has_sum else None
    dx_ref, dx_other_ref = take(2) if last else take(1) * 2
    out_hbm = take(4 * count)
    xt_ref, gt_ref, kept_ref, hidden_ref, gu_ref, down_ref, acc_ref, out_ref, act_sem, weight_sem, out_sem = refs
    _, _, block, width = weight_hbm[0].shape
    rows_all = x_ref.shape[0]
    half = rows_all // 2
    copies_of, late_copies = [], []
    for p in range(count):
        copies = []
        for n, source in enumerate((slope_hbm[p], silu_hbm[p])):
            copies.append(pltpu.make_async_copy(source, kept_ref.at[p, :, pl.ds(n * width, width)], act_sem.at[p, n]))
        for r in range(4):
            features = pl.ds(r * block, block)
            source = weight_hbm[p * 4 + r].at[places[p * 4 + r]]
            for n, target in enumerate((gu_ref.at[p, features, pl.ds(0, width)], gu_ref.at[p, features, pl.ds(width, width)], down_ref.at[p, features, :])):
                copies.append(pltpu.make_async_copy(source.at[n], target, weight_sem.at[p, r, n]))
        copies_of.append(copies)
        late_copies.append(pltpu.make_async_copy(hidden_hbm[p], hidden_ref.at[p], act_sem.at[p, 2]))
    for copy in copies_of[0]:
        copy.start()
    for t in range(4):
        rows = slice(t * rows_all // 4, (t + 1) * rows_all // 4)
        xt_ref[:, rows] = jnp.transpose(x_ref[rows, :])
        gt_ref[:, rows] = jnp.transpose(g_ref[rows, :])

    for p in range(count):
        for copy in copies_of[p]:
            copy.wait()
        for copy in copies_of[p + 1] if p < count - 1 else late_copies:
            copy.start()
        for t in range(2):
            rows = slice(t * half, (t + 1) * half)
            grad_hidden = dot_nn(g_ref[rows, :], down_ref[p])
            kept_ref[p, rows, :width] = (grad_hidden * kept_ref[p, rows, :width].astype(F32)).astype(BF)
            kept_ref[p, rows, width:] = (grad_hidden * kept_ref[p, rows, width:].astype(F32)).astype(BF)
            part = dot_nt(kept_ref[p, rows, :], gu_ref[p])
            if p > 0:
                part = acc_ref[rows, :] + part
            elif has_sum:
                part = sum_ref[rows, :] + part
            if p < count - 1:
                acc_ref[rows, :] = part
            elif not last:
                dx_ref[rows, :] = part
            elif t == 0:
                dx_ref[...] = part
            else:
                dx_other_ref[...] = part.astype(BF)

    slots = out_ref.shape[0]
    copies = []
    for p in range(count):
        late_copies[p].wait()
        for r in range(3, -1, -1):
            features = slice(r * block, (r + 1) * block)
            slot = len(copies) % slots
            if len(copies) >= slots:
                copies[len(copies) - slots].wait()
            gu = dot_nn(xt_ref[features, :], kept_ref[p]).astype(BF)
            out_ref[slot, 0] = gu[:, :width]
            out_ref[slot, 1] = gu[:, width:]
            out_ref[slot, 2] = dot_nn(gt_ref[features, :], hidden_ref[p]).astype(BF)
            copies.append(pltpu.make_async_copy(out_ref.at[slot], out_hbm[p * 4 + r], out_sem.at[slot]))
            copies[-1].start()
    for copy in copies[-slots:]:
        copy.wait()


def feed_backward(x, g, silus, slopes, hiddens, pieces, total, last):
    count = len(pieces)
    extra = [] if total is None else [total]
    rows, model = x.shape
    _, _, block, width = pieces[0][0][0].shape
    places = [n for piece in pieces for _, n in piece]
    vmem = pl.BlockSpec(memory_space=pltpu.VMEM)
    hbm = pl.BlockSpec(memory_space=pl.ANY)
    outs = pl.pallas_call(
        lambda *refs: feed_backward_kernel(places, total is not None, last, *refs),
        out_shape=(
            (jax.ShapeDtypeStruct((rows // 2, model), F32), jax.ShapeDtypeStruct((rows // 2, model), BF))
            if last
            else (jax.ShapeDtypeStruct((rows, model), F32),)
        )
        + tuple(jax.ShapeDtypeStruct((3, block, width), BF) for _ in range(4 * count)),
        in_specs=[vmem] * 2 + [hbm] * (7 * count) + [vmem] * len(extra),
        out_specs=((vmem, vmem) if last else (vmem,)) + (hbm,) * (4 * count),
        scratch_shapes=[
            pltpu.VMEM((model, rows), BF),
            pltpu.VMEM((model, rows), BF),
            pltpu.VMEM((count, rows, 2 * width), BF),
            pltpu.VMEM((count, rows, width), BF),
            pltpu.VMEM((count, model, 2 * width), BF),
            pltpu.VMEM((count, model, width), BF),
            pltpu.VMEM((rows, model), F32),
            pltpu.VMEM((3, 3, block, width), BF),
            pltpu.SemaphoreType.DMA((count, 3)),
            pltpu.SemaphoreType.DMA((count, 4, 3)),
            pltpu.SemaphoreType.DMA((3,)),
        ],
        compiler_params=pltpu.CompilerParams(vmem_limit_bytes=60 << 20),
        cost_estimate=LIGHT,
        name="feed_backward",
    )(x, g, *silus, *slopes, *hiddens, *[w for piece in pieces for w, _ in piece], *extra)
    first = 2 if last else 1
    return outs[:first], [outs[first + 4 * p : first + 4 + 4 * p] for p in range(count)]


class Order:
    def __init__(self):
        self.last = ()

    def event(self, *values):
        out = lax.optimization_barrier((*values, *self.last))[: len(values)]
        self.last = out
        return out


def on_square(inputs, teacher, lengths, w_qkv, w_out_t, w_gate_up, w_down_t, gains):
    chunk, model = inputs.shape
    slot = chunk * 4
    total_rows = slot * 8
    dp = lax.axis_index("dp")
    z = lax.axis_index("tensor")
    core = dp % 2
    first = core == 0
    odd_x = (dp // 2) % 2 == 1
    odd_y = dp // 4 == 1
    inner = jnp.where((z == 1) | (z == 2), 1, 0)
    moves = (core == 1) == (z < 2)
    chunk_low, chunk_high = inner, 3 - inner
    length = lax.dynamic_index_in_dim(lengths, (dp // 2) * 2 + z // 2, 0, keepdims=False)
    count = jnp.sum(lengths).astype(F32)
    places = jnp.stack([chunk_low, chunk_high, 1 - chunk_low, 2 + inner]) * chunk
    counts = jnp.clip(length - places, 0, chunk)
    outer = 1 - inner
    low_row, high_row = core * chunk, (1 - core) * chunk
    low_partner, high_partner = low_row + 2 * chunk, high_row + 2 * chunk
    scalars = jnp.stack(
        [
            low_row,
            high_row,
            low_partner,
            jnp.where(outer == 1, high_row, low_row),
            jnp.where(outer == 1, high_partner, low_partner),
            counts[0],
            counts[1],
            counts[2],
            jnp.where(outer == 1, counts[3], counts[2]),
        ]
    ).astype(jnp.int32)

    def turn(value):
        a, b, c, d = jnp.split(value, 4, axis=-1)
        a, b, c, d = jnp.where(odd_x, b, a), jnp.where(odd_x, a, b), jnp.where(odd_x, d, c), jnp.where(odd_x, c, d)
        return jnp.concatenate([jnp.where(odd_y, c, a), jnp.where(odd_y, d, b), jnp.where(odd_y, a, c), jnp.where(odd_y, b, d)], axis=-1)

    def sort_cores(own, other, axis):
        return jnp.where(first, jnp.concatenate([own, other], axis=axis), jnp.concatenate([other, own], axis=axis))

    def pick(pair):
        return jnp.where(first, pair[0], pair[1]), jnp.where(first, pair[1], pair[0])

    def join_rows(partial):
        return partial[:chunk] + core_swap(partial[chunk:].astype(BF)).astype(F32)

    def core_piece(stacked):
        keep, give = pick(jnp.split(stacked, 2, axis=2))
        return sort_cores(keep, core_swap(give), 1)

    def matmul(a, b):
        return jnp.einsum("ab,bc->ac", a, b, preferred_element_type=F32)

    def matmul_nt(a, b):
        return jnp.einsum("ab,cb->ac", a, b, preferred_element_type=F32)

    def matmul_tn(a, b):
        return jnp.einsum("ba,bc->ac", a, b, preferred_element_type=F32)

    order = Order()
    event = order.event

    attention_piece = core_piece(jnp.concatenate([jnp.swapaxes(w_qkv, 0, 1), w_out_t[None]], axis=0))
    attention_piece = jnp.concatenate([attention_piece[n] for n in range(4)], axis=1)
    feed_piece = core_piece(jnp.concatenate([jnp.swapaxes(w_gate_up, 0, 1), w_down_t[None]], axis=0))
    feed_p, feed_x, feed_y, feed_d = [None] * 4, [None] * 4, [None] * 4, [None] * 4
    (gains_pair,) = event(sort_cores(gains, core_swap(gains), 0))
    gains_x, gains_y, gains_d = x_swap(gains_pair), y_swap(gains_pair), square_swap(gains_pair)
    inputs_rel = turn(inputs)
    gains_x, gains_y, gains_d, attention_piece, feed_p[0] = event(gains_x, gains_y, gains_d, attention_piece, feed_piece)
    gains_all = jnp.concatenate([gains_pair, gains_x, gains_y, gains_d], axis=0)

    inputs_rel, attention_piece = event(inputs_rel, attention_piece)
    own_rows, partner_rows = home_swap(inputs_rel), shift(inputs_rel, partner_of_home)
    att_1, att_2, att_3 = z_swap(attention_piece, 1), z_swap(attention_piece, 2), z_swap(attention_piece, 3)
    att_1, att_2, att_3, feed_piece = event(att_1, att_2, att_3, feed_p[0])
    att_low, att_high = jnp.stack([attention_piece, att_1]), jnp.stack([att_2, att_3])
    att_low_x, att_high_y = x_swap(att_low), y_swap(att_high)
    att_low_y, att_high_x = y_swap(att_low), x_swap(att_high)
    att_low_x, att_high_y = event(att_low_x, att_high_y)
    att_low_d, att_high_d = y_swap(att_low_x), x_swap(att_high_y)
    (own_rows,) = event(own_rows)
    other_rows = core_swap(own_rows)
    partner_rows, feed_piece = event(partner_rows, feed_piece)
    other_partner = core_swap(partner_rows)
    feed_x[0], feed_y[0] = x_swap(feed_piece), y_swap(feed_piece)
    feed_p[1] = z_swap(feed_piece, 1)
    att_low_y, att_high_x, att_low_d, att_high_d = event(att_low_y, att_high_x, att_low_d, att_high_d)
    other_rows, other_partner, feed_piece = event(other_rows, other_partner, feed_piece)
    feed_p[2] = z_swap(feed_piece, 2)
    rows = own_rows.astype(F32)
    gain_one = gains_all[:, 0].astype(F32)
    gain_two = gains_all[:, 1].astype(F32)

    normed_all, queries, keys_all, values_all, w_queries, w_keys, w_values, w_out = project(
        (own_rows, other_rows, partner_rows, other_partner), gain_one[None], [att_low, att_low_x, att_low_y, att_low_d, att_high, att_high_x, att_high_y, att_high_d]
    )
    normed_own = normed_all[: 2 * chunk]
    outer_only = (1 - inner)[None].astype(jnp.int32)
    parts = [None] * 4

    def attend(n):
        return attend_forward(outer_only, scalars, queries, keys_all, values_all, n, 1)

    queries, feed_x[0], feed_y[0] = event(queries, feed_x[0], feed_y[0])
    feed_d[0] = y_swap(feed_x[0])
    parts[0] = attend(0)
    queries, feed_p[1], _ = event(queries, feed_p[1], parts[0][0])
    feed_x[1], feed_y[1] = x_swap(feed_p[1]), y_swap(feed_p[1])
    parts[1] = attend(1)
    queries, feed_d[0], feed_p[2], _ = event(queries, feed_d[0], feed_p[2], parts[1][0])
    feed_y[2] = y_swap(feed_p[2])
    feed_p[3] = z_swap(feed_p[2], 1)
    parts[2] = attend(2)
    queries, feed_x[1], feed_y[1], _ = event(queries, feed_x[1], feed_y[1], parts[2][0])
    batch_x = x_swap(jnp.stack([feed_y[1], feed_p[2]]))
    parts[3] = attend(3)
    mixed = jnp.concatenate([p[0] for p in parts], axis=1)
    branch = matmul_nt(mixed, w_out)
    branch_own, branch_other, feed_p[3], feed_y[2], teacher = event(
        branch[:chunk], branch[chunk:].astype(BF), feed_p[3], feed_y[2], teacher
    )
    feed_y[3] = y_swap(feed_p[3])
    branch_other, batch_x, feed_y[3] = event(core_swap(branch_other), batch_x, feed_y[3])
    batch_x3, x_2 = event(jnp.stack([feed_p[3], feed_y[3]]), batch_x[1])
    batch_x3 = x_swap(batch_x3)
    feed_d[2] = y_swap(x_2)
    teacher_rel = turn(teacher)
    middle = rows + branch_own + branch_other.astype(F32)

    scaled_two, inverse_two = norm_forward(middle)
    normed_two = (scaled_two * gain_two).astype(BF)
    normed_two_all = jnp.concatenate([normed_two, core_swap_halves(normed_two)], axis=0)
    silus, slopes, hiddens, feed = [None] * 4, [None] * 4, [None] * 4, None
    pieces = [
        [alone(feed_p[0]), alone(feed_x[0]), alone(feed_y[0]), alone(feed_d[0])],
        [alone(feed_p[1]), alone(feed_x[1]), alone(feed_y[1]), (batch_x, 0)],
    ]
    for k in range(4):
        if k == 2:
            feed, feed_d[2], teacher_rel = event(feed, feed_d[2], teacher_rel)
            teacher_rows = moved_home(teacher_rel)
            pieces.append([alone(feed_p[2]), (batch_x, 1), alone(feed_y[2]), alone(feed_d[2])])
        if k == 3:
            feed, batch_x3 = event(feed, batch_x3)
            pieces.append([alone(feed_p[3]), (batch_x3, 0), alone(feed_y[3]), (batch_x3, 1)])
        silus[k], slopes[k], hiddens[k], feed = feed_forward(normed_two_all, pieces[k], feed)
    feed_own, feed_other, teacher_rows = event(feed[:chunk], feed[chunk:].astype(BF), teacher_rows)
    final = middle + feed_own + core_swap(feed_other).astype(F32)

    own_place = jnp.where(first, chunk_low, chunk_high) * chunk
    valid = (own_place + jnp.arange(chunk, dtype=jnp.int32) < length)[:, None]
    teacher_rows = jnp.where(moves, teacher_rows, teacher_rel)
    grad_final = jnp.where(valid, final - teacher_rows.astype(F32), 0.0) * (total_rows / count)
    grad_feed = grad_final.astype(BF)
    grad_feed_all, output = event(jnp.concatenate([grad_feed, core_swap(grad_feed)], axis=0), turn(final.astype(BF)))
    output_rel = output
    output = moved_home(output)

    def add(a, b):
        return (a.astype(F32) + b.astype(F32)).astype(BF)

    def total_of(own, x, y):
        return own.astype(F32) + x.astype(F32) + y.astype(F32)

    def feed_back(k, total):
        pair = slice(k, k + 2)
        return feed_backward(normed_two_all, grad_feed_all, silus[pair], slopes[pair], hiddens[pair], pieces[pair], total, k == 0)

    (grad_x,), ((own_2, x_2, y_2, d_2), (own_3, x_3, y_3, d_3)) = feed_back(2, None)
    grad_x, d_2, d_3 = event(grad_x, d_2, d_3)
    d_2, d_3 = y_swap(d_2), x_swap(d_3)
    (grad_x, grad_x_other), ((own_0, x_0, y_0, d_0), (own_1, x_1, y_1, d_1)) = feed_back(0, grad_x)
    grad_x, grad_x_other, output, d_2, d_3, d_0, d_1, y_2, x_3 = event(grad_x, grad_x_other, output, d_2, d_3, d_0, d_1, y_2, x_3)
    grad_x_other, batch_x, batch_y = event(grad_x_other, jnp.stack([add(x_2, d_2), x_3]), jnp.stack([y_2, add(y_3, d_3)]))
    batch_x, batch_y = x_swap(batch_x), y_swap(batch_y)
    tile = chunk // 2
    first_rows, second_rows = core_swap(grad_x_other[:tile]), core_swap(grad_x_other[tile:])
    grad_middle, grad_branch, grad_gain_two = norm_grads(grad_x, first_rows, second_rows, middle, grad_final, gain_two)
    grad_gain_two = grad_gain_two[0]
    grad_branch_both = jnp.concatenate([grad_branch, core_swap_halves(grad_branch)], axis=0)
    grad_mixed = matmul(grad_branch_both, w_out).astype(BF)
    half_width = mixed.shape[1] // 2

    def attend_back(n):
        lse = jnp.concatenate([parts[2 * n][1], parts[2 * n + 1][1]], axis=0)
        return attend_backward(scalars, queries, keys_all, values_all, mixed[:, n * half_width : (n + 1) * half_width], grad_mixed, lse, 2 * n)

    gq_a, gk_a, gv_a = attend_back(0)
    gq_a, grad_mixed, d_0, d_1 = event(gq_a, grad_mixed, d_0, d_1)
    d_0, d_1 = y_swap(d_0), x_swap(d_1)
    gq_b, gk_b, gv_b = attend_back(1)

    gq_b, batch_x, batch_y, d_0, d_1, x_1, y_0 = event(gq_b, batch_x, batch_y, d_0, d_1, x_1, y_0)
    grad_queries, batch_x, batch_y, part_3, part_2, gk_b, gv_b = event(
        jnp.concatenate([gq_a, gq_b], axis=1),
        jnp.stack([add(x_0, d_0), x_1]),
        jnp.stack([y_0, add(y_1, d_1)]),
        total_of(own_3, batch_x[1], batch_y[1]).astype(BF),
        total_of(own_2, batch_x[0], batch_y[0]).astype(BF),
        gk_b,
        gv_b,
    )
    batch_x, batch_y, part_3 = x_swap(batch_x), y_swap(batch_y), z_swap(part_3, 1)
    grad_keys = jnp.concatenate([gk_a, gk_b], axis=1)
    grad_values = jnp.concatenate([gv_a, gv_b], axis=1)
    part_own, part_other, partner_part, other_partner_part = rows_grads(grad_queries, grad_keys, grad_values, w_queries, w_keys, w_values)
    part_other, other_partner_part, grad_queries = event(core_swap(part_other), core_swap(other_partner_part), grad_queries)
    (from_partner,) = event((partner_part + other_partner_part.astype(F32)).astype(BF))
    from_partner = z_swap(from_partner, 1)
    (own_e, x_e, y_e, d_e), (own_o, x_o, y_o, d_o) = attention_grads(normed_all, grad_branch_both, grad_queries, grad_keys, grad_values, mixed)
    quarter_cols = grad_queries.shape[1] // 4
    half_cols = 4 * quarter_cols
    d_e, d_o, x_e, y_e, x_o, y_o, part_3, part_2, batch_x, batch_y = event(d_e, d_o, x_e, y_e, x_o, y_o, part_3, part_2, batch_x, batch_y)
    d_e, d_o = y_swap(d_e), x_swap(d_o)
    part_2, part_1 = event(add(part_2, part_3), total_of(own_1, batch_x[1], batch_y[1]).astype(BF))
    part_2, part_1 = z_swap(part_2, 2), z_swap(part_1, 1)
    part_0 = total_of(own_0, batch_x[0], batch_y[0])
    (from_partner,) = event(from_partner)
    grad_normed_one = part_own + part_other.astype(F32) + from_partner.astype(F32)
    scaled_one, inverse_one = norm_forward(rows)
    grad_norm_one, grad_gain_one = norm_backward(grad_normed_one, scaled_one, inverse_one, gain_one)
    grad_rows, gain_a, gain_b = event(turn((grad_middle + grad_norm_one).astype(BF)), grad_gain_one, grad_gain_two)
    grad_inputs = moved_home(grad_rows)
    d_e, d_o = event(d_e, d_o)
    batch_x, batch_y = event(jnp.stack([add(x_e, d_e), x_o]), jnp.stack([y_e, add(y_o, d_o)]))
    batch_x, batch_y = x_swap(batch_x), y_swap(batch_y)
    part_1, part_2, part_0 = event(part_1, part_2, part_0)
    feed_total = part_0 + part_1.astype(F32) + part_2.astype(F32)
    feed_keep, feed_give = pick(jnp.split(feed_total, 2, axis=1))
    feed_give = core_swap(feed_give.astype(BF))

    quarter = model // 4
    a, b, c, d = jnp.split(jnp.stack([gain_a, gain_b], axis=0), 4, axis=1)
    sent = x_swap(jnp.concatenate([b, d], axis=1))

    batch_x, batch_y, sent = event(batch_x, batch_y, sent)
    even, odd = total_of(own_e, batch_x[0], batch_y[0]), total_of(own_o, batch_x[1], batch_y[1])
    att_3, att_1, att_2 = odd[:, half_cols:].astype(BF), even[:, half_cols:].astype(BF), odd[:, :half_cols].astype(BF)
    att_3, att_1, a, c, sent = event(att_3, att_1, a, c, sent)
    att_3, att_1 = z_swap(att_3, 1), z_swap(att_1, 1)
    a, c = a + sent[:, :quarter], c + sent[:, quarter:]
    sent = y_swap(c)
    att_3, att_2, sent = event(att_3, att_2, sent)
    att_2 = z_swap(add(att_2, att_3), 2)
    a = a + sent
    keep, give = pick(jnp.split(a, 2, axis=1))
    sent = core_swap(give)
    feed_give, sent = event(feed_give, sent)
    a = keep + sent
    size = a.shape[1] // 4
    total = lax.dynamic_slice_in_dim(a, z * size, size, 1)
    for k in range(1, 4):
        total = total + z_swap(lax.dynamic_slice_in_dim(a, (z ^ k) * size, size, 1), k)
    grad_gains = jnp.swapaxes(total, 0, 1)
    grad_inputs = jnp.where(moves, grad_inputs, grad_rows).astype(F32)
    output = jnp.where(moves, output, output_rel)
    feed_out = sort_cores(feed_keep, feed_give.astype(F32), 2)
    attention_total = even[:, :half_cols] + att_1.astype(F32) + att_2.astype(F32)
    attention_total = jnp.stack([attention_total[:, n * quarter_cols : (n + 1) * quarter_cols] for n in range(4)])

    def to_home(total):
        keep, give = pick(jnp.split(total, 2, axis=1))
        return sort_cores(keep, core_swap(give.astype(BF)).astype(F32), 2)

    attention_out = to_home(attention_total)

    return (
        output,
        grad_inputs,
        jnp.swapaxes(attention_out[:3], 0, 1),
        attention_out[3],
        jnp.swapaxes(feed_out[:2], 0, 1),
        feed_out[2],
        grad_gains,
    )


def solution(mesh):
    square = dict(mesh.shape) == {"dp": 8, "tensor": 4}
    return jax.shard_map(
        on_square if square else on_device,
        mesh=mesh,
        in_specs=(
            P(("dp", "tensor"), None),
            P(("dp", "tensor"), None),
            P(),
            P("dp", None, "tensor"),
            P("dp", "tensor"),
            P("dp", None, "tensor"),
            P("dp", "tensor"),
            P("dp", None),
        ),
        out_specs=(
            P(("dp", "tensor"), None),
            P(("dp", "tensor"), None),
            P("dp", None, "tensor"),
            P("dp", "tensor"),
            P("dp", None, "tensor"),
            P("dp", "tensor"),
            P(("dp", "tensor"), None),
        ),
        check_vma=False,
    )
```

```python
import math

import jax
import jax.numpy as jnp
from jax import lax
from jax.experimental import pallas as pl
from jax.experimental.pallas import tpu as pltpu
from jax.sharding import PartitionSpec as P

HEAD = 64


negative = -1e30


def norm_forward(values):
    inverse = lax.rsqrt(jnp.mean(values * values, axis=-1, keepdims=True) + 1e-05)
    return (values * inverse, inverse)


def norm_backward(grad_normed, scaled, inverse, gain):
    grad_scaled = grad_normed * gain
    grad_values = inverse * (
        grad_scaled - scaled * jnp.mean(grad_scaled * scaled, axis=-1, keepdims=True)
    )
    return (grad_values, jnp.sum(grad_normed * scaled, axis=0))


def key_limit(query_index):
    return query_index + 1


def score_block(query_block, keys_all, query_start, key_start, length):
    block = query_block.shape[0]
    key_block = lax.dynamic_slice_in_dim(keys_all, key_start, block, 0)
    scores = jnp.einsum("qhe,khe->hqk", query_block, key_block, preferred_element_type=jnp.float32)
    query_pos = query_start + jnp.arange(block, dtype=jnp.int32)
    key_pos = key_start + jnp.arange(block, dtype=jnp.int32)
    allowed = (key_pos[None, :] <= query_pos[:, None]) & (key_pos[None, :] < length)
    return jnp.where(allowed[None], scores, negative)


def attention_forward(queries, keys_all, values_all, length):
    slot, heads, head = queries.shape
    block = min(512, slot)
    block_count = slot // block

    def query_step(index, carry):
        mixed, maxima, totals = carry
        query_start = index * block
        query_block = lax.dynamic_slice_in_dim(queries, query_start, block, 0)
        upper = key_limit(index)

        def stats_step(inner, state):
            maximum, total = state
            scores = score_block(query_block, keys_all, query_start, inner * block, length)
            larger = jnp.maximum(maximum, jnp.max(scores, axis=-1))
            total = total * jnp.exp(maximum - larger) + jnp.sum(
                jnp.exp(scores - larger[..., None]), axis=-1
            )
            return (larger, total)

        start_state = (
            jnp.full((heads, block), negative, jnp.float32),
            jnp.zeros((heads, block), jnp.float32),
        )
        maximum, total = lax.fori_loop(0, upper, stats_step, start_state)

        def mix_step(inner, accum):
            key_start = inner * block
            scores = score_block(query_block, keys_all, query_start, key_start, length)
            weights = (jnp.exp(scores - maximum[..., None]) / total[..., None]).astype(jnp.bfloat16)
            value_block = lax.dynamic_slice_in_dim(values_all, key_start, block, 0)
            return accum + jnp.einsum(
                "hqk,khe->qhe", weights, value_block, preferred_element_type=jnp.float32
            )

        accum = lax.fori_loop(0, upper, mix_step, jnp.zeros((block, heads, head), jnp.float32))
        mixed = lax.dynamic_update_slice_in_dim(mixed, accum, query_start, 0)
        maxima = lax.dynamic_update_index_in_dim(maxima, maximum, index, 0)
        totals = lax.dynamic_update_index_in_dim(totals, total, index, 0)
        return (mixed, maxima, totals)

    start = (
        jnp.zeros((slot, heads, head), jnp.float32),
        jnp.zeros((block_count, heads, block), jnp.float32),
        jnp.zeros((block_count, heads, block), jnp.float32),
    )
    return lax.fori_loop(0, block_count, query_step, start)


def attention_backward(queries, keys_all, values_all, grad_mixed, maxima, totals, length):
    slot, heads, head = queries.shape
    block = min(512, slot)
    block_count = slot // block

    def query_step(index, carry):
        grad_queries, grad_keys, grad_values = carry
        query_start = index * block
        query_block = lax.dynamic_slice_in_dim(queries, query_start, block, 0)
        grad_block = lax.dynamic_slice_in_dim(grad_mixed, query_start, block, 0)
        maximum = lax.dynamic_index_in_dim(maxima, index, 0, keepdims=False)
        total = lax.dynamic_index_in_dim(totals, index, 0, keepdims=False)
        upper = key_limit(index)

        def probs_of(inner):
            key_start = inner * block
            scores = score_block(query_block, keys_all, query_start, key_start, length)
            probs = jnp.exp(scores - maximum[..., None]) / total[..., None]
            value_block = lax.dynamic_slice_in_dim(values_all, key_start, block, 0)
            grad_probs = jnp.einsum(
                "qhe,khe->hqk", grad_block, value_block, preferred_element_type=jnp.float32
            )
            return (probs, grad_probs, key_start)

        def delta_step(inner, delta):
            probs, grad_probs, key_start = probs_of(inner)
            return delta + jnp.sum(probs * grad_probs, axis=-1)

        delta = lax.fori_loop(0, upper, delta_step, jnp.zeros((heads, block), jnp.float32))

        def grad_step(inner, state):
            grad_query, grad_keys, grad_values = state
            probs, grad_probs, key_start = probs_of(inner)
            grad_scores = (probs * (grad_probs - delta[..., None])).astype(jnp.bfloat16)
            key_block = lax.dynamic_slice_in_dim(keys_all, key_start, block, 0)
            grad_query = grad_query + jnp.einsum(
                "hqk,khe->qhe", grad_scores, key_block, preferred_element_type=jnp.float32
            )
            key_part = jnp.einsum(
                "hqk,qhe->khe", grad_scores, query_block, preferred_element_type=jnp.float32
            )
            value_part = jnp.einsum(
                "hqk,qhe->khe",
                probs.astype(jnp.bfloat16),
                grad_block,
                preferred_element_type=jnp.float32,
            )
            old_keys = lax.dynamic_slice_in_dim(grad_keys, key_start, block, 0)
            old_values = lax.dynamic_slice_in_dim(grad_values, key_start, block, 0)
            grad_keys = lax.dynamic_update_slice_in_dim(
                grad_keys, old_keys + key_part, key_start, 0
            )
            grad_values = lax.dynamic_update_slice_in_dim(
                grad_values, old_values + value_part, key_start, 0
            )
            return (grad_query, grad_keys, grad_values)

        start_state = (jnp.zeros((block, heads, head), jnp.float32), grad_keys, grad_values)
        grad_query, grad_keys, grad_values = lax.fori_loop(0, upper, grad_step, start_state)
        grad_queries = lax.dynamic_update_slice_in_dim(grad_queries, grad_query, query_start, 0)
        return (grad_queries, grad_keys, grad_values)

    empty = jnp.zeros((slot, heads, head), jnp.float32)
    return lax.fori_loop(0, block_count, query_step, (empty, empty, empty))


def on_device(inputs, teacher, lengths, w_qkv, w_out_t, w_gate_up, w_down_t, gains):
    own_rows = inputs.shape[0]
    slot = own_rows * lax.axis_size("tensor")
    total_rows = slot * lax.axis_size("dp")
    local_width = w_qkv.shape[2]
    local_heads = local_width // HEAD
    scale = 1.0 / math.sqrt(HEAD)
    length = lax.dynamic_index_in_dim(lengths, lax.axis_index("dp"), 0, keepdims=False)
    count = jnp.sum(lengths).astype(jnp.float32)
    own_start = lax.axis_index("tensor") * own_rows
    row_pos = own_start + jnp.arange(own_rows, dtype=jnp.int32)
    valid = (row_pos < length)[:, None]
    qkv_all, out_all, gains_all = (
        lax.all_gather(w_qkv, "dp", axis=0, tiled=True),
        lax.all_gather(w_out_t, "dp", axis=0, tiled=True),
        lax.all_gather(gains, "dp", axis=0, tiled=True),
    )
    gate_up_all, down_all = (
        lax.all_gather(w_gate_up, "dp", axis=0, tiled=True),
        lax.all_gather(w_down_t, "dp", axis=0, tiled=True),
    )
    gain_one = gains_all[:, 0].astype(jnp.float32)
    gain_two = gains_all[:, 1].astype(jnp.float32)
    rows = inputs.astype(jnp.float32)
    scaled_one, inverse_one = norm_forward(rows)
    normed_one = (scaled_one * gain_one).astype(jnp.bfloat16)
    gathered_one = lax.all_gather(normed_one, "tensor", axis=0, tiled=True)
    qkv = jnp.einsum("rd,dcf->rcf", gathered_one, qkv_all, preferred_element_type=jnp.float32)
    queries = (qkv[:, 0] * scale).astype(jnp.bfloat16).reshape(slot, local_heads, HEAD)
    keys_all = qkv[:, 1].astype(jnp.bfloat16).reshape(slot, local_heads, HEAD)
    values_all = qkv[:, 2].astype(jnp.bfloat16).reshape(slot, local_heads, HEAD)
    mixed, maxima, totals = attention_forward(queries, keys_all, values_all, length)
    mixed = mixed.reshape(slot, local_width).astype(jnp.bfloat16)
    piece = mixed
    middle = rows + lax.psum_scatter(
        jnp.einsum("rk,dk->rd", piece, out_all, preferred_element_type=jnp.float32).astype(
            jnp.bfloat16
        ),
        "tensor",
        scatter_dimension=0,
        tiled=True,
    ).astype(jnp.float32)
    scaled_two, inverse_two = norm_forward(middle)
    normed_two = (scaled_two * gain_two).astype(jnp.bfloat16)
    gathered_two = lax.all_gather(normed_two, "tensor", axis=0, tiled=True)
    rows_two = None
    gate_up = jnp.einsum(
        "rd,dcf->rcf", gathered_two, gate_up_all, preferred_element_type=jnp.float32
    )
    gate = gate_up[:, 0]
    upper = gate_up[:, 1]
    sigmoid = jax.nn.sigmoid(gate)
    hidden = (gate * sigmoid * upper).astype(jnp.bfloat16)
    piece = hidden
    final = middle + lax.psum_scatter(
        jnp.einsum("rf,df->rd", piece, down_all, preferred_element_type=jnp.float32).astype(
            jnp.bfloat16
        ),
        "tensor",
        scatter_dimension=0,
        tiled=True,
    ).astype(jnp.float32)
    output = final.astype(jnp.bfloat16)
    grad_final = jnp.where(valid, final - teacher.astype(jnp.float32), 0.0) * (total_rows / count)
    grad_feed = lax.all_gather(grad_final.astype(jnp.bfloat16), "tensor", axis=0, tiled=True)
    grad_down = jnp.einsum("rd,rf->df", grad_feed, hidden, preferred_element_type=jnp.float32)
    grad_hidden = jnp.einsum("rd,df->rf", grad_feed, down_all, preferred_element_type=jnp.float32)
    grad_gate = grad_hidden * upper * (sigmoid * (1.0 + gate * (1.0 - sigmoid)))
    grad_upper = grad_hidden * (gate * sigmoid)
    grad_gu = jnp.stack([grad_gate, grad_upper], axis=1).astype(jnp.bfloat16)
    rows_two = lax.all_gather(normed_two, "tensor", axis=0, tiled=True)
    grad_gate_up = jnp.einsum("rd,rcf->dcf", rows_two, grad_gu, preferred_element_type=jnp.float32)
    piece = grad_gu
    grad_normed_two = lax.psum_scatter(
        jnp.einsum("rcf,dcf->rd", piece, gate_up_all, preferred_element_type=jnp.float32).astype(
            jnp.bfloat16
        ),
        "tensor",
        scatter_dimension=0,
        tiled=True,
    ).astype(jnp.float32)
    grad_norm_two, grad_gain_two = norm_backward(grad_normed_two, scaled_two, inverse_two, gain_two)
    grad_middle = grad_final + grad_norm_two
    grad_branch = lax.all_gather(grad_middle.astype(jnp.bfloat16), "tensor", axis=0, tiled=True)
    grad_out = jnp.einsum("rd,rk->dk", grad_branch, mixed, preferred_element_type=jnp.float32)
    grad_mixed = jnp.einsum("rd,dk->rk", grad_branch, out_all, preferred_element_type=jnp.float32)
    grad_mixed = grad_mixed.astype(jnp.bfloat16).reshape(slot, local_heads, HEAD)
    grad_queries, grad_keys, grad_values = attention_backward(
        queries, keys_all, values_all, grad_mixed, maxima, totals, length
    )
    grad_rows_qkv = jnp.stack(
        [
            grad_queries.reshape(slot, local_width).astype(jnp.bfloat16) * scale,
            grad_keys.reshape(slot, local_width).astype(jnp.bfloat16),
            grad_values.reshape(slot, local_width).astype(jnp.bfloat16),
        ],
        axis=1,
    )
    rows_one = lax.all_gather(normed_one, "tensor", axis=0, tiled=True)
    grad_qkv = jnp.einsum(
        "rd,rcf->dcf", rows_one, grad_rows_qkv, preferred_element_type=jnp.float32
    )
    piece = grad_rows_qkv
    grad_normed_one = lax.psum_scatter(
        jnp.einsum("rcf,dcf->rd", piece, qkv_all, preferred_element_type=jnp.float32).astype(
            jnp.bfloat16
        ),
        "tensor",
        scatter_dimension=0,
        tiled=True,
    ).astype(jnp.float32)
    grad_norm_one, grad_gain_one = norm_backward(grad_normed_one, scaled_one, inverse_one, gain_one)
    grad_inputs = grad_middle + grad_norm_one
    grad_qkv, grad_out, grad_gate_up, grad_down = (
        lax.psum_scatter(
            grad_qkv.astype(jnp.bfloat16), "dp", scatter_dimension=0, tiled=True
        ).astype(jnp.float32),
        lax.psum_scatter(
            grad_out.astype(jnp.bfloat16), "dp", scatter_dimension=0, tiled=True
        ).astype(jnp.float32),
        lax.psum_scatter(
            grad_gate_up.astype(jnp.bfloat16), "dp", scatter_dimension=0, tiled=True
        ).astype(jnp.float32),
        lax.psum_scatter(
            grad_down.astype(jnp.bfloat16), "dp", scatter_dimension=0, tiled=True
        ).astype(jnp.float32),
    )
    grad_gains = lax.psum_scatter(
        jnp.stack([grad_gain_one, grad_gain_two], axis=1),
        ("dp", "tensor"),
        scatter_dimension=0,
        tiled=True,
    )
    return (output, grad_inputs, grad_qkv, grad_out, grad_gate_up, grad_down, grad_gains)


BF = jnp.bfloat16
F32 = jnp.float32
AXES = ("dp", "tensor")
LIGHT = pl.CostEstimate(flops=1000, bytes_accessed=1000, transcendentals=0)


def shift(value, where):
    pairs = []
    for y in range(2):
        for x in range(2):
            for c in range(2):
                for z in range(4):
                    to = where(y, x, c, z)
                    if to is not None:
                        ty, tx, tc, tz = to
                        pairs.append((((y * 2 + x) * 2 + c) * 4 + z, ((ty * 2 + tx) * 2 + tc) * 4 + tz))
    return lax.ppermute(value, AXES, pairs)


def core_swap(value):
    return shift(value, lambda y, x, c, z: (y, x, 1 - c, z))


def core_swap_halves(value):
    half = value.shape[0] // 2
    return jnp.concatenate([core_swap(value[:half]), core_swap(value[half:])], axis=0)


def x_swap(value):
    return shift(value, lambda y, x, c, z: (y, 1 - x, c, z))


def y_swap(value):
    return shift(value, lambda y, x, c, z: (1 - y, x, c, z))


def square_swap(value):
    return shift(value, lambda y, x, c, z: (1 - y, 1 - x, c, z))


def z_swap(value, bits):
    return shift(value, lambda y, x, c, z: (y, x, c, z ^ bits))


def home_of(y, x, c, z):
    if (c == 1 and z < 2) or (c == 0 and z >= 2):
        return (y, x, 1 - c, 3 - z)
    return (y, x, c, z)


def home_swap(value):
    return shift(value, home_of)


def moved_home(value):
    return shift(value, lambda *place: None if home_of(*place) == place else home_of(*place))


def partner_of_home(y, x, c, z):
    y, x, c, z = home_of(y, x, c, z)
    z ^= 1
    if c == 1 and z in (1, 2):
        return None
    return (y, x, c, z)


def head_masks(rows):
    lanes = lax.broadcasted_iota(jnp.int32, (rows, 2 * HEAD), 1)
    return (lanes < HEAD, lanes >= HEAD)


def dot_nt(a, b):
    return lax.dot_general(a, b, (((1,), (1,)), ((), ())), preferred_element_type=F32)


def dot_nn(a, b):
    return lax.dot_general(a, b, (((1,), (0,)), ((), ())), preferred_element_type=F32)


def dot_tn(a, b):
    return lax.dot_general(a, b, (((0,), (0,)), ((), ())), preferred_element_type=F32)


def attend_forward_kernel(outer_ref, sc_ref, q_ref, k_ref, v_ref, o_ref, lse_ref):
    chunk = q_ref.shape[0] // 2
    tile = chunk // 2
    lanes = 2 * HEAD
    head = pl.program_id(0) % 2
    low, high, low_partner, extra_row, extra_key = [pl.multiple_of(sc_ref[i], chunk) for i in range(5)]
    mine = lax.broadcasted_iota(jnp.int32, (tile, lanes), 1) // HEAD == head

    def fold(op, parts):
        parts = [p[:, i * lanes : (i + 1) * lanes] for p in parts for i in range(p.shape[1] // lanes)]
        while len(parts) > 1:
            parts = [op(parts[i], parts[i + 1]) if i + 1 < len(parts) else parts[i] for i in range(0, len(parts), 2)]
        return parts[0]

    def unit(row, own, own_count, half, others):
        rows = pl.ds(pl.multiple_of(row + half * tile, tile), tile)
        query = jnp.where(mine, q_ref[rows, :], 0)
        blocks = [(pl.ds(start, chunk), count, chunk, None) for start, count in others]
        blocks.append((pl.ds(own, (half + 1) * tile), own_count, (half + 1) * tile, half * tile))
        scores = []
        for keys, count, width, diagonal in blocks:
            s = dot_nt(query, k_ref[keys, :])
            s = s + jnp.where(lax.broadcasted_iota(jnp.int32, (1, width), 1) < count, 0.0, negative)
            if diagonal is not None:
                cols = lax.broadcasted_iota(jnp.int32, (tile, width), 1)
                s = jnp.where(cols <= lax.broadcasted_iota(jnp.int32, (tile, width), 0) + diagonal, s, negative)
            scores.append(s)
        top = jnp.max(fold(jnp.maximum, scores), axis=1, keepdims=True)
        weights = [jnp.exp(s - top) for s in scores]
        total = jnp.sum(fold(jnp.add, weights), axis=1, keepdims=True)
        mixed = None
        for w, (keys, _, _, _) in zip(weights, blocks):
            part = dot_nn(w.astype(BF), v_ref[keys, :])
            mixed = part if mixed is None else mixed + part
        return rows, mixed / total, top + jnp.log(total)

    def finish(units):
        for rows, mixed, lse in units:
            mixed = mixed.astype(BF)
            o_ref[rows, :] = jnp.where(mine, mixed, o_ref[rows, :])
            lse_ref[0, pl.ds(head, 1), rows] = jnp.transpose(jnp.broadcast_to(lse, (tile, lanes)))[0:1]

    near = [(low, sc_ref[5]), (low_partner, sc_ref[7])]
    extra = [(extra_key, sc_ref[8])]

    @pl.when(outer_ref[0] == 1)
    def _():
        for half in range(2):
            finish([unit(high, high, sc_ref[6], half, near + extra), unit(low, low, sc_ref[5], half, [])])

    @pl.when(outer_ref[0] == 0)
    def _():
        for half in range(2):
            finish([unit(high, high, sc_ref[6], half, near), unit(low, low, sc_ref[5], half, extra)])


def attend_forward(outer, scalars, queries, keys_all, values_all, start, pairs):
    rows = queries.shape[0]
    width = pairs * 2 * HEAD
    slot = keys_all.shape[0]
    own = lambda i, *_: (0, i // 2)
    column = lambda i, *_: (0, i // 2 + start)
    return pl.pallas_call(
        attend_forward_kernel,
        out_shape=(
            jax.ShapeDtypeStruct((rows, width), BF),
            jax.ShapeDtypeStruct((pairs, 8, rows), F32),
        ),
        grid_spec=pltpu.PrefetchScalarGridSpec(
            num_scalar_prefetch=2,
            grid=(2 * pairs,),
            in_specs=[
                pl.BlockSpec((rows, 2 * HEAD), column),
                pl.BlockSpec((slot, 2 * HEAD), column),
                pl.BlockSpec((slot, 2 * HEAD), column),
            ],
            out_specs=(
                pl.BlockSpec((rows, 2 * HEAD), own),
                pl.BlockSpec((1, 8, rows), lambda i, *_: (i // 2, 0, 0)),
            ),
        ),
        compiler_params=pltpu.CompilerParams(vmem_limit_bytes=24 << 20),
        cost_estimate=LIGHT,
        name="attend_forward",
    )(outer, scalars, queries, keys_all, values_all)


def attend_backward_kernel(sc_ref, q_ref, k_ref, v_ref, o_ref, g_ref, lse_ref, dq_ref, dk_ref, dv_ref, dq_acc, dk_acc, dv_acc, delta_ref):
    chunk = q_ref.shape[0] // 2
    tile = chunk // 2
    low, high_row, low_partner, extra_row, extra_key = [pl.multiple_of(sc_ref[i], chunk) for i in range(5)]
    dq_acc[...] = jnp.zeros_like(dq_acc)
    dk_acc[...] = jnp.zeros_like(dk_acc)
    dv_acc[...] = jnp.zeros_like(dv_acc)
    for part in range(4):
        rows = pl.ds(part * tile, tile)
        product = jnp.transpose(o_ref[rows, :].astype(F32) * g_ref[rows, :].astype(F32))
        delta_ref[0:1, rows] = jnp.sum(product[:HEAD], axis=0, keepdims=True)
        delta_ref[1:2, rows] = jnp.sum(product[HEAD:], axis=0, keepdims=True)

    def step(head, row, width, key, count, shift_rows):
        rows = pl.ds(row, width)
        keys = pl.ds(key, tile)
        query = jnp.where(head_masks(width)[head], q_ref[rows, :], 0)
        grad = jnp.where(head_masks(width)[head], g_ref[rows, :], 0)
        key_block = k_ref[keys, :]
        scores = dot_nt(key_block, query)
        index = lax.broadcasted_iota(jnp.int32, (tile, width), 0)
        allowed = index < count
        if shift_rows is not None:
            allowed = allowed & (index <= lax.broadcasted_iota(jnp.int32, (tile, width), 1) + shift_rows)
        probs = jnp.exp(jnp.where(allowed, scores, negative) - lse_ref[0, head : head + 1, rows])
        grad_probs = dot_nt(v_ref[keys, :], grad)
        grad_scores = (probs * (grad_probs - delta_ref[head : head + 1, rows])).astype(BF)
        dv_acc[keys, :] += dot_nn(probs.astype(BF), grad)
        dk_acc[keys, :] += dot_nn(grad_scores, query)
        key_masked = jnp.where(head_masks(tile)[head], key_block, 0)
        dq_acc[rows, :] += dot_tn(grad_scores, key_masked)

    for head in range(2):
        for half in range(2):
            down = half * tile
            add = lambda start: pl.multiple_of(start + down, tile)
            step(head, add(low), chunk - down, add(low), sc_ref[5] - down, 0)
            step(head, add(high_row), chunk - down, add(high_row), sc_ref[6] - down, 0)
            step(head, high_row, chunk, add(low), sc_ref[5] - down, None)
            step(head, high_row, chunk, add(low_partner), sc_ref[7] - down, None)
            step(head, extra_row, chunk, add(extra_key), sc_ref[8] - down, None)
    dq_ref[...] = (dq_acc[...] * (1.0 / math.sqrt(HEAD))).astype(BF)
    dk_ref[...] = dk_acc[...].astype(BF)
    dv_ref[...] = dv_acc[...].astype(BF)


def attend_backward(scalars, queries, keys_all, values_all, mixed, grad_mixed, lse, start):
    rows, width = mixed.shape
    pairs = width // (2 * HEAD)
    slot = keys_all.shape[0]
    own = lambda i, sc: (0, i)
    column = lambda i, sc: (0, i + start)
    own_spec = pl.BlockSpec((rows, 2 * HEAD), own)
    row_spec = pl.BlockSpec((rows, 2 * HEAD), column)
    slot_spec = pl.BlockSpec((slot, 2 * HEAD), column)
    return pl.pallas_call(
        attend_backward_kernel,
        out_shape=(
            jax.ShapeDtypeStruct((rows, width), BF),
            jax.ShapeDtypeStruct((slot, width), BF),
            jax.ShapeDtypeStruct((slot, width), BF),
        ),
        grid_spec=pltpu.PrefetchScalarGridSpec(
            num_scalar_prefetch=1,
            grid=(pairs,),
            in_specs=[row_spec, slot_spec, slot_spec, own_spec, row_spec, pl.BlockSpec((1, 8, rows), lambda i, sc: (i, 0, 0))],
            out_specs=(own_spec, pl.BlockSpec((slot, 2 * HEAD), own), pl.BlockSpec((slot, 2 * HEAD), own)),
            scratch_shapes=[
                pltpu.VMEM((rows, 2 * HEAD), F32),
                pltpu.VMEM((slot, 2 * HEAD), F32),
                pltpu.VMEM((slot, 2 * HEAD), F32),
                pltpu.VMEM((8, rows), F32),
            ],
        ),
        compiler_params=pltpu.CompilerParams(vmem_limit_bytes=32 << 20),
        cost_estimate=LIGHT,
    )(scalars, queries, keys_all, values_all, mixed, grad_mixed, lse)


def project_kernel(*refs):
    rows_refs, gain_ref, weight_refs = refs[:4], refs[4], (refs[5:9], refs[9:13])
    normed_ref, q_ref, k_ref, v_ref, wq_ref, wk_ref, wv_ref, wo_ref = refs[13:]
    step = pl.program_id(0)
    _, block, width = weight_refs[0][0].shape
    part = width // 4
    tile = rows_refs[0].shape[0] // 2

    @pl.when(step == 0)
    def _():
        for k in range(4):
            for r in range(4):
                source = weight_refs[k // 2][r].at[k % 2]
                for n, out in enumerate((wq_ref, wk_ref, wv_ref, wo_ref)):
                    out[r * block : (r + 1) * block, k * part : (k + 1) * part] = source[:, n * part : (n + 1) * part]

    for n in range(4):

        @pl.when(step == n)
        def _():
            for half in range(2):
                rows = slice(half * tile, (half + 1) * tile)
                values = rows_refs[n][rows, :].astype(F32)
                inverse = lax.rsqrt(jnp.mean(values * values, axis=-1, keepdims=True) + 1e-05)
                normed = (values * inverse * gain_ref[...]).astype(BF)
                normed_ref[rows, :] = normed
                k_ref[rows, :] = dot_nn(normed, wk_ref[...]).astype(BF)
                v_ref[rows, :] = dot_nn(normed, wv_ref[...]).astype(BF)
                if n < 2:
                    q_ref[rows, :] = (dot_nn(normed, wq_ref[...]) * (1.0 / math.sqrt(HEAD))).astype(BF)


def project(rows_parts, gain, weights):
    chunk, model = rows_parts[0].shape
    _, block, width = weights[0].shape
    whole = lambda shape: pl.BlockSpec(shape, lambda i: (0,) * len(shape))
    tiles = lambda cols: pl.BlockSpec((chunk, cols), lambda i: (i, 0))
    shape = lambda r, c: jax.ShapeDtypeStruct((r, c), BF)
    return pl.pallas_call(
        project_kernel,
        out_shape=(
            shape(4 * chunk, model),
            shape(2 * chunk, width),
            shape(4 * chunk, width),
            shape(4 * chunk, width),
            shape(model, width),
            shape(model, width),
            shape(model, width),
            shape(model, width),
        ),
        grid=(4,),
        in_specs=[whole((chunk, model))] * 4 + [whole((1, model))] + [whole(w.shape) for w in weights],
        out_specs=(
            tiles(model),
            pl.BlockSpec((chunk, width), lambda i: (jnp.minimum(i, 1), 0)),
            tiles(width),
            tiles(width),
        )
        + tuple(whole((model, width)) for _ in range(4)),
        compiler_params=pltpu.CompilerParams(vmem_limit_bytes=60 << 20),
        cost_estimate=LIGHT,
        name="project",
    )(*rows_parts, gain, *weights)


def rows_grads_kernel(dq_ref, dk_ref, dv_ref, wq_ref, wk_ref, wv_ref, own_ref, other_ref, partner_ref, partner_other_ref):
    step = pl.program_id(0)
    part = dot_nt(dk_ref[...], wk_ref[...]) + dot_nt(dv_ref[...], wv_ref[...])

    @pl.when(step == 0)
    def _():
        own_ref[...] = part + dot_nt(dq_ref[...], wq_ref[...])

    @pl.when(step == 1)
    def _():
        other_ref[...] = (part + dot_nt(dq_ref[...], wq_ref[...])).astype(BF)

    @pl.when(step == 2)
    def _():
        partner_ref[...] = part

    @pl.when(step == 3)
    def _():
        partner_other_ref[...] = part.astype(BF)


def rows_grads(dq, dk, dv, wq, wk, wv):
    slot, width = dk.shape
    model = wq.shape[0]
    chunk = slot // 4
    whole = pl.BlockSpec((model, width), lambda i: (0, 0))
    tiles = pl.BlockSpec((chunk, width), lambda i: (i, 0))
    out = pl.BlockSpec((chunk, model), lambda i: (0, 0))
    shape = lambda t: jax.ShapeDtypeStruct((chunk, model), t)
    return pl.pallas_call(
        rows_grads_kernel,
        out_shape=(shape(F32), shape(BF), shape(F32), shape(BF)),
        grid=(4,),
        in_specs=[pl.BlockSpec((chunk, width), lambda i: (jnp.minimum(i, 1), 0)), tiles, tiles, whole, whole, whole],
        out_specs=(out,) * 4,
        compiler_params=pltpu.CompilerParams(vmem_limit_bytes=40 << 20),
        cost_estimate=LIGHT,
        name="rows_grads",
    )(dq, dk, dv, wq, wk, wv)


def attention_grads_kernel(x_ref, g_ref, dq_ref, dk_ref, dv_ref, mixed_ref, *out_refs):
    rows = g_ref.shape[0]
    x_turned = jnp.transpose(x_ref[...])
    g_turned = jnp.transpose(g_ref[...])
    grads = (
        dot_nn(x_turned[:, :rows], dq_ref[...]),
        dot_nn(x_turned, dk_ref[...]),
        dot_nn(x_turned, dv_ref[...]),
        dot_nn(g_turned, mixed_ref[...]),
    )
    part = dq_ref.shape[1] // 4
    for r in range(4):

        @pl.when(pl.program_id(0) == r)
        def _():
            for k in range(4):
                for n in range(4):
                    start = (k % 2 * 4 + n) * part
                    out_refs[k // 2 * 4 + r][:, start : start + part] = grads[n][:, k * part : (k + 1) * part].astype(BF)


def attention_grads(x, g, dq, dk, dv, mixed):
    rows, model = g.shape
    slot, width = dk.shape
    block = model // 4
    whole = lambda a: pl.BlockSpec(a.shape, lambda i: (0, 0))
    out = pl.pallas_call(
        attention_grads_kernel,
        out_shape=(jax.ShapeDtypeStruct((block, 2 * width), BF),) * 8,
        grid=(4,),
        in_specs=[
            pl.BlockSpec((slot, block), lambda i: (0, i)),
            pl.BlockSpec((rows, block), lambda i: (0, i)),
            whole(dq),
            whole(dk),
            whole(dv),
            whole(mixed),
        ],
        out_specs=(pl.BlockSpec((block, 2 * width), lambda i: (0, 0)),) * 8,
        compiler_params=pltpu.CompilerParams(vmem_limit_bytes=40 << 20),
        cost_estimate=LIGHT,
        name="attention_grads",
    )(x, g, dq, dk, dv, mixed)
    return out[:4], out[4:]


def norm_grads_kernel(halves, part_ref, first_ref, second_ref, values_ref, grad_ref, gain_ref, out_ref, low_ref, gain_grad_ref):
    step = pl.program_id(0)
    values = values_ref[...].astype(F32)
    inverse = lax.rsqrt(jnp.mean(values * values, axis=-1, keepdims=True) + 1e-05)
    scaled = values * inverse

    @pl.when(step == 0)
    def _():
        gain_grad_ref[...] = jnp.zeros_like(gain_grad_ref)

    first, second = first_ref[...].astype(F32), second_ref[...].astype(F32)
    received = jnp.where(step < 2, first, second) if halves else first + second
    grad_normed = part_ref[...] + received
    grad_scaled = grad_normed * gain_ref[...]
    grad = grad_ref[...] + inverse * (grad_scaled - scaled * jnp.mean(grad_scaled * scaled, axis=-1, keepdims=True))
    out_ref[...] = grad
    low_ref[...] = grad.astype(BF)
    gain_grad_ref[...] += jnp.sum(grad_normed * scaled, axis=0, keepdims=True)


def norm_grads(part, first, second, values, grad, gain):
    rows, model = part.shape
    tile = rows // 4
    halves = first.shape[0] < rows
    tiles = pl.BlockSpec((tile, model), lambda i: (i, 0))
    row = pl.BlockSpec((1, model), lambda i: (0, 0))
    return pl.pallas_call(
        lambda *refs: norm_grads_kernel(halves, *refs),
        out_shape=(
            jax.ShapeDtypeStruct((rows, model), F32),
            jax.ShapeDtypeStruct((rows, model), BF),
            jax.ShapeDtypeStruct((1, model), F32),
        ),
        grid=(4,),
        in_specs=[
            tiles,
            pl.BlockSpec((tile, model), lambda i: (jnp.minimum(i, 1), 0)) if halves else tiles,
            pl.BlockSpec((tile, model), lambda i: (jnp.maximum(i - 2, 0), 0)) if halves else tiles,
            tiles,
            tiles,
            row,
        ],
        out_specs=(tiles, tiles, row),
        compiler_params=pltpu.CompilerParams(vmem_limit_bytes=24 << 20),
        cost_estimate=LIGHT,
        name="norm_grads",
    )(part, first, second, values, grad, gain[None])


def feed_forward_kernel(first_piece, *refs):
    x_ref, weight_refs = refs[0], refs[1:5]
    block = weight_refs[0].shape[1]
    if not first_piece:
        y_in_ref = refs[5]
    silu_ref, slope_ref, hidden_ref, y_ref = refs[-4:]
    x = x_ref[...]
    gate = upper = None
    for r in range(4):
        part = x[:, r * block : (r + 1) * block]
        g = dot_nn(part, weight_refs[r][0])
        u = dot_nn(part, weight_refs[r][1])
        gate = g if gate is None else gate + g
        upper = u if upper is None else upper + u
    sigmoid = jax.nn.sigmoid(gate)
    silu = gate * sigmoid
    hidden = (silu * upper).astype(BF)
    silu_ref[...] = silu.astype(BF)
    slope_ref[...] = (upper * (sigmoid * (1.0 + gate * (1.0 - sigmoid)))).astype(BF)
    hidden_ref[...] = hidden
    for r in range(4):
        cols = slice(r * block, (r + 1) * block)
        y = dot_nt(hidden, weight_refs[r][2])
        y_ref[:, cols] = y if first_piece else y + y_in_ref[:, cols]


def alone(piece):
    return (piece[None], 0)


def feed_forward(x, pieces, y):
    rows, model = x.shape
    _, _, block, width = pieces[0][0].shape
    tile = rows // 4
    tiles = lambda cols: pl.BlockSpec((tile, cols), lambda i: (i, 0))
    weight_specs = [pl.BlockSpec((None, 3, block, width), lambda i, n=n: (n, 0, 0, 0)) for _, n in pieces]
    extra = [] if y is None else [y]
    return pl.pallas_call(
        lambda *refs: feed_forward_kernel(y is None, *refs),
        out_shape=tuple(jax.ShapeDtypeStruct((rows, width), BF) for _ in range(3)) + (jax.ShapeDtypeStruct((rows, model), F32),),
        grid=(4,),
        in_specs=[tiles(model)] + weight_specs + [tiles(model) for _ in extra],
        out_specs=(tiles(width), tiles(width), tiles(width), tiles(model)),
        input_output_aliases={5: 3} if extra else {},
        compiler_params=pltpu.CompilerParams(vmem_limit_bytes=24 << 20),
        cost_estimate=LIGHT,
        name="feed_forward",
    )(x, *[w for w, _ in pieces], *extra)


def feed_backward_kernel(places, has_sum, last, *refs):
    count = len(places) // 4
    refs = list(refs)
    take = lambda n: [refs.pop(0) for _ in range(n)]
    x_ref, g_ref = take(2)
    silu_hbm, slope_hbm, hidden_hbm, weight_hbm = take(count), take(count), take(count), take(4 * count)
    sum_ref = take(1)[0] if has_sum else None
    dx_ref, dx_other_ref = take(2) if last else take(1) * 2
    out_hbm = take(4 * count)
    xt_ref, gt_ref, kept_ref, hidden_ref, gu_ref, down_ref, acc_ref, out_ref, act_sem, weight_sem, out_sem = refs
    _, _, block, width = weight_hbm[0].shape
    rows_all = x_ref.shape[0]
    half = rows_all // 2
    copies_of, late_copies = [], []
    for p in range(count):
        copies = []
        for n, source in enumerate((slope_hbm[p], silu_hbm[p])):
            copies.append(pltpu.make_async_copy(source, kept_ref.at[p, :, pl.ds(n * width, width)], act_sem.at[p, n]))
        for r in range(4):
            features = pl.ds(r * block, block)
            source = weight_hbm[p * 4 + r].at[places[p * 4 + r]]
            for n, target in enumerate((gu_ref.at[p, features, pl.ds(0, width)], gu_ref.at[p, features, pl.ds(width, width)], down_ref.at[p, features, :])):
                copies.append(pltpu.make_async_copy(source.at[n], target, weight_sem.at[p, r, n]))
        copies_of.append(copies)
        late_copies.append(pltpu.make_async_copy(hidden_hbm[p], hidden_ref.at[p], act_sem.at[p, 2]))
    for copy in copies_of[0]:
        copy.start()
    for t in range(4):
        rows = slice(t * rows_all // 4, (t + 1) * rows_all // 4)
        xt_ref[:, rows] = jnp.transpose(x_ref[rows, :])
        gt_ref[:, rows] = jnp.transpose(g_ref[rows, :])

    for p in range(count):
        for copy in copies_of[p]:
            copy.wait()
        for copy in copies_of[p + 1] if p < count - 1 else late_copies:
            copy.start()
        for t in range(2):
            rows = slice(t * half, (t + 1) * half)
            grad_hidden = dot_nn(g_ref[rows, :], down_ref[p])
            kept_ref[p, rows, :width] = (grad_hidden * kept_ref[p, rows, :width].astype(F32)).astype(BF)
            kept_ref[p, rows, width:] = (grad_hidden * kept_ref[p, rows, width:].astype(F32)).astype(BF)
            part = dot_nt(kept_ref[p, rows, :], gu_ref[p])
            if p > 0:
                part = acc_ref[rows, :] + part
            elif has_sum:
                part = sum_ref[rows, :] + part
            if p < count - 1:
                acc_ref[rows, :] = part
            elif not last:
                dx_ref[rows, :] = part
            elif t == 0:
                dx_ref[...] = part
            else:
                dx_other_ref[...] = part.astype(BF)

    slots = out_ref.shape[0]
    copies = []
    for p in range(count):
        late_copies[p].wait()
        for r in range(3, -1, -1):
            features = slice(r * block, (r + 1) * block)
            slot = len(copies) % slots
            if len(copies) >= slots:
                copies[len(copies) - slots].wait()
            gu = dot_nn(xt_ref[features, :], kept_ref[p]).astype(BF)
            out_ref[slot, 0] = gu[:, :width]
            out_ref[slot, 1] = gu[:, width:]
            out_ref[slot, 2] = dot_nn(gt_ref[features, :], hidden_ref[p]).astype(BF)
            copies.append(pltpu.make_async_copy(out_ref.at[slot], out_hbm[p * 4 + r], out_sem.at[slot]))
            copies[-1].start()
    for copy in copies[-slots:]:
        copy.wait()


def feed_backward(x, g, silus, slopes, hiddens, pieces, total, last):
    count = len(pieces)
    extra = [] if total is None else [total]
    rows, model = x.shape
    _, _, block, width = pieces[0][0][0].shape
    places = [n for piece in pieces for _, n in piece]
    vmem = pl.BlockSpec(memory_space=pltpu.VMEM)
    hbm = pl.BlockSpec(memory_space=pl.ANY)
    outs = pl.pallas_call(
        lambda *refs: feed_backward_kernel(places, total is not None, last, *refs),
        out_shape=(
            (jax.ShapeDtypeStruct((rows // 2, model), F32), jax.ShapeDtypeStruct((rows // 2, model), BF))
            if last
            else (jax.ShapeDtypeStruct((rows, model), F32),)
        )
        + tuple(jax.ShapeDtypeStruct((3, block, width), BF) for _ in range(4 * count)),
        in_specs=[vmem] * 2 + [hbm] * (7 * count) + [vmem] * len(extra),
        out_specs=((vmem, vmem) if last else (vmem,)) + (hbm,) * (4 * count),
        scratch_shapes=[
            pltpu.VMEM((model, rows), BF),
            pltpu.VMEM((model, rows), BF),
            pltpu.VMEM((count, rows, 2 * width), BF),
            pltpu.VMEM((count, rows, width), BF),
            pltpu.VMEM((count, model, 2 * width), BF),
            pltpu.VMEM((count, model, width), BF),
            pltpu.VMEM((rows, model), F32),
            pltpu.VMEM((3, 3, block, width), BF),
            pltpu.SemaphoreType.DMA((count, 3)),
            pltpu.SemaphoreType.DMA((count, 4, 3)),
            pltpu.SemaphoreType.DMA((3,)),
        ],
        compiler_params=pltpu.CompilerParams(vmem_limit_bytes=60 << 20),
        cost_estimate=LIGHT,
        name="feed_backward",
    )(x, g, *silus, *slopes, *hiddens, *[w for piece in pieces for w, _ in piece], *extra)
    first = 2 if last else 1
    return outs[:first], [outs[first + 4 * p : first + 4 + 4 * p] for p in range(count)]


class Order:
    def __init__(self):
        self.last = ()

    def event(self, *values):
        out = lax.optimization_barrier((*values, *self.last))[: len(values)]
        self.last = out
        return out


def on_square(inputs, teacher, lengths, w_qkv, w_out_t, w_gate_up, w_down_t, gains):
    chunk, model = inputs.shape
    slot = chunk * 4
    total_rows = slot * 8
    dp = lax.axis_index("dp")
    z = lax.axis_index("tensor")
    core = dp % 2
    first = core == 0
    odd_x = (dp // 2) % 2 == 1
    odd_y = dp // 4 == 1
    inner = jnp.where((z == 1) | (z == 2), 1, 0)
    moves = (core == 1) == (z < 2)
    chunk_low, chunk_high = inner, 3 - inner
    length = lax.dynamic_index_in_dim(lengths, (dp // 2) * 2 + z // 2, 0, keepdims=False)
    count = jnp.sum(lengths).astype(F32)
    places = jnp.stack([chunk_low, chunk_high, 1 - chunk_low, 2 + inner]) * chunk
    counts = jnp.clip(length - places, 0, chunk)
    outer = 1 - inner
    low_row, high_row = core * chunk, (1 - core) * chunk
    low_partner, high_partner = low_row + 2 * chunk, high_row + 2 * chunk
    scalars = jnp.stack(
        [
            low_row,
            high_row,
            low_partner,
            jnp.where(outer == 1, high_row, low_row),
            jnp.where(outer == 1, high_partner, low_partner),
            counts[0],
            counts[1],
            counts[2],
            jnp.where(outer == 1, counts[3], counts[2]),
        ]
    ).astype(jnp.int32)

    def turn(value):
        a, b, c, d = jnp.split(value, 4, axis=-1)
        a, b, c, d = jnp.where(odd_x, b, a), jnp.where(odd_x, a, b), jnp.where(odd_x, d, c), jnp.where(odd_x, c, d)
        return jnp.concatenate([jnp.where(odd_y, c, a), jnp.where(odd_y, d, b), jnp.where(odd_y, a, c), jnp.where(odd_y, b, d)], axis=-1)

    def sort_cores(own, other, axis):
        return jnp.where(first, jnp.concatenate([own, other], axis=axis), jnp.concatenate([other, own], axis=axis))

    def pick(pair):
        return jnp.where(first, pair[0], pair[1]), jnp.where(first, pair[1], pair[0])

    def join_rows(partial):
        return partial[:chunk] + core_swap(partial[chunk:].astype(BF)).astype(F32)

    def core_piece(stacked):
        keep, give = pick(jnp.split(stacked, 2, axis=2))
        return sort_cores(keep, core_swap(give), 1)

    def matmul(a, b):
        return jnp.einsum("ab,bc->ac", a, b, preferred_element_type=F32)

    def matmul_nt(a, b):
        return jnp.einsum("ab,cb->ac", a, b, preferred_element_type=F32)

    def matmul_tn(a, b):
        return jnp.einsum("ba,bc->ac", a, b, preferred_element_type=F32)

    order = Order()
    event = order.event

    attention_piece = core_piece(jnp.concatenate([jnp.swapaxes(w_qkv, 0, 1), w_out_t[None]], axis=0))
    attention_piece = jnp.concatenate([attention_piece[n] for n in range(4)], axis=1)
    feed_piece = core_piece(jnp.concatenate([jnp.swapaxes(w_gate_up, 0, 1), w_down_t[None]], axis=0))
    feed_p, feed_x, feed_y, feed_d = [None] * 4, [None] * 4, [None] * 4, [None] * 4
    (gains_pair,) = event(sort_cores(gains, core_swap(gains), 0))
    gains_x, gains_y, gains_d = x_swap(gains_pair), y_swap(gains_pair), square_swap(gains_pair)
    inputs_rel = turn(inputs)
    gains_x, gains_y, gains_d, attention_piece, feed_p[0] = event(gains_x, gains_y, gains_d, attention_piece, feed_piece)
    gains_all = jnp.concatenate([gains_pair, gains_x, gains_y, gains_d], axis=0)

    own_rows, partner_rows = home_swap(inputs_rel), shift(inputs_rel, partner_of_home)
    att_1, att_2 = z_swap(attention_piece, 1), z_swap(attention_piece, 2)
    att_1, feed_piece = event(att_1, feed_p[0])
    att_low = jnp.stack([attention_piece, att_1])
    att_low_x, att_low_y = x_swap(att_low), y_swap(att_low)
    (att_2,) = event(att_2)
    (att_3,) = event(z_swap(att_2, 1))
    att_high = jnp.stack([att_2, att_3])
    att_high_x, att_high_y = x_swap(att_high), y_swap(att_high)
    (att_low_x,) = event(att_low_x)
    att_low_d = y_swap(att_low_x)
    (att_high_y,) = event(att_high_y)
    att_high_d = x_swap(att_high_y)
    (own_rows,) = event(own_rows)
    other_rows = core_swap(own_rows)
    partner_rows, feed_piece = event(partner_rows, feed_piece)
    other_partner = core_swap(partner_rows)
    feed_x[0], feed_y[0] = x_swap(feed_piece), y_swap(feed_piece)
    feed_p[1] = z_swap(feed_piece, 1)
    att_low_y, att_high_x, att_low_d, att_high_d = event(att_low_y, att_high_x, att_low_d, att_high_d)
    other_rows, other_partner, feed_piece = event(other_rows, other_partner, feed_piece)
    feed_p[2] = z_swap(feed_piece, 2)
    rows = own_rows.astype(F32)
    gain_one = gains_all[:, 0].astype(F32)
    gain_two = gains_all[:, 1].astype(F32)

    normed_all, queries, keys_all, values_all, w_queries, w_keys, w_values, w_out = project(
        (own_rows, other_rows, partner_rows, other_partner), gain_one[None], [att_low, att_low_x, att_low_y, att_low_d, att_high, att_high_x, att_high_y, att_high_d]
    )
    normed_own = normed_all[: 2 * chunk]
    outer_only = (1 - inner)[None].astype(jnp.int32)
    parts = [None] * 4

    def attend(n):
        return attend_forward(outer_only, scalars, queries, keys_all, values_all, n, 1)

    queries, feed_x[0], feed_y[0] = event(queries, feed_x[0], feed_y[0])
    feed_d[0] = y_swap(feed_x[0])
    parts[0] = attend(0)
    queries, feed_p[1], _ = event(queries, feed_p[1], parts[0][0])
    feed_x[1], feed_y[1] = x_swap(feed_p[1]), y_swap(feed_p[1])
    parts[1] = attend(1)
    queries, feed_d[0], feed_p[2], _ = event(queries, feed_d[0], feed_p[2], parts[1][0])
    feed_y[2] = y_swap(feed_p[2])
    feed_p[3] = z_swap(feed_p[2], 1)
    parts[2] = attend(2)
    queries, feed_x[1], feed_y[1], _ = event(queries, feed_x[1], feed_y[1], parts[2][0])
    batch_x = x_swap(jnp.stack([feed_y[1], feed_p[2]]))
    parts[3] = attend(3)
    mixed = jnp.concatenate([p[0] for p in parts], axis=1)
    branch = matmul_nt(mixed, w_out)
    branch_own, branch_other, feed_p[3], feed_y[2], teacher = event(
        branch[:chunk], branch[chunk:].astype(BF), feed_p[3], feed_y[2], teacher
    )
    feed_y[3] = y_swap(feed_p[3])
    branch_other, batch_x, feed_y[3] = event(core_swap(branch_other), batch_x, feed_y[3])
    batch_x3, x_2 = event(jnp.stack([feed_p[3], feed_y[3]]), batch_x[1])
    batch_x3 = x_swap(batch_x3)
    feed_d[2] = y_swap(x_2)
    teacher_rel = turn(teacher)
    middle = rows + branch_own + branch_other.astype(F32)

    scaled_two, inverse_two = norm_forward(middle)
    normed_two = (scaled_two * gain_two).astype(BF)
    normed_two_all = jnp.concatenate([normed_two, core_swap_halves(normed_two)], axis=0)
    silus, slopes, hiddens, feed = [None] * 4, [None] * 4, [None] * 4, None
    pieces = [
        [alone(feed_p[0]), alone(feed_x[0]), alone(feed_y[0]), alone(feed_d[0])],
        [alone(feed_p[1]), alone(feed_x[1]), alone(feed_y[1]), (batch_x, 0)],
    ]
    for k in range(4):
        if k == 2:
            feed, feed_d[2], teacher_rel = event(feed, feed_d[2], teacher_rel)
            teacher_rows = moved_home(teacher_rel)
            pieces.append([alone(feed_p[2]), (batch_x, 1), alone(feed_y[2]), alone(feed_d[2])])
        if k == 3:
            feed, batch_x3 = event(feed, batch_x3)
            pieces.append([alone(feed_p[3]), (batch_x3, 0), alone(feed_y[3]), (batch_x3, 1)])
        silus[k], slopes[k], hiddens[k], feed = feed_forward(normed_two_all, pieces[k], feed)
    feed_own, feed_other, teacher_rows = event(feed[:chunk], feed[chunk:].astype(BF), teacher_rows)
    final = middle + feed_own + core_swap(feed_other).astype(F32)

    own_place = jnp.where(first, chunk_low, chunk_high) * chunk
    valid = (own_place + jnp.arange(chunk, dtype=jnp.int32) < length)[:, None]
    teacher_rows = jnp.where(moves, teacher_rows, teacher_rel)
    grad_final = jnp.where(valid, final - teacher_rows.astype(F32), 0.0) * (total_rows / count)
    grad_feed = grad_final.astype(BF)
    grad_feed_all, output = event(jnp.concatenate([grad_feed, core_swap(grad_feed)], axis=0), turn(final.astype(BF)))
    output_rel = output
    output = moved_home(output)

    def add(a, b):
        return (a.astype(F32) + b.astype(F32)).astype(BF)

    def total_of(own, x, y):
        return own.astype(F32) + x.astype(F32) + y.astype(F32)

    def feed_back(k, total):
        pair = slice(k, k + 2)
        return feed_backward(normed_two_all, grad_feed_all, silus[pair], slopes[pair], hiddens[pair], pieces[pair], total, k == 0)

    (grad_x,), ((own_2, x_2, y_2, d_2), (own_3, x_3, y_3, d_3)) = feed_back(2, None)
    grad_x, d_2, d_3 = event(grad_x, d_2, d_3)
    d_2, d_3 = y_swap(d_2), x_swap(d_3)
    (grad_x, grad_x_other), ((own_0, x_0, y_0, d_0), (own_1, x_1, y_1, d_1)) = feed_back(0, grad_x)
    grad_x, grad_x_other, output, d_2, d_3, d_0, d_1, y_2, x_3 = event(grad_x, grad_x_other, output, d_2, d_3, d_0, d_1, y_2, x_3)
    grad_x_other, batch_x, batch_y = event(grad_x_other, jnp.stack([add(x_2, d_2), x_3]), jnp.stack([y_2, add(y_3, d_3)]))
    batch_x, batch_y = x_swap(batch_x), y_swap(batch_y)
    tile = chunk // 2
    first_rows, second_rows = core_swap(grad_x_other[:tile]), core_swap(grad_x_other[tile:])
    grad_middle, grad_branch, grad_gain_two = norm_grads(grad_x, first_rows, second_rows, middle, grad_final, gain_two)
    grad_gain_two = grad_gain_two[0]
    grad_branch_both = jnp.concatenate([grad_branch, core_swap_halves(grad_branch)], axis=0)
    grad_mixed = matmul(grad_branch_both, w_out).astype(BF)
    half_width = mixed.shape[1] // 2

    def attend_back(n):
        lse = jnp.concatenate([parts[2 * n][1], parts[2 * n + 1][1]], axis=0)
        return attend_backward(scalars, queries, keys_all, values_all, mixed[:, n * half_width : (n + 1) * half_width], grad_mixed, lse, 2 * n)

    gq_a, gk_a, gv_a = attend_back(0)
    gq_a, grad_mixed, d_0, d_1 = event(gq_a, grad_mixed, d_0, d_1)
    d_0, d_1 = y_swap(d_0), x_swap(d_1)
    gq_b, gk_b, gv_b = attend_back(1)

    gq_b, batch_x, batch_y, d_0, d_1, x_1, y_0 = event(gq_b, batch_x, batch_y, d_0, d_1, x_1, y_0)
    grad_queries, batch_x, batch_y, part_3, part_2, gk_b, gv_b = event(
        jnp.concatenate([gq_a, gq_b], axis=1),
        jnp.stack([add(x_0, d_0), x_1]),
        jnp.stack([y_0, add(y_1, d_1)]),
        total_of(own_3, batch_x[1], batch_y[1]).astype(BF),
        total_of(own_2, batch_x[0], batch_y[0]).astype(BF),
        gk_b,
        gv_b,
    )
    batch_x, batch_y, part_3 = x_swap(batch_x), y_swap(batch_y), z_swap(part_3, 1)
    grad_keys = jnp.concatenate([gk_a, gk_b], axis=1)
    grad_values = jnp.concatenate([gv_a, gv_b], axis=1)
    part_own, part_other, partner_part, other_partner_part = rows_grads(grad_queries, grad_keys, grad_values, w_queries, w_keys, w_values)
    part_other, other_partner_part, grad_queries = event(core_swap(part_other), core_swap(other_partner_part), grad_queries)
    (from_partner,) = event((partner_part + other_partner_part.astype(F32)).astype(BF))
    from_partner = z_swap(from_partner, 1)
    (own_e, x_e, y_e, d_e), (own_o, x_o, y_o, d_o) = attention_grads(normed_all, grad_branch_both, grad_queries, grad_keys, grad_values, mixed)
    quarter_cols = grad_queries.shape[1] // 4
    half_cols = 4 * quarter_cols
    d_e, d_o, x_e, y_e, x_o, y_o, part_3, part_2 = event(d_e, d_o, x_e, y_e, x_o, y_o, part_3, part_2)
    (part_2,) = event(add(part_2, part_3))
    part_2 = z_swap(part_2, 2)
    batch_x, batch_y, d_e, d_o = event(batch_x, batch_y, d_e, d_o)
    d_e, d_o = y_swap(d_e), x_swap(d_o)
    (part_1,) = event(total_of(own_1, batch_x[1], batch_y[1]).astype(BF))
    part_1 = z_swap(part_1, 1)
    part_0 = total_of(own_0, batch_x[0], batch_y[0])
    (from_partner,) = event(from_partner)
    _, grad_rows, grad_gain_one = norm_grads(part_own, part_other, from_partner, own_rows, grad_middle, gain_one)
    grad_rows, gain_a, gain_b, part_2 = event(grad_rows, grad_gain_one[0], grad_gain_two, part_2)
    grad_rows = turn(grad_rows)
    grad_inputs = moved_home(grad_rows)
    d_e, d_o = event(d_e, d_o)
    batch_x, batch_y = event(jnp.stack([add(x_e, d_e), x_o]), jnp.stack([y_e, add(y_o, d_o)]))
    batch_x, batch_y = x_swap(batch_x), y_swap(batch_y)
    part_1, part_2, part_0 = event(part_1, part_2, part_0)
    feed_total = part_0 + part_1.astype(F32) + part_2.astype(F32)
    feed_keep, feed_give = pick(jnp.split(feed_total, 2, axis=1))
    feed_give = core_swap(feed_give.astype(BF))

    quarter = model // 4
    a, b, c, d = jnp.split(jnp.stack([gain_a, gain_b], axis=0), 4, axis=1)
    sent = x_swap(jnp.concatenate([b, d], axis=1))

    batch_x, batch_y, sent = event(batch_x, batch_y, sent)
    even, odd = total_of(own_e, batch_x[0], batch_y[0]), total_of(own_o, batch_x[1], batch_y[1])
    att_13, att_2 = jnp.stack([even[:, half_cols:], odd[:, half_cols:]]).astype(BF), odd[:, :half_cols].astype(BF)
    att_13, att_2, a, c, sent = event(att_13, att_2, a, c, sent)
    att_13 = z_swap(att_13, 1)
    a, c = a + sent[:, :quarter], c + sent[:, quarter:]
    sent = y_swap(c)
    att_13, att_2, sent = event(att_13, att_2, sent)
    att_2 = z_swap(add(att_2, att_13[1]), 2)
    att_1 = att_13[0]
    a = a + sent
    keep, give = pick(jnp.split(a, 2, axis=1))
    sent = core_swap(give)
    feed_give, sent = event(feed_give, sent)
    a = keep + sent
    size = a.shape[1] // 4
    total = lax.dynamic_slice_in_dim(a, z * size, size, 1)
    for k in range(1, 4):
        total = total + z_swap(lax.dynamic_slice_in_dim(a, (z ^ k) * size, size, 1), k)
    grad_gains = jnp.swapaxes(total, 0, 1)
    grad_inputs = jnp.where(moves, grad_inputs, grad_rows).astype(F32)
    output = jnp.where(moves, output, output_rel)
    feed_out = sort_cores(feed_keep, feed_give.astype(F32), 2)
    attention_total = even[:, :half_cols] + att_1.astype(F32) + att_2.astype(F32)
    attention_total = jnp.stack([attention_total[:, n * quarter_cols : (n + 1) * quarter_cols] for n in range(4)])

    def to_home(total):
        keep, give = pick(jnp.split(total, 2, axis=1))
        return sort_cores(keep, core_swap(give.astype(BF)).astype(F32), 2)

    attention_out = to_home(attention_total)

    return (
        output,
        grad_inputs,
        jnp.swapaxes(attention_out[:3], 0, 1),
        attention_out[3],
        jnp.swapaxes(feed_out[:2], 0, 1),
        feed_out[2],
        grad_gains,
    )


def solution(mesh):
    square = dict(mesh.shape) == {"dp": 8, "tensor": 4}
    return jax.shard_map(
        on_square if square else on_device,
        mesh=mesh,
        in_specs=(
            P(("dp", "tensor"), None),
            P(("dp", "tensor"), None),
            P(),
            P("dp", None, "tensor"),
            P("dp", "tensor"),
            P("dp", None, "tensor"),
            P("dp", "tensor"),
            P("dp", None),
        ),
        out_specs=(
            P(("dp", "tensor"), None),
            P(("dp", "tensor"), None),
            P("dp", None, "tensor"),
            P("dp", "tensor"),
            P("dp", None, "tensor"),
            P("dp", "tensor"),
            P(("dp", "tensor"), None),
        ),
        check_vma=False,
    )
```

```python
import math

import jax
import jax.numpy as jnp
from jax import lax
from jax.experimental import pallas as pl
from jax.experimental.pallas import tpu as pltpu
from jax.sharding import PartitionSpec as P

HEAD = 64


negative = -1e30


def norm_forward(values):
    inverse = lax.rsqrt(jnp.mean(values * values, axis=-1, keepdims=True) + 1e-05)
    return (values * inverse, inverse)


def norm_backward(grad_normed, scaled, inverse, gain):
    grad_scaled = grad_normed * gain
    grad_values = inverse * (
        grad_scaled - scaled * jnp.mean(grad_scaled * scaled, axis=-1, keepdims=True)
    )
    return (grad_values, jnp.sum(grad_normed * scaled, axis=0))


def key_limit(query_index):
    return query_index + 1


def score_block(query_block, keys_all, query_start, key_start, length):
    block = query_block.shape[0]
    key_block = lax.dynamic_slice_in_dim(keys_all, key_start, block, 0)
    scores = jnp.einsum("qhe,khe->hqk", query_block, key_block, preferred_element_type=jnp.float32)
    query_pos = query_start + jnp.arange(block, dtype=jnp.int32)
    key_pos = key_start + jnp.arange(block, dtype=jnp.int32)
    allowed = (key_pos[None, :] <= query_pos[:, None]) & (key_pos[None, :] < length)
    return jnp.where(allowed[None], scores, negative)


def attention_forward(queries, keys_all, values_all, length):
    slot, heads, head = queries.shape
    block = min(512, slot)
    block_count = slot // block

    def query_step(index, carry):
        mixed, maxima, totals = carry
        query_start = index * block
        query_block = lax.dynamic_slice_in_dim(queries, query_start, block, 0)
        upper = key_limit(index)

        def stats_step(inner, state):
            maximum, total = state
            scores = score_block(query_block, keys_all, query_start, inner * block, length)
            larger = jnp.maximum(maximum, jnp.max(scores, axis=-1))
            total = total * jnp.exp(maximum - larger) + jnp.sum(
                jnp.exp(scores - larger[..., None]), axis=-1
            )
            return (larger, total)

        start_state = (
            jnp.full((heads, block), negative, jnp.float32),
            jnp.zeros((heads, block), jnp.float32),
        )
        maximum, total = lax.fori_loop(0, upper, stats_step, start_state)

        def mix_step(inner, accum):
            key_start = inner * block
            scores = score_block(query_block, keys_all, query_start, key_start, length)
            weights = (jnp.exp(scores - maximum[..., None]) / total[..., None]).astype(jnp.bfloat16)
            value_block = lax.dynamic_slice_in_dim(values_all, key_start, block, 0)
            return accum + jnp.einsum(
                "hqk,khe->qhe", weights, value_block, preferred_element_type=jnp.float32
            )

        accum = lax.fori_loop(0, upper, mix_step, jnp.zeros((block, heads, head), jnp.float32))
        mixed = lax.dynamic_update_slice_in_dim(mixed, accum, query_start, 0)
        maxima = lax.dynamic_update_index_in_dim(maxima, maximum, index, 0)
        totals = lax.dynamic_update_index_in_dim(totals, total, index, 0)
        return (mixed, maxima, totals)

    start = (
        jnp.zeros((slot, heads, head), jnp.float32),
        jnp.zeros((block_count, heads, block), jnp.float32),
        jnp.zeros((block_count, heads, block), jnp.float32),
    )
    return lax.fori_loop(0, block_count, query_step, start)


def attention_backward(queries, keys_all, values_all, grad_mixed, maxima, totals, length):
    slot, heads, head = queries.shape
    block = min(512, slot)
    block_count = slot // block

    def query_step(index, carry):
        grad_queries, grad_keys, grad_values = carry
        query_start = index * block
        query_block = lax.dynamic_slice_in_dim(queries, query_start, block, 0)
        grad_block = lax.dynamic_slice_in_dim(grad_mixed, query_start, block, 0)
        maximum = lax.dynamic_index_in_dim(maxima, index, 0, keepdims=False)
        total = lax.dynamic_index_in_dim(totals, index, 0, keepdims=False)
        upper = key_limit(index)

        def probs_of(inner):
            key_start = inner * block
            scores = score_block(query_block, keys_all, query_start, key_start, length)
            probs = jnp.exp(scores - maximum[..., None]) / total[..., None]
            value_block = lax.dynamic_slice_in_dim(values_all, key_start, block, 0)
            grad_probs = jnp.einsum(
                "qhe,khe->hqk", grad_block, value_block, preferred_element_type=jnp.float32
            )
            return (probs, grad_probs, key_start)

        def delta_step(inner, delta):
            probs, grad_probs, key_start = probs_of(inner)
            return delta + jnp.sum(probs * grad_probs, axis=-1)

        delta = lax.fori_loop(0, upper, delta_step, jnp.zeros((heads, block), jnp.float32))

        def grad_step(inner, state):
            grad_query, grad_keys, grad_values = state
            probs, grad_probs, key_start = probs_of(inner)
            grad_scores = (probs * (grad_probs - delta[..., None])).astype(jnp.bfloat16)
            key_block = lax.dynamic_slice_in_dim(keys_all, key_start, block, 0)
            grad_query = grad_query + jnp.einsum(
                "hqk,khe->qhe", grad_scores, key_block, preferred_element_type=jnp.float32
            )
            key_part = jnp.einsum(
                "hqk,qhe->khe", grad_scores, query_block, preferred_element_type=jnp.float32
            )
            value_part = jnp.einsum(
                "hqk,qhe->khe",
                probs.astype(jnp.bfloat16),
                grad_block,
                preferred_element_type=jnp.float32,
            )
            old_keys = lax.dynamic_slice_in_dim(grad_keys, key_start, block, 0)
            old_values = lax.dynamic_slice_in_dim(grad_values, key_start, block, 0)
            grad_keys = lax.dynamic_update_slice_in_dim(
                grad_keys, old_keys + key_part, key_start, 0
            )
            grad_values = lax.dynamic_update_slice_in_dim(
                grad_values, old_values + value_part, key_start, 0
            )
            return (grad_query, grad_keys, grad_values)

        start_state = (jnp.zeros((block, heads, head), jnp.float32), grad_keys, grad_values)
        grad_query, grad_keys, grad_values = lax.fori_loop(0, upper, grad_step, start_state)
        grad_queries = lax.dynamic_update_slice_in_dim(grad_queries, grad_query, query_start, 0)
        return (grad_queries, grad_keys, grad_values)

    empty = jnp.zeros((slot, heads, head), jnp.float32)
    return lax.fori_loop(0, block_count, query_step, (empty, empty, empty))


def on_device(inputs, teacher, lengths, w_qkv, w_out_t, w_gate_up, w_down_t, gains):
    own_rows = inputs.shape[0]
    slot = own_rows * lax.axis_size("tensor")
    total_rows = slot * lax.axis_size("dp")
    local_width = w_qkv.shape[2]
    local_heads = local_width // HEAD
    scale = 1.0 / math.sqrt(HEAD)
    length = lax.dynamic_index_in_dim(lengths, lax.axis_index("dp"), 0, keepdims=False)
    count = jnp.sum(lengths).astype(jnp.float32)
    own_start = lax.axis_index("tensor") * own_rows
    row_pos = own_start + jnp.arange(own_rows, dtype=jnp.int32)
    valid = (row_pos < length)[:, None]
    qkv_all, out_all, gains_all = (
        lax.all_gather(w_qkv, "dp", axis=0, tiled=True),
        lax.all_gather(w_out_t, "dp", axis=0, tiled=True),
        lax.all_gather(gains, "dp", axis=0, tiled=True),
    )
    gate_up_all, down_all = (
        lax.all_gather(w_gate_up, "dp", axis=0, tiled=True),
        lax.all_gather(w_down_t, "dp", axis=0, tiled=True),
    )
    gain_one = gains_all[:, 0].astype(jnp.float32)
    gain_two = gains_all[:, 1].astype(jnp.float32)
    rows = inputs.astype(jnp.float32)
    scaled_one, inverse_one = norm_forward(rows)
    normed_one = (scaled_one * gain_one).astype(jnp.bfloat16)
    gathered_one = lax.all_gather(normed_one, "tensor", axis=0, tiled=True)
    qkv = jnp.einsum("rd,dcf->rcf", gathered_one, qkv_all, preferred_element_type=jnp.float32)
    queries = (qkv[:, 0] * scale).astype(jnp.bfloat16).reshape(slot, local_heads, HEAD)
    keys_all = qkv[:, 1].astype(jnp.bfloat16).reshape(slot, local_heads, HEAD)
    values_all = qkv[:, 2].astype(jnp.bfloat16).reshape(slot, local_heads, HEAD)
    mixed, maxima, totals = attention_forward(queries, keys_all, values_all, length)
    mixed = mixed.reshape(slot, local_width).astype(jnp.bfloat16)
    piece = mixed
    middle = rows + lax.psum_scatter(
        jnp.einsum("rk,dk->rd", piece, out_all, preferred_element_type=jnp.float32).astype(
            jnp.bfloat16
        ),
        "tensor",
        scatter_dimension=0,
        tiled=True,
    ).astype(jnp.float32)
    scaled_two, inverse_two = norm_forward(middle)
    normed_two = (scaled_two * gain_two).astype(jnp.bfloat16)
    gathered_two = lax.all_gather(normed_two, "tensor", axis=0, tiled=True)
    rows_two = None
    gate_up = jnp.einsum(
        "rd,dcf->rcf", gathered_two, gate_up_all, preferred_element_type=jnp.float32
    )
    gate = gate_up[:, 0]
    upper = gate_up[:, 1]
    sigmoid = jax.nn.sigmoid(gate)
    hidden = (gate * sigmoid * upper).astype(jnp.bfloat16)
    piece = hidden
    final = middle + lax.psum_scatter(
        jnp.einsum("rf,df->rd", piece, down_all, preferred_element_type=jnp.float32).astype(
            jnp.bfloat16
        ),
        "tensor",
        scatter_dimension=0,
        tiled=True,
    ).astype(jnp.float32)
    output = final.astype(jnp.bfloat16)
    grad_final = jnp.where(valid, final - teacher.astype(jnp.float32), 0.0) * (total_rows / count)
    grad_feed = lax.all_gather(grad_final.astype(jnp.bfloat16), "tensor", axis=0, tiled=True)
    grad_down = jnp.einsum("rd,rf->df", grad_feed, hidden, preferred_element_type=jnp.float32)
    grad_hidden = jnp.einsum("rd,df->rf", grad_feed, down_all, preferred_element_type=jnp.float32)
    grad_gate = grad_hidden * upper * (sigmoid * (1.0 + gate * (1.0 - sigmoid)))
    grad_upper = grad_hidden * (gate * sigmoid)
    grad_gu = jnp.stack([grad_gate, grad_upper], axis=1).astype(jnp.bfloat16)
    rows_two = lax.all_gather(normed_two, "tensor", axis=0, tiled=True)
    grad_gate_up = jnp.einsum("rd,rcf->dcf", rows_two, grad_gu, preferred_element_type=jnp.float32)
    piece = grad_gu
    grad_normed_two = lax.psum_scatter(
        jnp.einsum("rcf,dcf->rd", piece, gate_up_all, preferred_element_type=jnp.float32).astype(
            jnp.bfloat16
        ),
        "tensor",
        scatter_dimension=0,
        tiled=True,
    ).astype(jnp.float32)
    grad_norm_two, grad_gain_two = norm_backward(grad_normed_two, scaled_two, inverse_two, gain_two)
    grad_middle = grad_final + grad_norm_two
    grad_branch = lax.all_gather(grad_middle.astype(jnp.bfloat16), "tensor", axis=0, tiled=True)
    grad_out = jnp.einsum("rd,rk->dk", grad_branch, mixed, preferred_element_type=jnp.float32)
    grad_mixed = jnp.einsum("rd,dk->rk", grad_branch, out_all, preferred_element_type=jnp.float32)
    grad_mixed = grad_mixed.astype(jnp.bfloat16).reshape(slot, local_heads, HEAD)
    grad_queries, grad_keys, grad_values = attention_backward(
        queries, keys_all, values_all, grad_mixed, maxima, totals, length
    )
    grad_rows_qkv = jnp.stack(
        [
            grad_queries.reshape(slot, local_width).astype(jnp.bfloat16) * scale,
            grad_keys.reshape(slot, local_width).astype(jnp.bfloat16),
            grad_values.reshape(slot, local_width).astype(jnp.bfloat16),
        ],
        axis=1,
    )
    rows_one = lax.all_gather(normed_one, "tensor", axis=0, tiled=True)
    grad_qkv = jnp.einsum(
        "rd,rcf->dcf", rows_one, grad_rows_qkv, preferred_element_type=jnp.float32
    )
    piece = grad_rows_qkv
    grad_normed_one = lax.psum_scatter(
        jnp.einsum("rcf,dcf->rd", piece, qkv_all, preferred_element_type=jnp.float32).astype(
            jnp.bfloat16
        ),
        "tensor",
        scatter_dimension=0,
        tiled=True,
    ).astype(jnp.float32)
    grad_norm_one, grad_gain_one = norm_backward(grad_normed_one, scaled_one, inverse_one, gain_one)
    grad_inputs = grad_middle + grad_norm_one
    grad_qkv, grad_out, grad_gate_up, grad_down = (
        lax.psum_scatter(
            grad_qkv.astype(jnp.bfloat16), "dp", scatter_dimension=0, tiled=True
        ).astype(jnp.float32),
        lax.psum_scatter(
            grad_out.astype(jnp.bfloat16), "dp", scatter_dimension=0, tiled=True
        ).astype(jnp.float32),
        lax.psum_scatter(
            grad_gate_up.astype(jnp.bfloat16), "dp", scatter_dimension=0, tiled=True
        ).astype(jnp.float32),
        lax.psum_scatter(
            grad_down.astype(jnp.bfloat16), "dp", scatter_dimension=0, tiled=True
        ).astype(jnp.float32),
    )
    grad_gains = lax.psum_scatter(
        jnp.stack([grad_gain_one, grad_gain_two], axis=1),
        ("dp", "tensor"),
        scatter_dimension=0,
        tiled=True,
    )
    return (output, grad_inputs, grad_qkv, grad_out, grad_gate_up, grad_down, grad_gains)


BF = jnp.bfloat16
F32 = jnp.float32
AXES = ("dp", "tensor")
LIGHT = pl.CostEstimate(flops=1000, bytes_accessed=1000, transcendentals=0)


def shift(value, where):
    pairs = []
    for y in range(2):
        for x in range(2):
            for c in range(2):
                for z in range(4):
                    to = where(y, x, c, z)
                    if to is not None:
                        ty, tx, tc, tz = to
                        pairs.append((((y * 2 + x) * 2 + c) * 4 + z, ((ty * 2 + tx) * 2 + tc) * 4 + tz))
    return lax.ppermute(value, AXES, pairs)


def core_swap(value):
    return shift(value, lambda y, x, c, z: (y, x, 1 - c, z))


def core_swap_halves(value):
    half = value.shape[0] // 2
    return jnp.concatenate([core_swap(value[:half]), core_swap(value[half:])], axis=0)


def x_swap(value):
    return shift(value, lambda y, x, c, z: (y, 1 - x, c, z))


def y_swap(value):
    return shift(value, lambda y, x, c, z: (1 - y, x, c, z))


def square_swap(value):
    return shift(value, lambda y, x, c, z: (1 - y, 1 - x, c, z))


def z_swap(value, bits):
    return shift(value, lambda y, x, c, z: (y, x, c, z ^ bits))


def home_of(y, x, c, z):
    if (c == 1 and z < 2) or (c == 0 and z >= 2):
        return (y, x, 1 - c, 3 - z)
    return (y, x, c, z)


def home_swap(value):
    return shift(value, home_of)


def moved_home(value):
    return shift(value, lambda *place: None if home_of(*place) == place else home_of(*place))


def partner_of_home(y, x, c, z):
    y, x, c, z = home_of(y, x, c, z)
    z ^= 1
    if c == 1 and z in (1, 2):
        return None
    return (y, x, c, z)


def head_masks(rows):
    lanes = lax.broadcasted_iota(jnp.int32, (rows, 2 * HEAD), 1)
    return (lanes < HEAD, lanes >= HEAD)


def dot_nt(a, b):
    return lax.dot_general(a, b, (((1,), (1,)), ((), ())), preferred_element_type=F32)


def dot_nn(a, b):
    return lax.dot_general(a, b, (((1,), (0,)), ((), ())), preferred_element_type=F32)


def dot_tn(a, b):
    return lax.dot_general(a, b, (((0,), (0,)), ((), ())), preferred_element_type=F32)


def attend_forward_kernel(outer_ref, sc_ref, q_ref, k_ref, v_ref, o_ref, lse_ref):
    chunk = q_ref.shape[0] // 2
    tile = chunk // 2
    lanes = 2 * HEAD
    head = pl.program_id(0) % 2
    low, high, low_partner, extra_row, extra_key = [pl.multiple_of(sc_ref[i], chunk) for i in range(5)]
    mine = lax.broadcasted_iota(jnp.int32, (tile, lanes), 1) // HEAD == head

    def fold(op, parts):
        parts = [p[:, i * lanes : (i + 1) * lanes] for p in parts for i in range(p.shape[1] // lanes)]
        while len(parts) > 1:
            parts = [op(parts[i], parts[i + 1]) if i + 1 < len(parts) else parts[i] for i in range(0, len(parts), 2)]
        return parts[0]

    def unit(row, own, own_count, half, others):
        rows = pl.ds(pl.multiple_of(row + half * tile, tile), tile)
        query = jnp.where(mine, q_ref[rows, :], 0)
        blocks = [(pl.ds(start, chunk), count, chunk, None) for start, count in others]
        blocks.append((pl.ds(own, (half + 1) * tile), own_count, (half + 1) * tile, half * tile))
        scores = []
        for keys, count, width, diagonal in blocks:
            s = dot_nt(query, k_ref[keys, :])
            s = s + jnp.where(lax.broadcasted_iota(jnp.int32, (1, width), 1) < count, 0.0, negative)
            if diagonal is not None:
                cols = lax.broadcasted_iota(jnp.int32, (tile, width), 1)
                s = jnp.where(cols <= lax.broadcasted_iota(jnp.int32, (tile, width), 0) + diagonal, s, negative)
            scores.append(s)
        top = jnp.max(fold(jnp.maximum, scores), axis=1, keepdims=True)
        weights = [jnp.exp(s - top) for s in scores]
        total = jnp.sum(fold(jnp.add, weights), axis=1, keepdims=True)
        mixed = None
        for w, (keys, _, _, _) in zip(weights, blocks):
            part = dot_nn(w.astype(BF), v_ref[keys, :])
            mixed = part if mixed is None else mixed + part
        return rows, mixed / total, top + jnp.log(total)

    def finish(units):
        for rows, mixed, lse in units:
            mixed = mixed.astype(BF)
            o_ref[rows, :] = jnp.where(mine, mixed, o_ref[rows, :])
            lse_ref[0, pl.ds(head, 1), rows] = jnp.transpose(jnp.broadcast_to(lse, (tile, lanes)))[0:1]

    near = [(low, sc_ref[5]), (low_partner, sc_ref[7])]
    extra = [(extra_key, sc_ref[8])]

    @pl.when(outer_ref[0] == 1)
    def _():
        for half in range(2):
            finish([unit(high, high, sc_ref[6], half, near + extra), unit(low, low, sc_ref[5], half, [])])

    @pl.when(outer_ref[0] == 0)
    def _():
        for half in range(2):
            finish([unit(high, high, sc_ref[6], half, near), unit(low, low, sc_ref[5], half, extra)])


def attend_forward(outer, scalars, queries, keys_all, values_all, start, pairs):
    rows = queries.shape[0]
    width = pairs * 2 * HEAD
    slot = keys_all.shape[0]
    own = lambda i, *_: (0, i // 2)
    column = lambda i, *_: (0, i // 2 + start)
    return pl.pallas_call(
        attend_forward_kernel,
        out_shape=(
            jax.ShapeDtypeStruct((rows, width), BF),
            jax.ShapeDtypeStruct((pairs, 8, rows), F32),
        ),
        grid_spec=pltpu.PrefetchScalarGridSpec(
            num_scalar_prefetch=2,
            grid=(2 * pairs,),
            in_specs=[
                pl.BlockSpec((rows, 2 * HEAD), column),
                pl.BlockSpec((slot, 2 * HEAD), column),
                pl.BlockSpec((slot, 2 * HEAD), column),
            ],
            out_specs=(
                pl.BlockSpec((rows, 2 * HEAD), own),
                pl.BlockSpec((1, 8, rows), lambda i, *_: (i // 2, 0, 0)),
            ),
        ),
        compiler_params=pltpu.CompilerParams(vmem_limit_bytes=24 << 20),
        cost_estimate=LIGHT,
        name="attend_forward",
    )(outer, scalars, queries, keys_all, values_all)


def attend_backward_kernel(sc_ref, q_ref, k_ref, v_ref, o_ref, g_ref, lse_ref, dq_ref, dk_ref, dv_ref, dq_acc, dk_acc, dv_acc, delta_ref):
    chunk = q_ref.shape[0] // 2
    tile = chunk // 2
    low, high_row, low_partner, extra_row, extra_key = [pl.multiple_of(sc_ref[i], chunk) for i in range(5)]
    dq_acc[...] = jnp.zeros_like(dq_acc)
    dk_acc[...] = jnp.zeros_like(dk_acc)
    dv_acc[...] = jnp.zeros_like(dv_acc)
    for part in range(4):
        rows = pl.ds(part * tile, tile)
        product = jnp.transpose(o_ref[rows, :].astype(F32) * g_ref[rows, :].astype(F32))
        delta_ref[0:1, rows] = jnp.sum(product[:HEAD], axis=0, keepdims=True)
        delta_ref[1:2, rows] = jnp.sum(product[HEAD:], axis=0, keepdims=True)

    def step(head, row, width, key, count, shift_rows):
        rows = pl.ds(row, width)
        keys = pl.ds(key, tile)
        query = jnp.where(head_masks(width)[head], q_ref[rows, :], 0)
        grad = jnp.where(head_masks(width)[head], g_ref[rows, :], 0)
        key_block = k_ref[keys, :]
        scores = dot_nt(key_block, query)
        index = lax.broadcasted_iota(jnp.int32, (tile, width), 0)
        allowed = index < count
        if shift_rows is not None:
            allowed = allowed & (index <= lax.broadcasted_iota(jnp.int32, (tile, width), 1) + shift_rows)
        probs = jnp.exp(jnp.where(allowed, scores, negative) - lse_ref[0, head : head + 1, rows])
        grad_probs = dot_nt(v_ref[keys, :], grad)
        grad_scores = (probs * (grad_probs - delta_ref[head : head + 1, rows])).astype(BF)
        dv_acc[keys, :] += dot_nn(probs.astype(BF), grad)
        dk_acc[keys, :] += dot_nn(grad_scores, query)
        key_masked = jnp.where(head_masks(tile)[head], key_block, 0)
        dq_acc[rows, :] += dot_tn(grad_scores, key_masked)

    for head in range(2):
        for half in range(2):
            down = half * tile
            add = lambda start: pl.multiple_of(start + down, tile)
            step(head, add(low), chunk - down, add(low), sc_ref[5] - down, 0)
            step(head, add(high_row), chunk - down, add(high_row), sc_ref[6] - down, 0)
            step(head, high_row, chunk, add(low), sc_ref[5] - down, None)
            step(head, high_row, chunk, add(low_partner), sc_ref[7] - down, None)
            step(head, extra_row, chunk, add(extra_key), sc_ref[8] - down, None)
    dq_ref[...] = (dq_acc[...] * (1.0 / math.sqrt(HEAD))).astype(BF)
    dk_ref[...] = dk_acc[...].astype(BF)
    dv_ref[...] = dv_acc[...].astype(BF)


def attend_backward(scalars, queries, keys_all, values_all, mixed, grad_mixed, lse, start):
    rows, width = mixed.shape
    pairs = width // (2 * HEAD)
    slot = keys_all.shape[0]
    own = lambda i, sc: (0, i)
    column = lambda i, sc: (0, i + start)
    own_spec = pl.BlockSpec((rows, 2 * HEAD), own)
    row_spec = pl.BlockSpec((rows, 2 * HEAD), column)
    slot_spec = pl.BlockSpec((slot, 2 * HEAD), column)
    return pl.pallas_call(
        attend_backward_kernel,
        out_shape=(
            jax.ShapeDtypeStruct((rows, width), BF),
            jax.ShapeDtypeStruct((slot, width), BF),
            jax.ShapeDtypeStruct((slot, width), BF),
        ),
        grid_spec=pltpu.PrefetchScalarGridSpec(
            num_scalar_prefetch=1,
            grid=(pairs,),
            in_specs=[row_spec, slot_spec, slot_spec, own_spec, row_spec, pl.BlockSpec((1, 8, rows), lambda i, sc: (i, 0, 0))],
            out_specs=(own_spec, pl.BlockSpec((slot, 2 * HEAD), own), pl.BlockSpec((slot, 2 * HEAD), own)),
            scratch_shapes=[
                pltpu.VMEM((rows, 2 * HEAD), F32),
                pltpu.VMEM((slot, 2 * HEAD), F32),
                pltpu.VMEM((slot, 2 * HEAD), F32),
                pltpu.VMEM((8, rows), F32),
            ],
        ),
        compiler_params=pltpu.CompilerParams(vmem_limit_bytes=32 << 20),
        cost_estimate=LIGHT,
    )(scalars, queries, keys_all, values_all, mixed, grad_mixed, lse)


def project_kernel(*refs):
    rows_refs, gain_ref, weight_refs = refs[:4], refs[4], (refs[5:9], refs[9:13])
    normed_ref, q_ref, k_ref, v_ref, wq_ref, wk_ref, wv_ref, wo_ref = refs[13:]
    step = pl.program_id(0)
    _, block, width = weight_refs[0][0].shape
    part = width // 4
    tile = rows_refs[0].shape[0] // 2

    @pl.when(step == 0)
    def _():
        for k in range(4):
            for r in range(4):
                source = weight_refs[k // 2][r].at[k % 2]
                for n, out in enumerate((wq_ref, wk_ref, wv_ref, wo_ref)):
                    out[r * block : (r + 1) * block, k * part : (k + 1) * part] = source[:, n * part : (n + 1) * part]

    for n in range(4):

        @pl.when(step == n)
        def _():
            for half in range(2):
                rows = slice(half * tile, (half + 1) * tile)
                values = rows_refs[n][rows, :].astype(F32)
                inverse = lax.rsqrt(jnp.mean(values * values, axis=-1, keepdims=True) + 1e-05)
                normed = (values * inverse * gain_ref[...]).astype(BF)
                normed_ref[rows, :] = normed
                k_ref[rows, :] = dot_nn(normed, wk_ref[...]).astype(BF)
                v_ref[rows, :] = dot_nn(normed, wv_ref[...]).astype(BF)
                if n < 2:
                    q_ref[rows, :] = (dot_nn(normed, wq_ref[...]) * (1.0 / math.sqrt(HEAD))).astype(BF)


def project(rows_parts, gain, weights):
    chunk, model = rows_parts[0].shape
    _, block, width = weights[0].shape
    whole = lambda shape: pl.BlockSpec(shape, lambda i: (0,) * len(shape))
    tiles = lambda cols: pl.BlockSpec((chunk, cols), lambda i: (i, 0))
    shape = lambda r, c: jax.ShapeDtypeStruct((r, c), BF)
    return pl.pallas_call(
        project_kernel,
        out_shape=(
            shape(4 * chunk, model),
            shape(2 * chunk, width),
            shape(4 * chunk, width),
            shape(4 * chunk, width),
            shape(model, width),
            shape(model, width),
            shape(model, width),
            shape(model, width),
        ),
        grid=(4,),
        in_specs=[whole((chunk, model))] * 4 + [whole((1, model))] + [whole(w.shape) for w in weights],
        out_specs=(
            tiles(model),
            pl.BlockSpec((chunk, width), lambda i: (jnp.minimum(i, 1), 0)),
            tiles(width),
            tiles(width),
        )
        + tuple(whole((model, width)) for _ in range(4)),
        compiler_params=pltpu.CompilerParams(vmem_limit_bytes=60 << 20),
        cost_estimate=LIGHT,
        name="project",
    )(*rows_parts, gain, *weights)


def rows_grads_kernel(dq_ref, dk_ref, dv_ref, wq_ref, wk_ref, wv_ref, own_ref, other_ref, partner_ref, partner_other_ref):
    step = pl.program_id(0)
    part = dot_nt(dk_ref[...], wk_ref[...]) + dot_nt(dv_ref[...], wv_ref[...])

    @pl.when(step == 0)
    def _():
        own_ref[...] = part + dot_nt(dq_ref[...], wq_ref[...])

    @pl.when(step == 1)
    def _():
        other_ref[...] = (part + dot_nt(dq_ref[...], wq_ref[...])).astype(BF)

    @pl.when(step == 2)
    def _():
        partner_ref[...] = part

    @pl.when(step == 3)
    def _():
        partner_other_ref[...] = part.astype(BF)


def rows_grads(dq, dk, dv, wq, wk, wv):
    slot, width = dk.shape
    model = wq.shape[0]
    chunk = slot // 4
    whole = pl.BlockSpec((model, width), lambda i: (0, 0))
    tiles = pl.BlockSpec((chunk, width), lambda i: (i, 0))
    out = pl.BlockSpec((chunk, model), lambda i: (0, 0))
    shape = lambda t: jax.ShapeDtypeStruct((chunk, model), t)
    return pl.pallas_call(
        rows_grads_kernel,
        out_shape=(shape(F32), shape(BF), shape(F32), shape(BF)),
        grid=(4,),
        in_specs=[pl.BlockSpec((chunk, width), lambda i: (jnp.minimum(i, 1), 0)), tiles, tiles, whole, whole, whole],
        out_specs=(out,) * 4,
        compiler_params=pltpu.CompilerParams(vmem_limit_bytes=40 << 20),
        cost_estimate=LIGHT,
        name="rows_grads",
    )(dq, dk, dv, wq, wk, wv)


def attention_grads_kernel(x_ref, g_ref, dq_ref, dk_ref, dv_ref, mixed_ref, *out_refs):
    rows = g_ref.shape[0]
    x_turned = jnp.transpose(x_ref[...])
    g_turned = jnp.transpose(g_ref[...])
    grads = (
        dot_nn(x_turned[:, :rows], dq_ref[...]),
        dot_nn(x_turned, dk_ref[...]),
        dot_nn(x_turned, dv_ref[...]),
        dot_nn(g_turned, mixed_ref[...]),
    )
    part = dq_ref.shape[1] // 4
    for r in range(4):

        @pl.when(pl.program_id(0) == r)
        def _():
            for k in range(4):
                for n in range(4):
                    start = (k % 2 * 4 + n) * part
                    out_refs[k // 2 * 4 + r][:, start : start + part] = grads[n][:, k * part : (k + 1) * part].astype(BF)


def attention_grads(x, g, dq, dk, dv, mixed):
    rows, model = g.shape
    slot, width = dk.shape
    block = model // 4
    whole = lambda a: pl.BlockSpec(a.shape, lambda i: (0, 0))
    out = pl.pallas_call(
        attention_grads_kernel,
        out_shape=(jax.ShapeDtypeStruct((block, 2 * width), BF),) * 8,
        grid=(4,),
        in_specs=[
            pl.BlockSpec((slot, block), lambda i: (0, i)),
            pl.BlockSpec((rows, block), lambda i: (0, i)),
            whole(dq),
            whole(dk),
            whole(dv),
            whole(mixed),
        ],
        out_specs=(pl.BlockSpec((block, 2 * width), lambda i: (0, 0)),) * 8,
        compiler_params=pltpu.CompilerParams(vmem_limit_bytes=40 << 20),
        cost_estimate=LIGHT,
        name="attention_grads",
    )(x, g, dq, dk, dv, mixed)
    return out[:4], out[4:]


def norm_grads_kernel(halves, part_ref, first_ref, second_ref, values_ref, grad_ref, gain_ref, out_ref, low_ref, gain_grad_ref):
    step = pl.program_id(0)
    values = values_ref[...].astype(F32)
    inverse = lax.rsqrt(jnp.mean(values * values, axis=-1, keepdims=True) + 1e-05)
    scaled = values * inverse

    @pl.when(step == 0)
    def _():
        gain_grad_ref[...] = jnp.zeros_like(gain_grad_ref)

    first, second = first_ref[...].astype(F32), second_ref[...].astype(F32)
    received = jnp.where(step < 2, first, second) if halves else first + second
    grad_normed = part_ref[...] + received
    grad_scaled = grad_normed * gain_ref[...]
    grad = grad_ref[...] + inverse * (grad_scaled - scaled * jnp.mean(grad_scaled * scaled, axis=-1, keepdims=True))
    out_ref[...] = grad
    low_ref[...] = grad.astype(BF)
    gain_grad_ref[...] += jnp.sum(grad_normed * scaled, axis=0, keepdims=True)


def norm_grads(part, first, second, values, grad, gain):
    rows, model = part.shape
    tile = rows // 4
    halves = first.shape[0] < rows
    tiles = pl.BlockSpec((tile, model), lambda i: (i, 0))
    row = pl.BlockSpec((1, model), lambda i: (0, 0))
    return pl.pallas_call(
        lambda *refs: norm_grads_kernel(halves, *refs),
        out_shape=(
            jax.ShapeDtypeStruct((rows, model), F32),
            jax.ShapeDtypeStruct((rows, model), BF),
            jax.ShapeDtypeStruct((1, model), F32),
        ),
        grid=(4,),
        in_specs=[
            tiles,
            pl.BlockSpec((tile, model), lambda i: (jnp.minimum(i, 1), 0)) if halves else tiles,
            pl.BlockSpec((tile, model), lambda i: (jnp.maximum(i - 2, 0), 0)) if halves else tiles,
            tiles,
            tiles,
            row,
        ],
        out_specs=(tiles, tiles, row),
        compiler_params=pltpu.CompilerParams(vmem_limit_bytes=24 << 20),
        cost_estimate=LIGHT,
        name="norm_grads",
    )(part, first, second, values, grad, gain[None])


def feed_forward_kernel(first_piece, *refs):
    x_ref, weight_refs = refs[0], refs[1:5]
    block = weight_refs[0].shape[1]
    if not first_piece:
        y_in_ref = refs[5]
    silu_ref, slope_ref, hidden_ref, y_ref = refs[-4:]
    x = x_ref[...]
    gate = upper = None
    for r in range(4):
        part = x[:, r * block : (r + 1) * block]
        g = dot_nn(part, weight_refs[r][0])
        u = dot_nn(part, weight_refs[r][1])
        gate = g if gate is None else gate + g
        upper = u if upper is None else upper + u
    sigmoid = jax.nn.sigmoid(gate)
    silu = gate * sigmoid
    hidden = (silu * upper).astype(BF)
    silu_ref[...] = silu.astype(BF)
    slope_ref[...] = (upper * (sigmoid * (1.0 + gate * (1.0 - sigmoid)))).astype(BF)
    hidden_ref[...] = hidden
    for r in range(4):
        cols = slice(r * block, (r + 1) * block)
        y = dot_nt(hidden, weight_refs[r][2])
        y_ref[:, cols] = y if first_piece else y + y_in_ref[:, cols]


def alone(piece):
    return (piece[None], 0)


def feed_forward(x, pieces, y):
    rows, model = x.shape
    _, _, block, width = pieces[0][0].shape
    tile = rows // 4
    tiles = lambda cols: pl.BlockSpec((tile, cols), lambda i: (i, 0))
    weight_specs = [pl.BlockSpec((None, 3, block, width), lambda i, n=n: (n, 0, 0, 0)) for _, n in pieces]
    extra = [] if y is None else [y]
    return pl.pallas_call(
        lambda *refs: feed_forward_kernel(y is None, *refs),
        out_shape=tuple(jax.ShapeDtypeStruct((rows, width), BF) for _ in range(3)) + (jax.ShapeDtypeStruct((rows, model), F32),),
        grid=(4,),
        in_specs=[tiles(model)] + weight_specs + [tiles(model) for _ in extra],
        out_specs=(tiles(width), tiles(width), tiles(width), tiles(model)),
        input_output_aliases={5: 3} if extra else {},
        compiler_params=pltpu.CompilerParams(vmem_limit_bytes=24 << 20),
        cost_estimate=LIGHT,
        name="feed_forward",
    )(x, *[w for w, _ in pieces], *extra)


def feed_backward_kernel(places, has_sum, last, *refs):
    count = len(places) // 4
    refs = list(refs)
    take = lambda n: [refs.pop(0) for _ in range(n)]
    x_ref, g_ref = take(2)
    silu_hbm, slope_hbm, hidden_hbm, weight_hbm = take(count), take(count), take(count), take(4 * count)
    sum_ref = take(1)[0] if has_sum else None
    dx_ref, dx_other_ref = take(2) if last else take(1) * 2
    out_hbm = take(4 * count)
    xt_ref, gt_ref, kept_ref, hidden_ref, gu_ref, down_ref, acc_ref, out_ref, act_sem, weight_sem, out_sem = refs
    _, _, block, width = weight_hbm[0].shape
    rows_all = x_ref.shape[0]
    half = rows_all // 2
    copies_of, late_copies = [], []
    for p in range(count):
        copies = []
        for n, source in enumerate((slope_hbm[p], silu_hbm[p])):
            copies.append(pltpu.make_async_copy(source, kept_ref.at[p, :, pl.ds(n * width, width)], act_sem.at[p, n]))
        for r in range(4):
            features = pl.ds(r * block, block)
            source = weight_hbm[p * 4 + r].at[places[p * 4 + r]]
            for n, target in enumerate((gu_ref.at[p, features, pl.ds(0, width)], gu_ref.at[p, features, pl.ds(width, width)], down_ref.at[p, features, :])):
                copies.append(pltpu.make_async_copy(source.at[n], target, weight_sem.at[p, r, n]))
        copies_of.append(copies)
        late_copies.append(pltpu.make_async_copy(hidden_hbm[p], hidden_ref.at[p], act_sem.at[p, 2]))
    for copy in copies_of[0]:
        copy.start()
    for t in range(4):
        rows = slice(t * rows_all // 4, (t + 1) * rows_all // 4)
        xt_ref[:, rows] = jnp.transpose(x_ref[rows, :])
        gt_ref[:, rows] = jnp.transpose(g_ref[rows, :])

    for p in range(count):
        for copy in copies_of[p]:
            copy.wait()
        for copy in copies_of[p + 1] if p < count - 1 else late_copies:
            copy.start()
        for t in range(2):
            rows = slice(t * half, (t + 1) * half)
            grad_hidden = dot_nn(g_ref[rows, :], down_ref[p])
            kept_ref[p, rows, :width] = (grad_hidden * kept_ref[p, rows, :width].astype(F32)).astype(BF)
            kept_ref[p, rows, width:] = (grad_hidden * kept_ref[p, rows, width:].astype(F32)).astype(BF)
            part = dot_nt(kept_ref[p, rows, :], gu_ref[p])
            if p > 0:
                part = acc_ref[rows, :] + part
            elif has_sum:
                part = sum_ref[rows, :] + part
            if p < count - 1:
                acc_ref[rows, :] = part
            elif not last:
                dx_ref[rows, :] = part
            elif t == 0:
                dx_ref[...] = part
            else:
                dx_other_ref[...] = part.astype(BF)

    slots = out_ref.shape[0]
    copies = []
    for p in range(count):
        late_copies[p].wait()
        for r in range(3, -1, -1):
            features = slice(r * block, (r + 1) * block)
            slot = len(copies) % slots
            if len(copies) >= slots:
                copies[len(copies) - slots].wait()
            gu = dot_nn(xt_ref[features, :], kept_ref[p]).astype(BF)
            out_ref[slot, 0] = gu[:, :width]
            out_ref[slot, 1] = gu[:, width:]
            out_ref[slot, 2] = dot_nn(gt_ref[features, :], hidden_ref[p]).astype(BF)
            copies.append(pltpu.make_async_copy(out_ref.at[slot], out_hbm[p * 4 + r], out_sem.at[slot]))
            copies[-1].start()
    for copy in copies[-slots:]:
        copy.wait()


def feed_backward(x, g, silus, slopes, hiddens, pieces, total, last):
    count = len(pieces)
    extra = [] if total is None else [total]
    rows, model = x.shape
    _, _, block, width = pieces[0][0][0].shape
    places = [n for piece in pieces for _, n in piece]
    vmem = pl.BlockSpec(memory_space=pltpu.VMEM)
    hbm = pl.BlockSpec(memory_space=pl.ANY)
    outs = pl.pallas_call(
        lambda *refs: feed_backward_kernel(places, total is not None, last, *refs),
        out_shape=(
            (jax.ShapeDtypeStruct((rows // 2, model), F32), jax.ShapeDtypeStruct((rows // 2, model), BF))
            if last
            else (jax.ShapeDtypeStruct((rows, model), F32),)
        )
        + tuple(jax.ShapeDtypeStruct((3, block, width), BF) for _ in range(4 * count)),
        in_specs=[vmem] * 2 + [hbm] * (7 * count) + [vmem] * len(extra),
        out_specs=((vmem, vmem) if last else (vmem,)) + (hbm,) * (4 * count),
        scratch_shapes=[
            pltpu.VMEM((model, rows), BF),
            pltpu.VMEM((model, rows), BF),
            pltpu.VMEM((count, rows, 2 * width), BF),
            pltpu.VMEM((count, rows, width), BF),
            pltpu.VMEM((count, model, 2 * width), BF),
            pltpu.VMEM((count, model, width), BF),
            pltpu.VMEM((rows, model), F32),
            pltpu.VMEM((3, 3, block, width), BF),
            pltpu.SemaphoreType.DMA((count, 3)),
            pltpu.SemaphoreType.DMA((count, 4, 3)),
            pltpu.SemaphoreType.DMA((3,)),
        ],
        compiler_params=pltpu.CompilerParams(vmem_limit_bytes=60 << 20),
        cost_estimate=LIGHT,
        name="feed_backward",
    )(x, g, *silus, *slopes, *hiddens, *[w for piece in pieces for w, _ in piece], *extra)
    first = 2 if last else 1
    return outs[:first], [outs[first + 4 * p : first + 4 + 4 * p] for p in range(count)]


class Order:
    def __init__(self):
        self.last = ()

    def event(self, *values):
        out = lax.optimization_barrier((*values, *self.last))[: len(values)]
        self.last = out
        return out


def on_square(inputs, teacher, lengths, w_qkv, w_out_t, w_gate_up, w_down_t, gains):
    chunk, model = inputs.shape
    slot = chunk * 4
    total_rows = slot * 8
    dp = lax.axis_index("dp")
    z = lax.axis_index("tensor")
    core = dp % 2
    first = core == 0
    odd_x = (dp // 2) % 2 == 1
    odd_y = dp // 4 == 1
    inner = jnp.where((z == 1) | (z == 2), 1, 0)
    moves = (core == 1) == (z < 2)
    chunk_low, chunk_high = inner, 3 - inner
    length = lax.dynamic_index_in_dim(lengths, (dp // 2) * 2 + z // 2, 0, keepdims=False)
    count = jnp.sum(lengths).astype(F32)
    places = jnp.stack([chunk_low, chunk_high, 1 - chunk_low, 2 + inner]) * chunk
    counts = jnp.clip(length - places, 0, chunk)
    outer = 1 - inner
    low_row, high_row = core * chunk, (1 - core) * chunk
    low_partner, high_partner = low_row + 2 * chunk, high_row + 2 * chunk
    scalars = jnp.stack(
        [
            low_row,
            high_row,
            low_partner,
            jnp.where(outer == 1, high_row, low_row),
            jnp.where(outer == 1, high_partner, low_partner),
            counts[0],
            counts[1],
            counts[2],
            jnp.where(outer == 1, counts[3], counts[2]),
        ]
    ).astype(jnp.int32)

    def turn(value):
        a, b, c, d = jnp.split(value, 4, axis=-1)
        a, b, c, d = jnp.where(odd_x, b, a), jnp.where(odd_x, a, b), jnp.where(odd_x, d, c), jnp.where(odd_x, c, d)
        return jnp.concatenate([jnp.where(odd_y, c, a), jnp.where(odd_y, d, b), jnp.where(odd_y, a, c), jnp.where(odd_y, b, d)], axis=-1)

    def sort_cores(own, other, axis):
        return jnp.where(first, jnp.concatenate([own, other], axis=axis), jnp.concatenate([other, own], axis=axis))

    def pick(pair):
        return jnp.where(first, pair[0], pair[1]), jnp.where(first, pair[1], pair[0])

    def join_rows(partial):
        return partial[:chunk] + core_swap(partial[chunk:].astype(BF)).astype(F32)

    def core_piece(stacked):
        keep, give = pick(jnp.split(stacked, 2, axis=2))
        return sort_cores(keep, core_swap(give), 1)

    def matmul(a, b):
        return jnp.einsum("ab,bc->ac", a, b, preferred_element_type=F32)

    def matmul_nt(a, b):
        return jnp.einsum("ab,cb->ac", a, b, preferred_element_type=F32)

    def matmul_tn(a, b):
        return jnp.einsum("ba,bc->ac", a, b, preferred_element_type=F32)

    order = Order()
    event = order.event

    attention_piece = core_piece(jnp.concatenate([jnp.swapaxes(w_qkv, 0, 1), w_out_t[None]], axis=0))
    attention_piece = jnp.concatenate([attention_piece[n] for n in range(4)], axis=1)
    feed_piece = core_piece(jnp.concatenate([jnp.swapaxes(w_gate_up, 0, 1), w_down_t[None]], axis=0))
    feed_p, feed_x, feed_y, feed_d = [None] * 4, [None] * 4, [None] * 4, [None] * 4
    (gains_pair,) = event(sort_cores(gains, core_swap(gains), 0))
    gains_x, gains_y, gains_d = x_swap(gains_pair), y_swap(gains_pair), square_swap(gains_pair)
    inputs_rel = turn(inputs)
    gains_x, gains_y, gains_d, attention_piece, feed_p[0] = event(gains_x, gains_y, gains_d, attention_piece, feed_piece)
    gains_all = jnp.concatenate([gains_pair, gains_x, gains_y, gains_d], axis=0)

    own_rows, partner_rows = home_swap(inputs_rel), shift(inputs_rel, partner_of_home)
    att_1, att_2 = z_swap(attention_piece, 1), z_swap(attention_piece, 2)
    att_1, feed_piece = event(att_1, feed_p[0])
    att_low = jnp.stack([attention_piece, att_1])
    att_low_x, att_low_y = x_swap(att_low), y_swap(att_low)
    (att_2,) = event(att_2)
    (att_3,) = event(z_swap(att_2, 1))
    att_high = jnp.stack([att_2, att_3])
    att_high_x, att_high_y = x_swap(att_high), y_swap(att_high)
    (att_low_x,) = event(att_low_x)
    att_low_d = y_swap(att_low_x)
    (att_high_y,) = event(att_high_y)
    att_high_d = x_swap(att_high_y)
    (own_rows,) = event(own_rows)
    other_rows = core_swap(own_rows)
    partner_rows, feed_piece = event(partner_rows, feed_piece)
    other_partner = core_swap(partner_rows)
    feed_x[0], feed_y[0] = x_swap(feed_piece), y_swap(feed_piece)
    feed_p[1] = z_swap(feed_piece, 1)
    att_low_y, att_high_x, att_low_d, att_high_d = event(att_low_y, att_high_x, att_low_d, att_high_d)
    other_rows, other_partner, feed_piece = event(other_rows, other_partner, feed_piece)
    feed_p[2] = z_swap(feed_piece, 2)
    rows = own_rows.astype(F32)
    gain_one = gains_all[:, 0].astype(F32)
    gain_two = gains_all[:, 1].astype(F32)

    normed_all, queries, keys_all, values_all, w_queries, w_keys, w_values, w_out = project(
        (own_rows, other_rows, partner_rows, other_partner), gain_one[None], [att_low, att_low_x, att_low_y, att_low_d, att_high, att_high_x, att_high_y, att_high_d]
    )
    normed_own = normed_all[: 2 * chunk]
    outer_only = (1 - inner)[None].astype(jnp.int32)
    parts = [None] * 4

    def attend(n):
        return attend_forward(outer_only, scalars, queries, keys_all, values_all, n, 1)

    queries, feed_x[0], feed_y[0] = event(queries, feed_x[0], feed_y[0])
    feed_d[0] = y_swap(feed_x[0])
    parts[0] = attend(0)
    queries, feed_p[1], _ = event(queries, feed_p[1], parts[0][0])
    feed_x[1], feed_y[1] = x_swap(feed_p[1]), y_swap(feed_p[1])
    parts[1] = attend(1)
    queries, feed_d[0], feed_p[2], _ = event(queries, feed_d[0], feed_p[2], parts[1][0])
    feed_y[2] = y_swap(feed_p[2])
    feed_p[3] = z_swap(feed_p[2], 1)
    parts[2] = attend(2)
    queries, feed_x[1], feed_y[1], _ = event(queries, feed_x[1], feed_y[1], parts[2][0])
    batch_x = x_swap(jnp.stack([feed_y[1], feed_p[2]]))
    parts[3] = attend(3)
    mixed = jnp.concatenate([p[0] for p in parts], axis=1)
    branch = matmul_nt(mixed, w_out)
    branch_own, branch_other, feed_p[3], feed_y[2], teacher = event(
        branch[:chunk], branch[chunk:].astype(BF), feed_p[3], feed_y[2], teacher
    )
    feed_y[3] = y_swap(feed_p[3])
    branch_other, batch_x, feed_y[3] = event(core_swap(branch_other), batch_x, feed_y[3])
    batch_x3, x_2 = event(jnp.stack([feed_p[3], feed_y[3]]), batch_x[1])
    batch_x3 = x_swap(batch_x3)
    feed_d[2] = y_swap(x_2)
    teacher_rel = turn(teacher)
    middle = rows + branch_own + branch_other.astype(F32)

    scaled_two, inverse_two = norm_forward(middle)
    normed_two = (scaled_two * gain_two).astype(BF)
    normed_two_all = jnp.concatenate([normed_two, core_swap_halves(normed_two)], axis=0)
    silus, slopes, hiddens, feed = [None] * 4, [None] * 4, [None] * 4, None
    pieces = [
        [alone(feed_p[0]), alone(feed_x[0]), alone(feed_y[0]), alone(feed_d[0])],
        [alone(feed_p[1]), alone(feed_x[1]), alone(feed_y[1]), (batch_x, 0)],
    ]
    for k in range(4):
        if k == 2:
            feed, feed_d[2], teacher_rel = event(feed, feed_d[2], teacher_rel)
            teacher_rows = moved_home(teacher_rel)
            pieces.append([alone(feed_p[2]), (batch_x, 1), alone(feed_y[2]), alone(feed_d[2])])
        if k == 3:
            feed, batch_x3 = event(feed, batch_x3)
            pieces.append([alone(feed_p[3]), (batch_x3, 0), alone(feed_y[3]), (batch_x3, 1)])
        silus[k], slopes[k], hiddens[k], feed = feed_forward(normed_two_all, pieces[k], feed)
    feed_own, feed_other, teacher_rows = event(feed[:chunk], feed[chunk:].astype(BF), teacher_rows)
    final = middle + feed_own + core_swap(feed_other).astype(F32)

    own_place = jnp.where(first, chunk_low, chunk_high) * chunk
    valid = (own_place + jnp.arange(chunk, dtype=jnp.int32) < length)[:, None]
    teacher_rows = jnp.where(moves, teacher_rows, teacher_rel)
    grad_final = jnp.where(valid, final - teacher_rows.astype(F32), 0.0) * (total_rows / count)
    grad_feed = grad_final.astype(BF)
    grad_feed_all, output = event(jnp.concatenate([grad_feed, core_swap(grad_feed)], axis=0), turn(final.astype(BF)))
    output_rel = output
    output = moved_home(output)

    def add(a, b):
        return (a.astype(F32) + b.astype(F32)).astype(BF)

    def total_of(own, x, y):
        return own.astype(F32) + x.astype(F32) + y.astype(F32)

    def feed_back(k, total):
        pair = slice(k, k + 2)
        return feed_backward(normed_two_all, grad_feed_all, silus[pair], slopes[pair], hiddens[pair], pieces[pair], total, k == 0)

    (grad_x,), ((own_2, x_2, y_2, d_2), (own_3, x_3, y_3, d_3)) = feed_back(2, None)
    grad_x, d_2, d_3 = event(grad_x, d_2, d_3)
    d_2, d_3 = y_swap(d_2), x_swap(d_3)
    (grad_x, grad_x_other), ((own_0, x_0, y_0, d_0), (own_1, x_1, y_1, d_1)) = feed_back(0, grad_x)
    grad_x, grad_x_other, output, d_2, d_3, d_0, d_1, y_2, x_3 = event(grad_x, grad_x_other, output, d_2, d_3, d_0, d_1, y_2, x_3)
    grad_x_other, batch_x, batch_y = event(grad_x_other, jnp.stack([add(x_2, d_2), x_3]), jnp.stack([y_2, add(y_3, d_3)]))
    batch_x, batch_y = x_swap(batch_x), y_swap(batch_y)
    tile = chunk // 2
    first_rows, second_rows = core_swap(grad_x_other[:tile]), core_swap(grad_x_other[tile:])
    grad_middle, grad_branch, grad_gain_two = norm_grads(grad_x, first_rows, second_rows, middle, grad_final, gain_two)
    grad_gain_two = grad_gain_two[0]
    grad_branch_both = jnp.concatenate([grad_branch, core_swap_halves(grad_branch)], axis=0)
    grad_mixed = matmul(grad_branch_both, w_out).astype(BF)
    half_width = mixed.shape[1] // 2

    def attend_back(n):
        lse = jnp.concatenate([parts[2 * n][1], parts[2 * n + 1][1]], axis=0)
        return attend_backward(scalars, queries, keys_all, values_all, mixed[:, n * half_width : (n + 1) * half_width], grad_mixed, lse, 2 * n)

    gq_a, gk_a, gv_a = attend_back(0)
    gq_a, grad_mixed, d_0, d_1 = event(gq_a, grad_mixed, d_0, d_1)
    d_0, d_1 = y_swap(d_0), x_swap(d_1)
    gq_b, gk_b, gv_b = attend_back(1)

    gq_b, batch_x, batch_y, d_0, d_1, x_1, y_0 = event(gq_b, batch_x, batch_y, d_0, d_1, x_1, y_0)
    grad_queries, batch_x, batch_y, part_3, part_2, gk_b, gv_b = event(
        jnp.concatenate([gq_a, gq_b], axis=1),
        jnp.stack([add(x_0, d_0), x_1]),
        jnp.stack([y_0, add(y_1, d_1)]),
        total_of(own_3, batch_x[1], batch_y[1]).astype(BF),
        total_of(own_2, batch_x[0], batch_y[0]).astype(BF),
        gk_b,
        gv_b,
    )
    batch_x, batch_y, part_3 = x_swap(batch_x), y_swap(batch_y), z_swap(part_3, 1)
    grad_keys = jnp.concatenate([gk_a, gk_b], axis=1)
    grad_values = jnp.concatenate([gv_a, gv_b], axis=1)
    part_own, part_other, partner_part, other_partner_part = rows_grads(grad_queries, grad_keys, grad_values, w_queries, w_keys, w_values)
    part_other, other_partner_part, grad_queries = event(core_swap(part_other), core_swap(other_partner_part), grad_queries)
    (from_partner,) = event((partner_part + other_partner_part.astype(F32)).astype(BF))
    from_partner = z_swap(from_partner, 1)
    (own_e, x_e, y_e, d_e), (own_o, x_o, y_o, d_o) = attention_grads(normed_all, grad_branch_both, grad_queries, grad_keys, grad_values, mixed)
    quarter_cols = grad_queries.shape[1] // 4
    half_cols = 4 * quarter_cols
    d_e, d_o, x_e, y_e, x_o, y_o, part_3, part_2 = event(d_e, d_o, x_e, y_e, x_o, y_o, part_3, part_2)
    (part_2,) = event(add(part_2, part_3))
    part_2 = z_swap(part_2, 2)
    batch_x, batch_y, d_e, d_o = event(batch_x, batch_y, d_e, d_o)
    d_e, d_o = y_swap(d_e), x_swap(d_o)
    (part_1,) = event(total_of(own_1, batch_x[1], batch_y[1]).astype(BF))
    part_1 = z_swap(part_1, 1)
    part_0 = total_of(own_0, batch_x[0], batch_y[0])
    (from_partner,) = event(from_partner)
    _, grad_rows, grad_gain_one = norm_grads(part_own, part_other, from_partner, own_rows, grad_middle, gain_one)
    grad_rows, gain_a, gain_b, part_2 = event(grad_rows, grad_gain_one[0], grad_gain_two, part_2)
    grad_rows = turn(grad_rows)
    grad_inputs = moved_home(grad_rows)
    d_e, d_o = event(d_e, d_o)
    batch_x, batch_y = event(jnp.stack([add(x_e, d_e), x_o]), jnp.stack([y_e, add(y_o, d_o)]))
    batch_x, batch_y = x_swap(batch_x), y_swap(batch_y)
    part_1, part_2, part_0 = event(part_1, part_2, part_0)
    feed_total = part_0 + part_1.astype(F32) + part_2.astype(F32)
    feed_keep, feed_give = pick(jnp.split(feed_total, 2, axis=1))
    feed_give = core_swap(feed_give.astype(BF))

    quarter = model // 4
    a, b, c, d = jnp.split(jnp.stack([gain_a, gain_b], axis=0), 4, axis=1)
    sent = x_swap(jnp.concatenate([b, d], axis=1))

    batch_x, batch_y, sent = event(batch_x, batch_y, sent)
    even, odd = total_of(own_e, batch_x[0], batch_y[0]), total_of(own_o, batch_x[1], batch_y[1])
    att_3, att_1, att_2 = odd[:, half_cols:].astype(BF), even[:, half_cols:].astype(BF), odd[:, :half_cols].astype(BF)
    att_3, att_1, a, c, sent = event(att_3, att_1, a, c, sent)
    att_3, att_1 = z_swap(att_3, 1), z_swap(att_1, 1)
    a, c = a + sent[:, :quarter], c + sent[:, quarter:]
    sent = y_swap(c)
    att_3, att_2, sent = event(att_3, att_2, sent)
    att_2 = z_swap(add(att_2, att_3), 2)
    a = a + sent
    keep, give = pick(jnp.split(a, 2, axis=1))
    sent = core_swap(give)
    feed_give, sent = event(feed_give, sent)
    a = keep + sent
    size = a.shape[1] // 4
    total = lax.dynamic_slice_in_dim(a, z * size, size, 1)
    for k in range(1, 4):
        total = total + z_swap(lax.dynamic_slice_in_dim(a, (z ^ k) * size, size, 1), k)
    grad_gains = jnp.swapaxes(total, 0, 1)
    grad_inputs = jnp.where(moves, grad_inputs, grad_rows).astype(F32)
    output = jnp.where(moves, output, output_rel)
    feed_out = sort_cores(feed_keep, feed_give.astype(F32), 2)
    attention_total = even[:, :half_cols] + att_1.astype(F32) + att_2.astype(F32)
    attention_total = jnp.stack([attention_total[:, n * quarter_cols : (n + 1) * quarter_cols] for n in range(4)])

    def to_home(total):
        keep, give = pick(jnp.split(total, 2, axis=1))
        return sort_cores(keep, core_swap(give.astype(BF)).astype(F32), 2)

    attention_out = to_home(attention_total)

    return (
        output,
        grad_inputs,
        jnp.swapaxes(attention_out[:3], 0, 1),
        attention_out[3],
        jnp.swapaxes(feed_out[:2], 0, 1),
        feed_out[2],
        grad_gains,
    )


def solution(mesh):
    square = dict(mesh.shape) == {"dp": 8, "tensor": 4}
    return jax.shard_map(
        on_square if square else on_device,
        mesh=mesh,
        in_specs=(
            P(("dp", "tensor"), None),
            P(("dp", "tensor"), None),
            P(),
            P("dp", None, "tensor"),
            P("dp", "tensor"),
            P("dp", None, "tensor"),
            P("dp", "tensor"),
            P("dp", None),
        ),
        out_specs=(
            P(("dp", "tensor"), None),
            P(("dp", "tensor"), None),
            P("dp", None, "tensor"),
            P("dp", "tensor"),
            P("dp", None, "tensor"),
            P("dp", "tensor"),
            P(("dp", "tensor"), None),
        ),
        check_vma=False,
    )
```

```python
import math

import jax
import jax.numpy as jnp
from jax import lax
from jax.experimental import pallas as pl
from jax.experimental.pallas import tpu as pltpu
from jax.sharding import PartitionSpec as P

HEAD = 64


negative = -1e30


def norm_forward(values):
    inverse = lax.rsqrt(jnp.mean(values * values, axis=-1, keepdims=True) + 1e-05)
    return (values * inverse, inverse)


def norm_backward(grad_normed, scaled, inverse, gain):
    grad_scaled = grad_normed * gain
    grad_values = inverse * (
        grad_scaled - scaled * jnp.mean(grad_scaled * scaled, axis=-1, keepdims=True)
    )
    return (grad_values, jnp.sum(grad_normed * scaled, axis=0))


def key_limit(query_index):
    return query_index + 1


def score_block(query_block, keys_all, query_start, key_start, length):
    block = query_block.shape[0]
    key_block = lax.dynamic_slice_in_dim(keys_all, key_start, block, 0)
    scores = jnp.einsum("qhe,khe->hqk", query_block, key_block, preferred_element_type=jnp.float32)
    query_pos = query_start + jnp.arange(block, dtype=jnp.int32)
    key_pos = key_start + jnp.arange(block, dtype=jnp.int32)
    allowed = (key_pos[None, :] <= query_pos[:, None]) & (key_pos[None, :] < length)
    return jnp.where(allowed[None], scores, negative)


def attention_forward(queries, keys_all, values_all, length):
    slot, heads, head = queries.shape
    block = min(512, slot)
    block_count = slot // block

    def query_step(index, carry):
        mixed, maxima, totals = carry
        query_start = index * block
        query_block = lax.dynamic_slice_in_dim(queries, query_start, block, 0)
        upper = key_limit(index)

        def stats_step(inner, state):
            maximum, total = state
            scores = score_block(query_block, keys_all, query_start, inner * block, length)
            larger = jnp.maximum(maximum, jnp.max(scores, axis=-1))
            total = total * jnp.exp(maximum - larger) + jnp.sum(
                jnp.exp(scores - larger[..., None]), axis=-1
            )
            return (larger, total)

        start_state = (
            jnp.full((heads, block), negative, jnp.float32),
            jnp.zeros((heads, block), jnp.float32),
        )
        maximum, total = lax.fori_loop(0, upper, stats_step, start_state)

        def mix_step(inner, accum):
            key_start = inner * block
            scores = score_block(query_block, keys_all, query_start, key_start, length)
            weights = (jnp.exp(scores - maximum[..., None]) / total[..., None]).astype(jnp.bfloat16)
            value_block = lax.dynamic_slice_in_dim(values_all, key_start, block, 0)
            return accum + jnp.einsum(
                "hqk,khe->qhe", weights, value_block, preferred_element_type=jnp.float32
            )

        accum = lax.fori_loop(0, upper, mix_step, jnp.zeros((block, heads, head), jnp.float32))
        mixed = lax.dynamic_update_slice_in_dim(mixed, accum, query_start, 0)
        maxima = lax.dynamic_update_index_in_dim(maxima, maximum, index, 0)
        totals = lax.dynamic_update_index_in_dim(totals, total, index, 0)
        return (mixed, maxima, totals)

    start = (
        jnp.zeros((slot, heads, head), jnp.float32),
        jnp.zeros((block_count, heads, block), jnp.float32),
        jnp.zeros((block_count, heads, block), jnp.float32),
    )
    return lax.fori_loop(0, block_count, query_step, start)


def attention_backward(queries, keys_all, values_all, grad_mixed, maxima, totals, length):
    slot, heads, head = queries.shape
    block = min(512, slot)
    block_count = slot // block

    def query_step(index, carry):
        grad_queries, grad_keys, grad_values = carry
        query_start = index * block
        query_block = lax.dynamic_slice_in_dim(queries, query_start, block, 0)
        grad_block = lax.dynamic_slice_in_dim(grad_mixed, query_start, block, 0)
        maximum = lax.dynamic_index_in_dim(maxima, index, 0, keepdims=False)
        total = lax.dynamic_index_in_dim(totals, index, 0, keepdims=False)
        upper = key_limit(index)

        def probs_of(inner):
            key_start = inner * block
            scores = score_block(query_block, keys_all, query_start, key_start, length)
            probs = jnp.exp(scores - maximum[..., None]) / total[..., None]
            value_block = lax.dynamic_slice_in_dim(values_all, key_start, block, 0)
            grad_probs = jnp.einsum(
                "qhe,khe->hqk", grad_block, value_block, preferred_element_type=jnp.float32
            )
            return (probs, grad_probs, key_start)

        def delta_step(inner, delta):
            probs, grad_probs, key_start = probs_of(inner)
            return delta + jnp.sum(probs * grad_probs, axis=-1)

        delta = lax.fori_loop(0, upper, delta_step, jnp.zeros((heads, block), jnp.float32))

        def grad_step(inner, state):
            grad_query, grad_keys, grad_values = state
            probs, grad_probs, key_start = probs_of(inner)
            grad_scores = (probs * (grad_probs - delta[..., None])).astype(jnp.bfloat16)
            key_block = lax.dynamic_slice_in_dim(keys_all, key_start, block, 0)
            grad_query = grad_query + jnp.einsum(
                "hqk,khe->qhe", grad_scores, key_block, preferred_element_type=jnp.float32
            )
            key_part = jnp.einsum(
                "hqk,qhe->khe", grad_scores, query_block, preferred_element_type=jnp.float32
            )
            value_part = jnp.einsum(
                "hqk,qhe->khe",
                probs.astype(jnp.bfloat16),
                grad_block,
                preferred_element_type=jnp.float32,
            )
            old_keys = lax.dynamic_slice_in_dim(grad_keys, key_start, block, 0)
            old_values = lax.dynamic_slice_in_dim(grad_values, key_start, block, 0)
            grad_keys = lax.dynamic_update_slice_in_dim(
                grad_keys, old_keys + key_part, key_start, 0
            )
            grad_values = lax.dynamic_update_slice_in_dim(
                grad_values, old_values + value_part, key_start, 0
            )
            return (grad_query, grad_keys, grad_values)

        start_state = (jnp.zeros((block, heads, head), jnp.float32), grad_keys, grad_values)
        grad_query, grad_keys, grad_values = lax.fori_loop(0, upper, grad_step, start_state)
        grad_queries = lax.dynamic_update_slice_in_dim(grad_queries, grad_query, query_start, 0)
        return (grad_queries, grad_keys, grad_values)

    empty = jnp.zeros((slot, heads, head), jnp.float32)
    return lax.fori_loop(0, block_count, query_step, (empty, empty, empty))


def on_device(inputs, teacher, lengths, w_qkv, w_out_t, w_gate_up, w_down_t, gains):
    own_rows = inputs.shape[0]
    slot = own_rows * lax.axis_size("tensor")
    total_rows = slot * lax.axis_size("dp")
    local_width = w_qkv.shape[2]
    local_heads = local_width // HEAD
    scale = 1.0 / math.sqrt(HEAD)
    length = lax.dynamic_index_in_dim(lengths, lax.axis_index("dp"), 0, keepdims=False)
    count = jnp.sum(lengths).astype(jnp.float32)
    own_start = lax.axis_index("tensor") * own_rows
    row_pos = own_start + jnp.arange(own_rows, dtype=jnp.int32)
    valid = (row_pos < length)[:, None]
    qkv_all, out_all, gains_all = (
        lax.all_gather(w_qkv, "dp", axis=0, tiled=True),
        lax.all_gather(w_out_t, "dp", axis=0, tiled=True),
        lax.all_gather(gains, "dp", axis=0, tiled=True),
    )
    gate_up_all, down_all = (
        lax.all_gather(w_gate_up, "dp", axis=0, tiled=True),
        lax.all_gather(w_down_t, "dp", axis=0, tiled=True),
    )
    gain_one = gains_all[:, 0].astype(jnp.float32)
    gain_two = gains_all[:, 1].astype(jnp.float32)
    rows = inputs.astype(jnp.float32)
    scaled_one, inverse_one = norm_forward(rows)
    normed_one = (scaled_one * gain_one).astype(jnp.bfloat16)
    gathered_one = lax.all_gather(normed_one, "tensor", axis=0, tiled=True)
    qkv = jnp.einsum("rd,dcf->rcf", gathered_one, qkv_all, preferred_element_type=jnp.float32)
    queries = (qkv[:, 0] * scale).astype(jnp.bfloat16).reshape(slot, local_heads, HEAD)
    keys_all = qkv[:, 1].astype(jnp.bfloat16).reshape(slot, local_heads, HEAD)
    values_all = qkv[:, 2].astype(jnp.bfloat16).reshape(slot, local_heads, HEAD)
    mixed, maxima, totals = attention_forward(queries, keys_all, values_all, length)
    mixed = mixed.reshape(slot, local_width).astype(jnp.bfloat16)
    piece = mixed
    middle = rows + lax.psum_scatter(
        jnp.einsum("rk,dk->rd", piece, out_all, preferred_element_type=jnp.float32).astype(
            jnp.bfloat16
        ),
        "tensor",
        scatter_dimension=0,
        tiled=True,
    ).astype(jnp.float32)
    scaled_two, inverse_two = norm_forward(middle)
    normed_two = (scaled_two * gain_two).astype(jnp.bfloat16)
    gathered_two = lax.all_gather(normed_two, "tensor", axis=0, tiled=True)
    rows_two = None
    gate_up = jnp.einsum(
        "rd,dcf->rcf", gathered_two, gate_up_all, preferred_element_type=jnp.float32
    )
    gate = gate_up[:, 0]
    upper = gate_up[:, 1]
    sigmoid = jax.nn.sigmoid(gate)
    hidden = (gate * sigmoid * upper).astype(jnp.bfloat16)
    piece = hidden
    final = middle + lax.psum_scatter(
        jnp.einsum("rf,df->rd", piece, down_all, preferred_element_type=jnp.float32).astype(
            jnp.bfloat16
        ),
        "tensor",
        scatter_dimension=0,
        tiled=True,
    ).astype(jnp.float32)
    output = final.astype(jnp.bfloat16)
    grad_final = jnp.where(valid, final - teacher.astype(jnp.float32), 0.0) * (total_rows / count)
    grad_feed = lax.all_gather(grad_final.astype(jnp.bfloat16), "tensor", axis=0, tiled=True)
    grad_down = jnp.einsum("rd,rf->df", grad_feed, hidden, preferred_element_type=jnp.float32)
    grad_hidden = jnp.einsum("rd,df->rf", grad_feed, down_all, preferred_element_type=jnp.float32)
    grad_gate = grad_hidden * upper * (sigmoid * (1.0 + gate * (1.0 - sigmoid)))
    grad_upper = grad_hidden * (gate * sigmoid)
    grad_gu = jnp.stack([grad_gate, grad_upper], axis=1).astype(jnp.bfloat16)
    rows_two = lax.all_gather(normed_two, "tensor", axis=0, tiled=True)
    grad_gate_up = jnp.einsum("rd,rcf->dcf", rows_two, grad_gu, preferred_element_type=jnp.float32)
    piece = grad_gu
    grad_normed_two = lax.psum_scatter(
        jnp.einsum("rcf,dcf->rd", piece, gate_up_all, preferred_element_type=jnp.float32).astype(
            jnp.bfloat16
        ),
        "tensor",
        scatter_dimension=0,
        tiled=True,
    ).astype(jnp.float32)
    grad_norm_two, grad_gain_two = norm_backward(grad_normed_two, scaled_two, inverse_two, gain_two)
    grad_middle = grad_final + grad_norm_two
    grad_branch = lax.all_gather(grad_middle.astype(jnp.bfloat16), "tensor", axis=0, tiled=True)
    grad_out = jnp.einsum("rd,rk->dk", grad_branch, mixed, preferred_element_type=jnp.float32)
    grad_mixed = jnp.einsum("rd,dk->rk", grad_branch, out_all, preferred_element_type=jnp.float32)
    grad_mixed = grad_mixed.astype(jnp.bfloat16).reshape(slot, local_heads, HEAD)
    grad_queries, grad_keys, grad_values = attention_backward(
        queries, keys_all, values_all, grad_mixed, maxima, totals, length
    )
    grad_rows_qkv = jnp.stack(
        [
            grad_queries.reshape(slot, local_width).astype(jnp.bfloat16) * scale,
            grad_keys.reshape(slot, local_width).astype(jnp.bfloat16),
            grad_values.reshape(slot, local_width).astype(jnp.bfloat16),
        ],
        axis=1,
    )
    rows_one = lax.all_gather(normed_one, "tensor", axis=0, tiled=True)
    grad_qkv = jnp.einsum(
        "rd,rcf->dcf", rows_one, grad_rows_qkv, preferred_element_type=jnp.float32
    )
    piece = grad_rows_qkv
    grad_normed_one = lax.psum_scatter(
        jnp.einsum("rcf,dcf->rd", piece, qkv_all, preferred_element_type=jnp.float32).astype(
            jnp.bfloat16
        ),
        "tensor",
        scatter_dimension=0,
        tiled=True,
    ).astype(jnp.float32)
    grad_norm_one, grad_gain_one = norm_backward(grad_normed_one, scaled_one, inverse_one, gain_one)
    grad_inputs = grad_middle + grad_norm_one
    grad_qkv, grad_out, grad_gate_up, grad_down = (
        lax.psum_scatter(
            grad_qkv.astype(jnp.bfloat16), "dp", scatter_dimension=0, tiled=True
        ).astype(jnp.float32),
        lax.psum_scatter(
            grad_out.astype(jnp.bfloat16), "dp", scatter_dimension=0, tiled=True
        ).astype(jnp.float32),
        lax.psum_scatter(
            grad_gate_up.astype(jnp.bfloat16), "dp", scatter_dimension=0, tiled=True
        ).astype(jnp.float32),
        lax.psum_scatter(
            grad_down.astype(jnp.bfloat16), "dp", scatter_dimension=0, tiled=True
        ).astype(jnp.float32),
    )
    grad_gains = lax.psum_scatter(
        jnp.stack([grad_gain_one, grad_gain_two], axis=1),
        ("dp", "tensor"),
        scatter_dimension=0,
        tiled=True,
    )
    return (output, grad_inputs, grad_qkv, grad_out, grad_gate_up, grad_down, grad_gains)


BF = jnp.bfloat16
F32 = jnp.float32
AXES = ("dp", "tensor")
LIGHT = pl.CostEstimate(flops=1000, bytes_accessed=1000, transcendentals=0)


def shift(value, where):
    pairs = []
    for y in range(2):
        for x in range(2):
            for c in range(2):
                for z in range(4):
                    to = where(y, x, c, z)
                    if to is not None:
                        ty, tx, tc, tz = to
                        pairs.append((((y * 2 + x) * 2 + c) * 4 + z, ((ty * 2 + tx) * 2 + tc) * 4 + tz))
    return lax.ppermute(value, AXES, pairs)


def core_swap(value):
    return shift(value, lambda y, x, c, z: (y, x, 1 - c, z))


def core_swap_halves(value):
    half = value.shape[0] // 2
    return jnp.concatenate([core_swap(value[:half]), core_swap(value[half:])], axis=0)


def x_swap(value):
    return shift(value, lambda y, x, c, z: (y, 1 - x, c, z))


def y_swap(value):
    return shift(value, lambda y, x, c, z: (1 - y, x, c, z))


def square_swap(value):
    return shift(value, lambda y, x, c, z: (1 - y, 1 - x, c, z))


def z_swap(value, bits):
    return shift(value, lambda y, x, c, z: (y, x, c, z ^ bits))


def home_of(y, x, c, z):
    if (c == 1 and z < 2) or (c == 0 and z >= 2):
        return (y, x, 1 - c, 3 - z)
    return (y, x, c, z)


def home_swap(value):
    return shift(value, home_of)


def moved_home(value):
    return shift(value, lambda *place: None if home_of(*place) == place else home_of(*place))


def partner_of_home(y, x, c, z):
    y, x, c, z = home_of(y, x, c, z)
    z ^= 1
    if c == 1 and z in (1, 2):
        return None
    return (y, x, c, z)


def head_masks(rows):
    lanes = lax.broadcasted_iota(jnp.int32, (rows, 2 * HEAD), 1)
    return (lanes < HEAD, lanes >= HEAD)


def dot_nt(a, b):
    return lax.dot_general(a, b, (((1,), (1,)), ((), ())), preferred_element_type=F32)


def dot_nn(a, b):
    return lax.dot_general(a, b, (((1,), (0,)), ((), ())), preferred_element_type=F32)


def dot_tn(a, b):
    return lax.dot_general(a, b, (((0,), (0,)), ((), ())), preferred_element_type=F32)


def attend_forward_kernel(outer_ref, sc_ref, q_ref, k_ref, v_ref, o_ref, lse_ref):
    chunk = q_ref.shape[0] // 2
    tile = chunk // 2
    lanes = 2 * HEAD
    head = pl.program_id(0) % 2
    low, high, low_partner, extra_row, extra_key = [pl.multiple_of(sc_ref[i], chunk) for i in range(5)]
    mine = lax.broadcasted_iota(jnp.int32, (tile, lanes), 1) // HEAD == head

    def fold(op, parts):
        parts = [p[:, i * lanes : (i + 1) * lanes] for p in parts for i in range(p.shape[1] // lanes)]
        while len(parts) > 1:
            parts = [op(parts[i], parts[i + 1]) if i + 1 < len(parts) else parts[i] for i in range(0, len(parts), 2)]
        return parts[0]

    def unit(row, own, own_count, half, others):
        rows = pl.ds(pl.multiple_of(row + half * tile, tile), tile)
        query = jnp.where(mine, q_ref[rows, :], 0)
        blocks = [(pl.ds(start, chunk), count, chunk, None) for start, count in others]
        blocks.append((pl.ds(own, (half + 1) * tile), own_count, (half + 1) * tile, half * tile))
        scores = []
        for keys, count, width, diagonal in blocks:
            s = dot_nt(query, k_ref[keys, :])
            s = s + jnp.where(lax.broadcasted_iota(jnp.int32, (1, width), 1) < count, 0.0, negative)
            if diagonal is not None:
                cols = lax.broadcasted_iota(jnp.int32, (tile, width), 1)
                s = jnp.where(cols <= lax.broadcasted_iota(jnp.int32, (tile, width), 0) + diagonal, s, negative)
            scores.append(s)
        top = jnp.max(fold(jnp.maximum, scores), axis=1, keepdims=True)
        weights = [jnp.exp(s - top) for s in scores]
        total = jnp.sum(fold(jnp.add, weights), axis=1, keepdims=True)
        mixed = None
        for w, (keys, _, _, _) in zip(weights, blocks):
            part = dot_nn(w.astype(BF), v_ref[keys, :])
            mixed = part if mixed is None else mixed + part
        return rows, mixed / total, top + jnp.log(total)

    def finish(units):
        for rows, mixed, lse in units:
            mixed = mixed.astype(BF)
            o_ref[rows, :] = jnp.where(mine, mixed, o_ref[rows, :])
            lse_ref[0, pl.ds(head, 1), rows] = jnp.transpose(jnp.broadcast_to(lse, (tile, lanes)))[0:1]

    near = [(low, sc_ref[5]), (low_partner, sc_ref[7])]
    extra = [(extra_key, sc_ref[8])]

    @pl.when(outer_ref[0] == 1)
    def _():
        for half in range(2):
            finish([unit(high, high, sc_ref[6], half, near + extra), unit(low, low, sc_ref[5], half, [])])

    @pl.when(outer_ref[0] == 0)
    def _():
        for half in range(2):
            finish([unit(high, high, sc_ref[6], half, near), unit(low, low, sc_ref[5], half, extra)])


def attend_forward(outer, scalars, queries, keys_all, values_all, start, pairs):
    rows = queries.shape[0]
    width = pairs * 2 * HEAD
    slot = keys_all.shape[0]
    own = lambda i, *_: (0, i // 2)
    column = lambda i, *_: (0, i // 2 + start)
    return pl.pallas_call(
        attend_forward_kernel,
        out_shape=(
            jax.ShapeDtypeStruct((rows, width), BF),
            jax.ShapeDtypeStruct((pairs, 8, rows), F32),
        ),
        grid_spec=pltpu.PrefetchScalarGridSpec(
            num_scalar_prefetch=2,
            grid=(2 * pairs,),
            in_specs=[
                pl.BlockSpec((rows, 2 * HEAD), column),
                pl.BlockSpec((slot, 2 * HEAD), column),
                pl.BlockSpec((slot, 2 * HEAD), column),
            ],
            out_specs=(
                pl.BlockSpec((rows, 2 * HEAD), own),
                pl.BlockSpec((1, 8, rows), lambda i, *_: (i // 2, 0, 0)),
            ),
        ),
        compiler_params=pltpu.CompilerParams(vmem_limit_bytes=24 << 20),
        cost_estimate=LIGHT,
        name="attend_forward",
    )(outer, scalars, queries, keys_all, values_all)


def attend_backward_kernel(sc_ref, q_ref, k_ref, v_ref, o_ref, g_ref, lse_ref, dq_ref, dk_ref, dv_ref, dq_acc, dk_acc, dv_acc, delta_ref):
    chunk = q_ref.shape[0] // 2
    tile = chunk // 2
    low, high_row, low_partner, extra_row, extra_key = [pl.multiple_of(sc_ref[i], chunk) for i in range(5)]
    dq_acc[...] = jnp.zeros_like(dq_acc)
    dk_acc[...] = jnp.zeros_like(dk_acc)
    dv_acc[...] = jnp.zeros_like(dv_acc)
    for part in range(4):
        rows = pl.ds(part * tile, tile)
        product = jnp.transpose(o_ref[rows, :].astype(F32) * g_ref[rows, :].astype(F32))
        delta_ref[0:1, rows] = jnp.sum(product[:HEAD], axis=0, keepdims=True)
        delta_ref[1:2, rows] = jnp.sum(product[HEAD:], axis=0, keepdims=True)

    def step(head, row, width, key, count, shift_rows):
        rows = pl.ds(row, width)
        keys = pl.ds(key, tile)
        query = jnp.where(head_masks(width)[head], q_ref[rows, :], 0)
        grad = jnp.where(head_masks(width)[head], g_ref[rows, :], 0)
        key_block = k_ref[keys, :]
        scores = dot_nt(key_block, query)
        index = lax.broadcasted_iota(jnp.int32, (tile, width), 0)
        allowed = index < count
        if shift_rows is not None:
            allowed = allowed & (index <= lax.broadcasted_iota(jnp.int32, (tile, width), 1) + shift_rows)
        probs = jnp.exp(jnp.where(allowed, scores, negative) - lse_ref[0, head : head + 1, rows])
        grad_probs = dot_nt(v_ref[keys, :], grad)
        grad_scores = (probs * (grad_probs - delta_ref[head : head + 1, rows])).astype(BF)
        dv_acc[keys, :] += dot_nn(probs.astype(BF), grad)
        dk_acc[keys, :] += dot_nn(grad_scores, query)
        key_masked = jnp.where(head_masks(tile)[head], key_block, 0)
        dq_acc[rows, :] += dot_tn(grad_scores, key_masked)

    for head in range(2):
        for half in range(2):
            down = half * tile
            add = lambda start: pl.multiple_of(start + down, tile)
            step(head, add(low), chunk - down, add(low), sc_ref[5] - down, 0)
            step(head, add(high_row), chunk - down, add(high_row), sc_ref[6] - down, 0)
            step(head, high_row, chunk, add(low), sc_ref[5] - down, None)
            step(head, high_row, chunk, add(low_partner), sc_ref[7] - down, None)
            step(head, extra_row, chunk, add(extra_key), sc_ref[8] - down, None)
    dq_ref[...] = (dq_acc[...] * (1.0 / math.sqrt(HEAD))).astype(BF)
    dk_ref[...] = dk_acc[...].astype(BF)
    dv_ref[...] = dv_acc[...].astype(BF)


def attend_backward(scalars, queries, keys_all, values_all, mixed, grad_mixed, lse, start):
    rows, width = mixed.shape
    pairs = width // (2 * HEAD)
    slot = keys_all.shape[0]
    own = lambda i, sc: (0, i)
    column = lambda i, sc: (0, i + start)
    own_spec = pl.BlockSpec((rows, 2 * HEAD), own)
    row_spec = pl.BlockSpec((rows, 2 * HEAD), column)
    slot_spec = pl.BlockSpec((slot, 2 * HEAD), column)
    return pl.pallas_call(
        attend_backward_kernel,
        out_shape=(
            jax.ShapeDtypeStruct((rows, width), BF),
            jax.ShapeDtypeStruct((slot, width), BF),
            jax.ShapeDtypeStruct((slot, width), BF),
        ),
        grid_spec=pltpu.PrefetchScalarGridSpec(
            num_scalar_prefetch=1,
            grid=(pairs,),
            in_specs=[row_spec, slot_spec, slot_spec, own_spec, row_spec, pl.BlockSpec((1, 8, rows), lambda i, sc: (i, 0, 0))],
            out_specs=(own_spec, pl.BlockSpec((slot, 2 * HEAD), own), pl.BlockSpec((slot, 2 * HEAD), own)),
            scratch_shapes=[
                pltpu.VMEM((rows, 2 * HEAD), F32),
                pltpu.VMEM((slot, 2 * HEAD), F32),
                pltpu.VMEM((slot, 2 * HEAD), F32),
                pltpu.VMEM((8, rows), F32),
            ],
        ),
        compiler_params=pltpu.CompilerParams(vmem_limit_bytes=32 << 20),
        cost_estimate=LIGHT,
    )(scalars, queries, keys_all, values_all, mixed, grad_mixed, lse)


def project_kernel(*refs):
    rows_refs, gain_ref, weight_refs = refs[:4], refs[4], (refs[5:9], refs[9:13])
    normed_ref, q_ref, k_ref, v_ref, wq_ref, wk_ref, wv_ref, wo_ref = refs[13:]
    step = pl.program_id(0)
    _, block, width = weight_refs[0][0].shape
    part = width // 4
    tile = rows_refs[0].shape[0] // 2

    @pl.when(step == 0)
    def _():
        for k in range(4):
            for r in range(4):
                source = weight_refs[k // 2][r].at[k % 2]
                for n, out in enumerate((wq_ref, wk_ref, wv_ref, wo_ref)):
                    out[r * block : (r + 1) * block, k * part : (k + 1) * part] = source[:, n * part : (n + 1) * part]

    for n in range(4):

        @pl.when(step == n)
        def _():
            for half in range(2):
                rows = slice(half * tile, (half + 1) * tile)
                values = rows_refs[n][rows, :].astype(F32)
                inverse = lax.rsqrt(jnp.mean(values * values, axis=-1, keepdims=True) + 1e-05)
                normed = (values * inverse * gain_ref[...]).astype(BF)
                normed_ref[rows, :] = normed
                k_ref[rows, :] = dot_nn(normed, wk_ref[...]).astype(BF)
                v_ref[rows, :] = dot_nn(normed, wv_ref[...]).astype(BF)
                if n < 2:
                    q_ref[rows, :] = (dot_nn(normed, wq_ref[...]) * (1.0 / math.sqrt(HEAD))).astype(BF)


def project(rows_parts, gain, weights):
    chunk, model = rows_parts[0].shape
    _, block, width = weights[0].shape
    whole = lambda shape: pl.BlockSpec(shape, lambda i: (0,) * len(shape))
    tiles = lambda cols: pl.BlockSpec((chunk, cols), lambda i: (i, 0))
    shape = lambda r, c: jax.ShapeDtypeStruct((r, c), BF)
    return pl.pallas_call(
        project_kernel,
        out_shape=(
            shape(4 * chunk, model),
            shape(2 * chunk, width),
            shape(4 * chunk, width),
            shape(4 * chunk, width),
            shape(model, width),
            shape(model, width),
            shape(model, width),
            shape(model, width),
        ),
        grid=(4,),
        in_specs=[whole((chunk, model))] * 4 + [whole((1, model))] + [whole(w.shape) for w in weights],
        out_specs=(
            tiles(model),
            pl.BlockSpec((chunk, width), lambda i: (jnp.minimum(i, 1), 0)),
            tiles(width),
            tiles(width),
        )
        + tuple(whole((model, width)) for _ in range(4)),
        compiler_params=pltpu.CompilerParams(vmem_limit_bytes=60 << 20),
        cost_estimate=LIGHT,
        name="project",
    )(*rows_parts, gain, *weights)


def rows_grads_kernel(dq_ref, dk_ref, dv_ref, wq_ref, wk_ref, wv_ref, own_ref, other_ref, partner_ref, partner_other_ref):
    step = pl.program_id(0)
    part = dot_nt(dk_ref[...], wk_ref[...]) + dot_nt(dv_ref[...], wv_ref[...])

    @pl.when(step == 0)
    def _():
        own_ref[...] = part + dot_nt(dq_ref[...], wq_ref[...])

    @pl.when(step == 1)
    def _():
        other_ref[...] = (part + dot_nt(dq_ref[...], wq_ref[...])).astype(BF)

    @pl.when(step == 2)
    def _():
        partner_ref[...] = part

    @pl.when(step == 3)
    def _():
        partner_other_ref[...] = part.astype(BF)


def rows_grads(dq, dk, dv, wq, wk, wv):
    slot, width = dk.shape
    model = wq.shape[0]
    chunk = slot // 4
    whole = pl.BlockSpec((model, width), lambda i: (0, 0))
    tiles = pl.BlockSpec((chunk, width), lambda i: (i, 0))
    out = pl.BlockSpec((chunk, model), lambda i: (0, 0))
    shape = lambda t: jax.ShapeDtypeStruct((chunk, model), t)
    return pl.pallas_call(
        rows_grads_kernel,
        out_shape=(shape(F32), shape(BF), shape(F32), shape(BF)),
        grid=(4,),
        in_specs=[pl.BlockSpec((chunk, width), lambda i: (jnp.minimum(i, 1), 0)), tiles, tiles, whole, whole, whole],
        out_specs=(out,) * 4,
        compiler_params=pltpu.CompilerParams(vmem_limit_bytes=40 << 20),
        cost_estimate=LIGHT,
        name="rows_grads",
    )(dq, dk, dv, wq, wk, wv)


def attention_grads_kernel(x_ref, g_ref, dq_ref, dk_ref, dv_ref, mixed_ref, *out_refs):
    rows = g_ref.shape[0]
    x_turned = jnp.transpose(x_ref[...])
    g_turned = jnp.transpose(g_ref[...])
    grads = (
        dot_nn(x_turned[:, :rows], dq_ref[...]),
        dot_nn(x_turned, dk_ref[...]),
        dot_nn(x_turned, dv_ref[...]),
        dot_nn(g_turned, mixed_ref[...]),
    )
    part = dq_ref.shape[1] // 4
    for r in range(4):

        @pl.when(pl.program_id(0) == r)
        def _():
            for k in range(4):
                for n in range(4):
                    start = (k % 2 * 4 + n) * part
                    out_refs[k // 2 * 4 + r][:, start : start + part] = grads[n][:, k * part : (k + 1) * part].astype(BF)


def attention_grads(x, g, dq, dk, dv, mixed):
    rows, model = g.shape
    slot, width = dk.shape
    block = model // 4
    whole = lambda a: pl.BlockSpec(a.shape, lambda i: (0, 0))
    out = pl.pallas_call(
        attention_grads_kernel,
        out_shape=(jax.ShapeDtypeStruct((block, 2 * width), BF),) * 8,
        grid=(4,),
        in_specs=[
            pl.BlockSpec((slot, block), lambda i: (0, i)),
            pl.BlockSpec((rows, block), lambda i: (0, i)),
            whole(dq),
            whole(dk),
            whole(dv),
            whole(mixed),
        ],
        out_specs=(pl.BlockSpec((block, 2 * width), lambda i: (0, 0)),) * 8,
        compiler_params=pltpu.CompilerParams(vmem_limit_bytes=40 << 20),
        cost_estimate=LIGHT,
        name="attention_grads",
    )(x, g, dq, dk, dv, mixed)
    return out[:4], out[4:]


def norm_grads_kernel(halves, part_ref, first_ref, second_ref, values_ref, grad_ref, gain_ref, out_ref, low_ref, gain_grad_ref):
    step = pl.program_id(0)
    values = values_ref[...].astype(F32)
    inverse = lax.rsqrt(jnp.mean(values * values, axis=-1, keepdims=True) + 1e-05)
    scaled = values * inverse

    @pl.when(step == 0)
    def _():
        gain_grad_ref[...] = jnp.zeros_like(gain_grad_ref)

    first, second = first_ref[...].astype(F32), second_ref[...].astype(F32)
    received = jnp.where(step < 2, first, second) if halves else first + second
    grad_normed = part_ref[...] + received
    grad_scaled = grad_normed * gain_ref[...]
    grad = grad_ref[...] + inverse * (grad_scaled - scaled * jnp.mean(grad_scaled * scaled, axis=-1, keepdims=True))
    out_ref[...] = grad
    low_ref[...] = grad.astype(BF)
    gain_grad_ref[...] += jnp.sum(grad_normed * scaled, axis=0, keepdims=True)


def norm_grads(part, first, second, values, grad, gain):
    rows, model = part.shape
    tile = rows // 4
    halves = first.shape[0] < rows
    tiles = pl.BlockSpec((tile, model), lambda i: (i, 0))
    row = pl.BlockSpec((1, model), lambda i: (0, 0))
    return pl.pallas_call(
        lambda *refs: norm_grads_kernel(halves, *refs),
        out_shape=(
            jax.ShapeDtypeStruct((rows, model), F32),
            jax.ShapeDtypeStruct((rows, model), BF),
            jax.ShapeDtypeStruct((1, model), F32),
        ),
        grid=(4,),
        in_specs=[
            tiles,
            pl.BlockSpec((tile, model), lambda i: (jnp.minimum(i, 1), 0)) if halves else tiles,
            pl.BlockSpec((tile, model), lambda i: (jnp.maximum(i - 2, 0), 0)) if halves else tiles,
            tiles,
            tiles,
            row,
        ],
        out_specs=(tiles, tiles, row),
        compiler_params=pltpu.CompilerParams(vmem_limit_bytes=24 << 20),
        cost_estimate=LIGHT,
        name="norm_grads",
    )(part, first, second, values, grad, gain[None])


def feed_forward_kernel(first_piece, *refs):
    x_ref, weight_refs = refs[0], refs[1:5]
    block = weight_refs[0].shape[1]
    if not first_piece:
        y_in_ref = refs[5]
    silu_ref, slope_ref, hidden_ref, y_ref = refs[-4:]
    x = x_ref[...]
    gate = upper = None
    for r in range(4):
        part = x[:, r * block : (r + 1) * block]
        g = dot_nn(part, weight_refs[r][0])
        u = dot_nn(part, weight_refs[r][1])
        gate = g if gate is None else gate + g
        upper = u if upper is None else upper + u
    sigmoid = jax.nn.sigmoid(gate)
    silu = gate * sigmoid
    hidden = (silu * upper).astype(BF)
    silu_ref[...] = silu.astype(BF)
    slope_ref[...] = (upper * (sigmoid * (1.0 + gate * (1.0 - sigmoid)))).astype(BF)
    hidden_ref[...] = hidden
    for r in range(4):
        cols = slice(r * block, (r + 1) * block)
        y = dot_nt(hidden, weight_refs[r][2])
        y_ref[:, cols] = y if first_piece else y + y_in_ref[:, cols]


def alone(piece):
    return (piece[None], 0)


def feed_forward(x, pieces, y):
    rows, model = x.shape
    _, _, block, width = pieces[0][0].shape
    tile = rows // 4
    tiles = lambda cols: pl.BlockSpec((tile, cols), lambda i: (i, 0))
    weight_specs = [pl.BlockSpec((None, 3, block, width), lambda i, n=n: (n, 0, 0, 0)) for _, n in pieces]
    extra = [] if y is None else [y]
    return pl.pallas_call(
        lambda *refs: feed_forward_kernel(y is None, *refs),
        out_shape=tuple(jax.ShapeDtypeStruct((rows, width), BF) for _ in range(3)) + (jax.ShapeDtypeStruct((rows, model), F32),),
        grid=(4,),
        in_specs=[tiles(model)] + weight_specs + [tiles(model) for _ in extra],
        out_specs=(tiles(width), tiles(width), tiles(width), tiles(model)),
        input_output_aliases={5: 3} if extra else {},
        compiler_params=pltpu.CompilerParams(vmem_limit_bytes=24 << 20),
        cost_estimate=LIGHT,
        name="feed_forward",
    )(x, *[w for w, _ in pieces], *extra)


def feed_backward_kernel(places, has_sum, last, *refs):
    count = len(places) // 4
    refs = list(refs)
    take = lambda n: [refs.pop(0) for _ in range(n)]
    x_ref, g_ref = take(2)
    silu_hbm, slope_hbm, hidden_hbm, weight_hbm = take(count), take(count), take(count), take(4 * count)
    sum_ref = take(1)[0] if has_sum else None
    dx_ref, dx_other_ref = take(2) if last else take(1) * 2
    out_hbm = take(4 * count)
    xt_ref, gt_ref, kept_ref, hidden_ref, gu_ref, down_ref, acc_ref, out_ref, act_sem, weight_sem, out_sem = refs
    _, _, block, width = weight_hbm[0].shape
    rows_all = x_ref.shape[0]
    half = rows_all // 2
    copies_of, late_copies = [], []
    for p in range(count):
        copies = []
        for n, source in enumerate((slope_hbm[p], silu_hbm[p])):
            copies.append(pltpu.make_async_copy(source, kept_ref.at[p, :, pl.ds(n * width, width)], act_sem.at[p, n]))
        for r in range(4):
            features = pl.ds(r * block, block)
            source = weight_hbm[p * 4 + r].at[places[p * 4 + r]]
            for n, target in enumerate((gu_ref.at[p, features, pl.ds(0, width)], gu_ref.at[p, features, pl.ds(width, width)], down_ref.at[p, features, :])):
                copies.append(pltpu.make_async_copy(source.at[n], target, weight_sem.at[p, r, n]))
        copies_of.append(copies)
        late_copies.append(pltpu.make_async_copy(hidden_hbm[p], hidden_ref.at[p], act_sem.at[p, 2]))
    for copy in copies_of[0]:
        copy.start()
    for t in range(4):
        rows = slice(t * rows_all // 4, (t + 1) * rows_all // 4)
        xt_ref[:, rows] = jnp.transpose(x_ref[rows, :])
        gt_ref[:, rows] = jnp.transpose(g_ref[rows, :])

    for p in range(count):
        for copy in copies_of[p]:
            copy.wait()
        for copy in copies_of[p + 1] if p < count - 1 else late_copies:
            copy.start()
        for t in range(2):
            rows = slice(t * half, (t + 1) * half)
            grad_hidden = dot_nn(g_ref[rows, :], down_ref[p])
            kept_ref[p, rows, :width] = (grad_hidden * kept_ref[p, rows, :width].astype(F32)).astype(BF)
            kept_ref[p, rows, width:] = (grad_hidden * kept_ref[p, rows, width:].astype(F32)).astype(BF)
            part = dot_nt(kept_ref[p, rows, :], gu_ref[p])
            if p > 0:
                part = acc_ref[rows, :] + part
            elif has_sum:
                part = sum_ref[rows, :] + part
            if p < count - 1:
                acc_ref[rows, :] = part
            elif not last:
                dx_ref[rows, :] = part
            elif t == 0:
                dx_ref[...] = part
            else:
                dx_other_ref[...] = part.astype(BF)

    slots = out_ref.shape[0]
    copies = []
    for p in range(count):
        late_copies[p].wait()
        for r in range(3, -1, -1):
            features = slice(r * block, (r + 1) * block)
            slot = len(copies) % slots
            if len(copies) >= slots:
                copies[len(copies) - slots].wait()
            gu = dot_nn(xt_ref[features, :], kept_ref[p]).astype(BF)
            out_ref[slot, 0] = gu[:, :width]
            out_ref[slot, 1] = gu[:, width:]
            out_ref[slot, 2] = dot_nn(gt_ref[features, :], hidden_ref[p]).astype(BF)
            copies.append(pltpu.make_async_copy(out_ref.at[slot], out_hbm[p * 4 + r], out_sem.at[slot]))
            copies[-1].start()
    for copy in copies[-slots:]:
        copy.wait()


def feed_backward(x, g, silus, slopes, hiddens, pieces, total, last):
    count = len(pieces)
    extra = [] if total is None else [total]
    rows, model = x.shape
    _, _, block, width = pieces[0][0][0].shape
    places = [n for piece in pieces for _, n in piece]
    vmem = pl.BlockSpec(memory_space=pltpu.VMEM)
    hbm = pl.BlockSpec(memory_space=pl.ANY)
    outs = pl.pallas_call(
        lambda *refs: feed_backward_kernel(places, total is not None, last, *refs),
        out_shape=(
            (jax.ShapeDtypeStruct((rows // 2, model), F32), jax.ShapeDtypeStruct((rows // 2, model), BF))
            if last
            else (jax.ShapeDtypeStruct((rows, model), F32),)
        )
        + tuple(jax.ShapeDtypeStruct((3, block, width), BF) for _ in range(4 * count)),
        in_specs=[vmem] * 2 + [hbm] * (7 * count) + [vmem] * len(extra),
        out_specs=((vmem, vmem) if last else (vmem,)) + (hbm,) * (4 * count),
        scratch_shapes=[
            pltpu.VMEM((model, rows), BF),
            pltpu.VMEM((model, rows), BF),
            pltpu.VMEM((count, rows, 2 * width), BF),
            pltpu.VMEM((count, rows, width), BF),
            pltpu.VMEM((count, model, 2 * width), BF),
            pltpu.VMEM((count, model, width), BF),
            pltpu.VMEM((rows, model), F32),
            pltpu.VMEM((3, 3, block, width), BF),
            pltpu.SemaphoreType.DMA((count, 3)),
            pltpu.SemaphoreType.DMA((count, 4, 3)),
            pltpu.SemaphoreType.DMA((3,)),
        ],
        compiler_params=pltpu.CompilerParams(vmem_limit_bytes=60 << 20),
        cost_estimate=LIGHT,
        name="feed_backward",
    )(x, g, *silus, *slopes, *hiddens, *[w for piece in pieces for w, _ in piece], *extra)
    first = 2 if last else 1
    return outs[:first], [outs[first + 4 * p : first + 4 + 4 * p] for p in range(count)]


class Order:
    def __init__(self):
        self.last = ()

    def event(self, *values):
        out = lax.optimization_barrier((*values, *self.last))[: len(values)]
        self.last = out
        return out


def on_square(inputs, teacher, lengths, w_qkv, w_out_t, w_gate_up, w_down_t, gains):
    chunk, model = inputs.shape
    slot = chunk * 4
    total_rows = slot * 8
    dp = lax.axis_index("dp")
    z = lax.axis_index("tensor")
    core = dp % 2
    first = core == 0
    odd_x = (dp // 2) % 2 == 1
    odd_y = dp // 4 == 1
    inner = jnp.where((z == 1) | (z == 2), 1, 0)
    moves = (core == 1) == (z < 2)
    chunk_low, chunk_high = inner, 3 - inner
    length = lax.dynamic_index_in_dim(lengths, (dp // 2) * 2 + z // 2, 0, keepdims=False)
    count = jnp.sum(lengths).astype(F32)
    places = jnp.stack([chunk_low, chunk_high, 1 - chunk_low, 2 + inner]) * chunk
    counts = jnp.clip(length - places, 0, chunk)
    outer = 1 - inner
    low_row, high_row = core * chunk, (1 - core) * chunk
    low_partner, high_partner = low_row + 2 * chunk, high_row + 2 * chunk
    scalars = jnp.stack(
        [
            low_row,
            high_row,
            low_partner,
            jnp.where(outer == 1, high_row, low_row),
            jnp.where(outer == 1, high_partner, low_partner),
            counts[0],
            counts[1],
            counts[2],
            jnp.where(outer == 1, counts[3], counts[2]),
        ]
    ).astype(jnp.int32)

    def turn(value):
        a, b, c, d = jnp.split(value, 4, axis=-1)
        a, b, c, d = jnp.where(odd_x, b, a), jnp.where(odd_x, a, b), jnp.where(odd_x, d, c), jnp.where(odd_x, c, d)
        return jnp.concatenate([jnp.where(odd_y, c, a), jnp.where(odd_y, d, b), jnp.where(odd_y, a, c), jnp.where(odd_y, b, d)], axis=-1)

    def sort_cores(own, other, axis):
        return jnp.where(first, jnp.concatenate([own, other], axis=axis), jnp.concatenate([other, own], axis=axis))

    def pick(pair):
        return jnp.where(first, pair[0], pair[1]), jnp.where(first, pair[1], pair[0])

    def join_rows(partial):
        return partial[:chunk] + core_swap(partial[chunk:].astype(BF)).astype(F32)

    def core_piece(stacked):
        keep, give = pick(jnp.split(stacked, 2, axis=2))
        return sort_cores(keep, core_swap(give), 1)

    def matmul(a, b):
        return jnp.einsum("ab,bc->ac", a, b, preferred_element_type=F32)

    def matmul_nt(a, b):
        return jnp.einsum("ab,cb->ac", a, b, preferred_element_type=F32)

    def matmul_tn(a, b):
        return jnp.einsum("ba,bc->ac", a, b, preferred_element_type=F32)

    order = Order()
    event = order.event

    attention_piece = core_piece(jnp.concatenate([jnp.swapaxes(w_qkv, 0, 1), w_out_t[None]], axis=0))
    attention_piece = jnp.concatenate([attention_piece[n] for n in range(4)], axis=1)
    feed_piece = core_piece(jnp.concatenate([jnp.swapaxes(w_gate_up, 0, 1), w_down_t[None]], axis=0))
    feed_p, feed_x, feed_y, feed_d = [None] * 4, [None] * 4, [None] * 4, [None] * 4
    (gains_pair,) = event(sort_cores(gains, core_swap(gains), 0))
    gains_x, gains_y, gains_d = x_swap(gains_pair), y_swap(gains_pair), square_swap(gains_pair)
    inputs_rel = turn(inputs)
    gains_x, gains_y, gains_d, attention_piece, feed_p[0] = event(gains_x, gains_y, gains_d, attention_piece, feed_piece)
    gains_all = jnp.concatenate([gains_pair, gains_x, gains_y, gains_d], axis=0)

    own_rows, partner_rows = home_swap(inputs_rel), shift(inputs_rel, partner_of_home)
    att_1, att_2 = z_swap(attention_piece, 1), z_swap(attention_piece, 2)
    att_1, feed_piece = event(att_1, feed_p[0])
    att_low = jnp.stack([attention_piece, att_1])
    att_low_x, att_low_y = x_swap(att_low), y_swap(att_low)
    (att_2,) = event(att_2)
    (att_3,) = event(z_swap(att_2, 1))
    att_high = jnp.stack([att_2, att_3])
    att_high_x, att_high_y = x_swap(att_high), y_swap(att_high)
    (att_low_x,) = event(att_low_x)
    att_low_d = y_swap(att_low_x)
    (att_high_y,) = event(att_high_y)
    att_high_d = x_swap(att_high_y)
    (own_rows,) = event(own_rows)
    other_rows = core_swap(own_rows)
    partner_rows, feed_piece = event(partner_rows, feed_piece)
    other_partner = core_swap(partner_rows)
    feed_x[0], feed_y[0] = x_swap(feed_piece), y_swap(feed_piece)
    feed_p[1] = z_swap(feed_piece, 1)
    att_low_y, att_high_x, att_low_d, att_high_d = event(att_low_y, att_high_x, att_low_d, att_high_d)
    other_rows, other_partner, feed_piece = event(other_rows, other_partner, feed_piece)
    feed_p[2] = z_swap(feed_piece, 2)
    rows = own_rows.astype(F32)
    gain_one = gains_all[:, 0].astype(F32)
    gain_two = gains_all[:, 1].astype(F32)

    normed_all, queries, keys_all, values_all, w_queries, w_keys, w_values, w_out = project(
        (own_rows, other_rows, partner_rows, other_partner), gain_one[None], [att_low, att_low_x, att_low_y, att_low_d, att_high, att_high_x, att_high_y, att_high_d]
    )
    normed_own = normed_all[: 2 * chunk]
    outer_only = (1 - inner)[None].astype(jnp.int32)
    parts = [None] * 4

    def attend(n):
        return attend_forward(outer_only, scalars, queries, keys_all, values_all, n, 1)

    queries, feed_x[0], feed_y[0] = event(queries, feed_x[0], feed_y[0])
    feed_d[0] = y_swap(feed_x[0])
    parts[0] = attend(0)
    queries, feed_p[1], _ = event(queries, feed_p[1], parts[0][0])
    feed_x[1], feed_y[1] = x_swap(feed_p[1]), y_swap(feed_p[1])
    parts[1] = attend(1)
    queries, feed_d[0], feed_p[2], _ = event(queries, feed_d[0], feed_p[2], parts[1][0])
    feed_y[2] = y_swap(feed_p[2])
    feed_p[3] = z_swap(feed_p[2], 1)
    parts[2] = attend(2)
    queries, feed_x[1], feed_y[1], _ = event(queries, feed_x[1], feed_y[1], parts[2][0])
    batch_x = x_swap(jnp.stack([feed_y[1], feed_p[2]]))
    parts[3] = attend(3)
    mixed = jnp.concatenate([p[0] for p in parts], axis=1)
    branch = matmul_nt(mixed, w_out)
    branch_own, branch_other, feed_p[3], feed_y[2], teacher = event(
        branch[:chunk], branch[chunk:].astype(BF), feed_p[3], feed_y[2], teacher
    )
    feed_y[3] = y_swap(feed_p[3])
    branch_other, batch_x, feed_y[3] = event(core_swap(branch_other), batch_x, feed_y[3])
    batch_x3, x_2 = event(jnp.stack([feed_p[3], feed_y[3]]), batch_x[1])
    batch_x3 = x_swap(batch_x3)
    feed_d[2] = y_swap(x_2)
    teacher_rel = turn(teacher)
    middle = rows + branch_own + branch_other.astype(F32)

    scaled_two, inverse_two = norm_forward(middle)
    normed_two = (scaled_two * gain_two).astype(BF)
    normed_two_all = jnp.concatenate([normed_two, core_swap_halves(normed_two)], axis=0)
    silus, slopes, hiddens, feed = [None] * 4, [None] * 4, [None] * 4, None
    pieces = [
        [alone(feed_p[0]), alone(feed_x[0]), alone(feed_y[0]), alone(feed_d[0])],
        [alone(feed_p[1]), alone(feed_x[1]), alone(feed_y[1]), (batch_x, 0)],
    ]
    for k in range(4):
        if k == 2:
            feed, feed_d[2], teacher_rel = event(feed, feed_d[2], teacher_rel)
            teacher_rows = moved_home(teacher_rel)
            pieces.append([alone(feed_p[2]), (batch_x, 1), alone(feed_y[2]), alone(feed_d[2])])
        if k == 3:
            feed, batch_x3 = event(feed, batch_x3)
            pieces.append([alone(feed_p[3]), (batch_x3, 0), alone(feed_y[3]), (batch_x3, 1)])
        silus[k], slopes[k], hiddens[k], feed = feed_forward(normed_two_all, pieces[k], feed)
    feed_own, feed_other, teacher_rows = event(feed[:chunk], feed[chunk:].astype(BF), teacher_rows)
    final = middle + feed_own + core_swap(feed_other).astype(F32)

    own_place = jnp.where(first, chunk_low, chunk_high) * chunk
    valid = (own_place + jnp.arange(chunk, dtype=jnp.int32) < length)[:, None]
    teacher_rows = jnp.where(moves, teacher_rows, teacher_rel)
    grad_final = jnp.where(valid, final - teacher_rows.astype(F32), 0.0) * (total_rows / count)
    grad_feed = grad_final.astype(BF)
    grad_feed_all, output = event(jnp.concatenate([grad_feed, core_swap(grad_feed)], axis=0), turn(final.astype(BF)))
    output_rel = output
    output = moved_home(output)

    def add(a, b):
        return (a.astype(F32) + b.astype(F32)).astype(BF)

    def total_of(own, x, y):
        return own.astype(F32) + x.astype(F32) + y.astype(F32)

    def feed_back(k, total):
        pair = slice(k, k + 2)
        return feed_backward(normed_two_all, grad_feed_all, silus[pair], slopes[pair], hiddens[pair], pieces[pair], total, k == 0)

    (grad_x,), ((own_2, x_2, y_2, d_2), (own_3, x_3, y_3, d_3)) = feed_back(2, None)
    grad_x, d_2, d_3 = event(grad_x, d_2, d_3)
    d_2, d_3 = y_swap(d_2), x_swap(d_3)
    (grad_x, grad_x_other), ((own_0, x_0, y_0, d_0), (own_1, x_1, y_1, d_1)) = feed_back(0, grad_x)
    grad_x, grad_x_other, output, d_2, d_3, d_0, d_1, y_2, x_3 = event(grad_x, grad_x_other, output, d_2, d_3, d_0, d_1, y_2, x_3)
    grad_x_other, batch_x, batch_y = event(grad_x_other, jnp.stack([add(x_2, d_2), x_3]), jnp.stack([y_2, add(y_3, d_3)]))
    batch_x, batch_y = x_swap(batch_x), y_swap(batch_y)
    tile = chunk // 2
    first_rows, second_rows = core_swap(grad_x_other[:tile]), core_swap(grad_x_other[tile:])
    grad_middle, grad_branch, grad_gain_two = norm_grads(grad_x, first_rows, second_rows, middle, grad_final, gain_two)
    grad_gain_two = grad_gain_two[0]
    grad_branch_both = jnp.concatenate([grad_branch, core_swap_halves(grad_branch)], axis=0)
    grad_mixed = matmul(grad_branch_both, w_out).astype(BF)
    half_width = mixed.shape[1] // 2

    def attend_back(n):
        lse = jnp.concatenate([parts[2 * n][1], parts[2 * n + 1][1]], axis=0)
        return attend_backward(scalars, queries, keys_all, values_all, mixed[:, n * half_width : (n + 1) * half_width], grad_mixed, lse, 2 * n)

    gq_a, gk_a, gv_a = attend_back(0)
    gq_a, grad_mixed, d_0, d_1 = event(gq_a, grad_mixed, d_0, d_1)
    d_0, d_1 = y_swap(d_0), x_swap(d_1)
    gq_b, gk_b, gv_b = attend_back(1)

    gq_b, batch_x, batch_y, d_0, d_1, x_1, y_0 = event(gq_b, batch_x, batch_y, d_0, d_1, x_1, y_0)
    part_3, part_2 = total_of(own_3, batch_x[1], batch_y[1]).astype(BF), total_of(own_2, batch_x[0], batch_y[0]).astype(BF)
    grad_queries, batch_x, batch_y, gk_b, gv_b = event(
        jnp.concatenate([gq_a, gq_b], axis=1), jnp.stack([add(x_0, d_0), x_1]), jnp.stack([y_0, add(y_1, d_1)]), gk_b, gv_b
    )
    batch_x, batch_y, part_3 = x_swap(batch_x), y_swap(batch_y), z_swap(part_3, 1)
    grad_keys = jnp.concatenate([gk_a, gk_b], axis=1)
    grad_values = jnp.concatenate([gv_a, gv_b], axis=1)
    part_own, part_other, partner_part, other_partner_part = rows_grads(grad_queries, grad_keys, grad_values, w_queries, w_keys, w_values)
    part_other, other_partner_part, grad_queries = event(core_swap(part_other), core_swap(other_partner_part), grad_queries)
    (from_partner,) = event((partner_part + other_partner_part.astype(F32)).astype(BF))
    from_partner = z_swap(from_partner, 1)
    (own_e, x_e, y_e, d_e), (own_o, x_o, y_o, d_o) = attention_grads(normed_all, grad_branch_both, grad_queries, grad_keys, grad_values, mixed)
    quarter_cols = grad_queries.shape[1] // 4
    half_cols = 4 * quarter_cols
    d_e, d_o, x_e, y_e, x_o, y_o, part_3, part_2 = event(d_e, d_o, x_e, y_e, x_o, y_o, part_3, part_2)
    (part_2,) = event(add(part_2, part_3))
    part_2 = z_swap(part_2, 2)
    batch_x, batch_y, d_e, d_o = event(batch_x, batch_y, d_e, d_o)
    d_e, d_o = y_swap(d_e), x_swap(d_o)
    (part_1,) = event(total_of(own_1, batch_x[1], batch_y[1]).astype(BF))
    part_1 = z_swap(part_1, 1)
    part_0 = total_of(own_0, batch_x[0], batch_y[0])
    (from_partner,) = event(from_partner)
    _, grad_rows, grad_gain_one = norm_grads(part_own, part_other, from_partner, own_rows, grad_middle, gain_one)
    grad_rows, gain_a, gain_b, part_2 = event(grad_rows, grad_gain_one[0], grad_gain_two, part_2)
    grad_rows = turn(grad_rows)
    grad_inputs = moved_home(grad_rows)
    d_e, d_o = event(d_e, d_o)
    batch_x, batch_y = event(jnp.stack([add(x_e, d_e), x_o]), jnp.stack([y_e, add(y_o, d_o)]))
    batch_x, batch_y = x_swap(batch_x), y_swap(batch_y)
    part_1, part_2, part_0 = event(part_1, part_2, part_0)
    feed_total = part_0 + part_1.astype(F32) + part_2.astype(F32)
    feed_keep, feed_give = pick(jnp.split(feed_total, 2, axis=1))
    feed_give = core_swap(feed_give.astype(BF))

    quarter = model // 4
    a, b, c, d = jnp.split(jnp.stack([gain_a, gain_b], axis=0), 4, axis=1)
    sent = x_swap(jnp.concatenate([b, d], axis=1))

    batch_x, batch_y, sent = event(batch_x, batch_y, sent)
    even, odd = total_of(own_e, batch_x[0], batch_y[0]), total_of(own_o, batch_x[1], batch_y[1])
    att_3, att_1, att_2 = odd[:, half_cols:].astype(BF), even[:, half_cols:].astype(BF), odd[:, :half_cols].astype(BF)
    att_3, att_1, a, c, sent = event(att_3, att_1, a, c, sent)
    att_3, att_1 = z_swap(att_3, 1), z_swap(att_1, 1)
    a, c = a + sent[:, :quarter], c + sent[:, quarter:]
    sent = y_swap(c)
    att_3, att_2, sent = event(att_3, att_2, sent)
    att_2 = z_swap(add(att_2, att_3), 2)
    a = a + sent
    keep, give = pick(jnp.split(a, 2, axis=1))
    sent = core_swap(give)
    feed_give, sent = event(feed_give, sent)
    a = keep + sent
    size = a.shape[1] // 4
    total = lax.dynamic_slice_in_dim(a, z * size, size, 1)
    for k in range(1, 4):
        total = total + z_swap(lax.dynamic_slice_in_dim(a, (z ^ k) * size, size, 1), k)
    grad_gains = jnp.swapaxes(total, 0, 1)
    grad_inputs = jnp.where(moves, grad_inputs, grad_rows).astype(F32)
    output = jnp.where(moves, output, output_rel)
    feed_out = sort_cores(feed_keep, feed_give.astype(F32), 2)
    attention_total = even[:, :half_cols] + att_1.astype(F32) + att_2.astype(F32)
    attention_total = jnp.stack([attention_total[:, n * quarter_cols : (n + 1) * quarter_cols] for n in range(4)])

    def to_home(total):
        keep, give = pick(jnp.split(total, 2, axis=1))
        return sort_cores(keep, core_swap(give.astype(BF)).astype(F32), 2)

    attention_out = to_home(attention_total)

    return (
        output,
        grad_inputs,
        jnp.swapaxes(attention_out[:3], 0, 1),
        attention_out[3],
        jnp.swapaxes(feed_out[:2], 0, 1),
        feed_out[2],
        grad_gains,
    )


def solution(mesh):
    square = dict(mesh.shape) == {"dp": 8, "tensor": 4}
    return jax.shard_map(
        on_square if square else on_device,
        mesh=mesh,
        in_specs=(
            P(("dp", "tensor"), None),
            P(("dp", "tensor"), None),
            P(),
            P("dp", None, "tensor"),
            P("dp", "tensor"),
            P("dp", None, "tensor"),
            P("dp", "tensor"),
            P("dp", None),
        ),
        out_specs=(
            P(("dp", "tensor"), None),
            P(("dp", "tensor"), None),
            P("dp", None, "tensor"),
            P("dp", "tensor"),
            P("dp", None, "tensor"),
            P("dp", "tensor"),
            P(("dp", "tensor"), None),
        ),
        check_vma=False,
    )
```
